256 devices in a mesh: dp: 8 (over z_lo, x), ctx: 32 (over z_hi, y, core).
Axes of the slice: x: 4, y: 4, z: 8 (z_hi: 4, z_lo: 2; z = z_hi * 2 + z_lo), core: 2. Of those that a mesh axis runs over, the one named last changes fastest.
Arguments:
- tokens: bfloat16 [8, 4096, 4096], P('dp', 'ctx'), may hold values from -6 to 6
- proj_weight: bfloat16 [4096, 512], P('dp'), may hold values from -0.09375 to 0.09375
- values: bfloat16 [8, 4096, 2048], P('dp', 'ctx'), may hold values from -60 to 60
- grad_out: bfloat16 [8, 4096, 2048], P('dp', 'ctx'), may hold values from -6 to 6
Outputs:
- attended: bfloat16 [8, 4096, 2048], P('dp', 'ctx')
- grad_tokens: bfloat16 [8, 4096, 4096], P('dp', 'ctx')
- grad_values: bfloat16 [8, 4096, 2048], P('dp', 'ctx')
- grad_proj: float32 [4096, 512], P(('dp', 'ctx'))
The draws below stay inside these ranges and needn't reach their ends.
All inputs are finite; a program needn't handle non-finite values.
Results may differ from the reference program's by a relative error of at most 0.0049.
Values may be sent and summed in bfloat16 or wider, within the bound.
A program may use at most 192 MiB of HBM per device.

```python
import jax
import jax.numpy as jnp
from jax import lax

D = 4096
H = 16
F = 16
DH = 128
E = 273
TOK_DEV = 128
BATCH = 8
SEQ = 4096


def draw_values(key, part):
    key_random, key_scale = jax.random.split(key, 2)
    scales = jnp.exp(jax.random.uniform(key_scale, (H * DH,), jnp.float32, 0.0, 2.302585))
    random_part = jnp.clip(jax.random.normal(key_random, (BATCH, SEQ, H * DH), jnp.float32), -6.0, 6.0)
    return (random_part * scales).astype(jnp.bfloat16)


def strengthened(entries, own_key, source, target, blocks, factor):
    owner, partner = [(jnp.arange(entries.shape[dim]) // (entries.shape[dim] // blocks)).reshape([-1 if axis == dim else 1 for axis in range(entries.ndim)]) for dim in (source, target)]
    chosen = jax.random.permutation(own_key, blocks)[partner]
    strong = (owner == chosen) | (owner == (partner + blocks // 2) % blocks)
    return jnp.where(strong, factor * entries, entries)


def steps_of(own_key, dims, cuts, smallest, high):
    def one(axis_at, blocks):
        steps = jax.random.uniform(jax.random.fold_in(jax.random.fold_in(own_key, 6), axis_at), (blocks,), jnp.float32, smallest / len(cuts), high / len(cuts))
        return jnp.repeat(jnp.exp(steps), dims[axis_at] // blocks).reshape((-1,) + (1,) * (len(dims) - axis_at - 1))

    loudness = one(*cuts[0])
    for cut in cuts[1:]:
        loudness = loudness * one(*cut)
    return loudness


def centred(rng, extent, width, most, shards=(), kind=jnp.bfloat16):
    gain = steps_of(rng, extent, shards, -0.22, 0.18) if shards else 1.0
    entries = jax.random.normal(rng, extent, jnp.float32) * width * gain
    return jnp.minimum(jnp.maximum(entries, -most), most).astype(kind)


def heavy_noise(rng, extent, scale, reach, shards, heavy, held_as=jnp.bfloat16):
    drawn = scale * jax.random.normal(rng, extent, jnp.float32)
    if shards:
        drawn = drawn * steps_of(rng, extent, shards, -0.22, 0.18)
    return jnp.clip(strengthened(drawn, jax.random.fold_in(rng, 3), *heavy), -reach, reach).astype(held_as)


def setup_inputs(seed: int = 0) -> dict:
    key_list = jax.random.split(jax.random.key(seed), 5)
    tokens = heavy_noise(key_list[0], (BATCH, SEQ, D), 1.0, 6.0, ((0, 8), (1, 32)), (1, 2, 32, 2.75))
    proj_weight = centred(key_list[1], (D, 2 * H * F), D ** -0.5, 0.09375, ((0, 8),))
    values = draw_values(jax.random.fold_in(key_list[4], 71), 0)
    grad_out = centred(key_list[3], (BATCH, SEQ, H * DH), 1.0, 6.0, ((0, 8), (1, 32)))
    return {"tokens": tokens, "proj_weight": proj_weight, "values": values, "grad_out": grad_out}


HIGHEST = lax.Precision.HIGHEST
QUAD_SCALE = 0.17677669529663687
EPSILON = 1e-05

def features(inputs):
    count_heads, count_rows, count_feat = inputs.shape
    linear = jnp.swapaxes(inputs, 1, 2) * 0.5
    square = (inputs[:, :, :, None] * inputs[:, :, None, :]).reshape(count_heads, count_rows, count_feat * count_feat)
    square = jnp.swapaxes(square, 1, 2) * QUAD_SCALE
    constant_row = jnp.ones((count_heads, 1, count_rows), inputs.dtype)
    return jnp.concatenate([constant_row, linear, square], axis=1)

def block_kernel(query_part, key_part):
    count_rows = query_part.shape[1]
    causal = lax.broadcasted_iota(jnp.int32, (count_rows, count_rows), 0) >= lax.broadcasted_iota(jnp.int32, (count_rows, count_rows), 1)
    scores = jnp.einsum('htf,hsf->hts', query_part, key_part, precision=HIGHEST) * 0.25
    kernel = jnp.where(causal, 1.0 + scores + 0.5 * scores * scores, 0.0)
    return (causal, scores, kernel)

def normalize(numerator):
    inv_rms = lax.rsqrt(lax.optimization_barrier(jnp.mean(numerator * numerator, axis=-1, keepdims=True)) + EPSILON)
    return (inv_rms, numerator * inv_rms)

def grad_normalize(inv_rms, normed, upstream):
    return inv_rms * (upstream - normed * lax.optimization_barrier(jnp.mean(normed * upstream, axis=-1, keepdims=True)))

def local_backward(query_part, key_part, value_part, grad_num, causal, scores, kernel, pull_query, pull_key, feat_key, prefix, suffix):
    mixing = jnp.where(causal, jnp.einsum('htd,hsd->hts', grad_num, value_part, precision=HIGHEST), 0.0)
    slope = mixing * (1.0 + scores)
    grad_query = jnp.einsum('hts,hsf->htf', slope, key_part, precision=HIGHEST) * 0.25
    grad_key = jnp.einsum('hts,htf->hsf', slope, query_part, precision=HIGHEST) * 0.25
    grad_query = grad_query + pull_query(jnp.einsum('hed,htd->het', prefix, grad_num, precision=HIGHEST))[0]
    grad_key = grad_key + pull_key(jnp.einsum('hed,htd->het', suffix, value_part, precision=HIGHEST))[0]
    grad_value = jnp.einsum('hts,htd->hsd', kernel, grad_num, precision=HIGHEST)
    grad_value = grad_value + jnp.einsum('het,hed->htd', feat_key, suffix, precision=HIGHEST)
    return (grad_query, grad_key, grad_value)

def split_blocks(matrix, size):
    blocks = matrix.shape[0] // TOK_DEV
    return matrix.reshape(blocks, TOK_DEV, H, size).transpose(0, 2, 1, 3)

def merge_blocks(blocked):
    return blocked.transpose(0, 2, 1, 3).reshape(blocked.shape[0] * blocked.shape[2], -1)

def sequence_pass(tokens_seq, proj_weight, values_seq, grad_seq):
    projected = jnp.dot(tokens_seq, proj_weight, preferred_element_type=jnp.float32)
    query_cols = H * F
    query_all = split_blocks(projected[:, :query_cols], F)
    key_all = split_blocks(projected[:, query_cols:], F)
    value_all = split_blocks(values_seq.astype(jnp.float32), DH)
    upstream_all = split_blocks(grad_seq.astype(jnp.float32), DH)
    zero_state = jnp.zeros((H, E, DH), jnp.float32)

    def forward_step(state, block):
        query_part, key_part, value_part = block
        feat_query = features(query_part)
        feat_key = features(key_part)
        causal, scores, kernel = block_kernel(query_part, key_part)
        numerator = jnp.einsum('hts,hsd->htd', kernel, value_part, precision=HIGHEST)
        numerator = numerator + jnp.einsum('het,hed->htd', feat_query, state, precision=HIGHEST)
        new_state = state + jnp.einsum('het,htd->hed', feat_key, value_part, precision=HIGHEST)
        return (new_state, (numerator, state))
    final_state, (numerators, prefixes) = lax.scan(forward_step, zero_state, (query_all, key_all, value_all))
    inv_rms, normed = normalize(numerators)
    attended = merge_blocks(normed).astype(jnp.bfloat16)
    grad_num_all = grad_normalize(inv_rms, normed, upstream_all)

    def backward_step(suffix, block):
        query_part, key_part, value_part, grad_num, prefix = block
        feat_query, pull_query = jax.vjp(features, query_part)
        feat_key, pull_key = jax.vjp(features, key_part)
        causal, scores, kernel = block_kernel(query_part, key_part)
        grads = local_backward(query_part, key_part, value_part, grad_num, causal, scores, kernel, pull_query, pull_key, feat_key, prefix, suffix)
        new_suffix = suffix + jnp.einsum('het,htd->hed', feat_query, grad_num, precision=HIGHEST)
        return (new_suffix, grads)
    last_suffix, (grad_query, grad_key, grad_value) = lax.scan(backward_step, zero_state, (query_all, key_all, value_all, grad_num_all, prefixes), reverse=True)
    grad_proj_rows = jnp.concatenate([merge_blocks(grad_query), merge_blocks(grad_key)], axis=1).astype(jnp.bfloat16)
    grad_tokens = jnp.dot(grad_proj_rows, proj_weight.T, preferred_element_type=jnp.float32).astype(jnp.bfloat16)
    grad_part = jnp.dot(tokens_seq.T, grad_proj_rows, preferred_element_type=jnp.float32)
    grad_values = merge_blocks(grad_value).astype(jnp.bfloat16)
    return (attended, grad_tokens, grad_values, grad_part)

def reference(tokens, proj_weight, values, grad_out):

    def per_sequence(total, inputs):
        tokens_seq, values_seq, grad_seq = inputs
        attended, grad_tokens, grad_values, grad_part = sequence_pass(tokens_seq, proj_weight, values_seq, grad_seq)
        return (total + grad_part, (attended, grad_tokens, grad_values))
    start_total = jnp.zeros((D, 2 * H * F), jnp.float32)
    grad_proj, (attended, grad_tokens, grad_values) = lax.scan(per_sequence, start_total, (tokens, values, grad_out))
    return (attended, grad_tokens, grad_values, grad_proj)
```

```python
import jax
import jax.numpy as jnp
from jax import lax
from jax.sharding import PartitionSpec as P

H = 16
F = 16
DH = 128


HIGHEST = lax.Precision.HIGHEST
QUAD_SCALE = 0.17677669529663687
EPSILON = 1e-05


def features(inputs):
    count_heads, count_rows, count_feat = inputs.shape
    linear = jnp.swapaxes(inputs, 1, 2) * 0.5
    square = (inputs[:, :, :, None] * inputs[:, :, None, :]).reshape(
        count_heads, count_rows, count_feat * count_feat
    )
    square = jnp.swapaxes(square, 1, 2) * QUAD_SCALE
    constant_row = jnp.ones((count_heads, 1, count_rows), inputs.dtype)
    return jnp.concatenate([constant_row, linear, square], axis=1)


def block_kernel(query_part, key_part):
    count_rows = query_part.shape[1]
    causal = lax.broadcasted_iota(jnp.int32, (count_rows, count_rows), 0) >= lax.broadcasted_iota(
        jnp.int32, (count_rows, count_rows), 1
    )
    scores = jnp.einsum("htf,hsf->hts", query_part, key_part, precision=HIGHEST) * 0.25
    kernel = jnp.where(causal, 1.0 + scores + 0.5 * scores * scores, 0.0)
    return (causal, scores, kernel)


def normalize(numerator):
    inv_rms = lax.rsqrt(jnp.mean(numerator * numerator, axis=-1, keepdims=True) + EPSILON)
    return (inv_rms, numerator * inv_rms)


def grad_normalize(inv_rms, normed, upstream):
    return inv_rms * (upstream - normed * jnp.mean(normed * upstream, axis=-1, keepdims=True))


def local_backward(
    query_part,
    key_part,
    value_part,
    grad_num,
    causal,
    scores,
    kernel,
    pull_query,
    pull_key,
    feat_key,
    prefix,
    suffix,
):
    mixing = jnp.where(
        causal, jnp.einsum("htd,hsd->hts", grad_num, value_part, precision=HIGHEST), 0.0
    )
    slope = mixing * (1.0 + scores)
    grad_query = jnp.einsum("hts,hsf->htf", slope, key_part, precision=HIGHEST) * 0.25
    grad_key = jnp.einsum("hts,htf->hsf", slope, query_part, precision=HIGHEST) * 0.25
    grad_query = (
        grad_query + pull_query(jnp.einsum("hed,htd->het", prefix, grad_num, precision=HIGHEST))[0]
    )
    grad_key = (
        grad_key + pull_key(jnp.einsum("hed,htd->het", suffix, value_part, precision=HIGHEST))[0]
    )
    grad_value = jnp.einsum("hts,htd->hsd", kernel, grad_num, precision=HIGHEST)
    grad_value = grad_value + jnp.einsum("het,hed->htd", feat_key, suffix, precision=HIGHEST)
    return (grad_query, grad_key, grad_value)


def exclusive(blocks, later):
    count = blocks.shape[0]
    row = lax.broadcasted_iota(jnp.int32, (count, count), 0)
    col = lax.broadcasted_iota(jnp.int32, (count, count), 1)
    chosen = (col > row) if later else (col < row)
    return jnp.dot(chosen.astype(jnp.float32), blocks, precision=HIGHEST)


def split_heads(matrix, size):
    return jnp.swapaxes(matrix.reshape(matrix.shape[0], -1, size), 0, 1)


def merge_heads(blocked):
    return jnp.swapaxes(blocked, 0, 1).reshape(blocked.shape[1], -1)


def local(tokens, proj_weight, values, grad_out):
    token_rows = tokens[0]
    query_cols = H * F
    tokens_cols = lax.all_to_all(token_rows, "dp", split_axis=1, concat_axis=0, tiled=True)
    projected = jnp.dot(
        token_rows,
        lax.all_gather(proj_weight, "dp", axis=0, tiled=True),
        preferred_element_type=jnp.float32,
    )
    query_part = split_heads(projected[:, :query_cols], F)
    key_part = split_heads(projected[:, query_cols:], F)
    value_part = split_heads(values[0].astype(jnp.float32), DH)
    upstream = split_heads(grad_out[0].astype(jnp.float32), DH)
    feat_query, pull_query = jax.vjp(features, query_part)
    feat_key, pull_key = jax.vjp(features, key_part)
    local_term = jnp.einsum("het,htd->hed", feat_key, value_part, precision=HIGHEST)
    columns_in = lax.all_to_all(
        local_term.reshape(1, -1), "ctx", split_axis=1, concat_axis=0, tiled=True
    )
    running = exclusive(columns_in, False)
    prefix = lax.all_to_all(running, "ctx", split_axis=0, concat_axis=1, tiled=True).reshape(
        local_term.shape
    )
    causal, scores, kernel = block_kernel(query_part, key_part)
    numerator = jnp.einsum("hts,hsd->htd", kernel, value_part, precision=HIGHEST)
    numerator = numerator + jnp.einsum("het,hed->htd", feat_query, prefix, precision=HIGHEST)
    inv_rms, normed = normalize(numerator)
    attended = merge_heads(normed).astype(jnp.bfloat16)
    grad_num = grad_normalize(inv_rms, normed, upstream)
    carried = jnp.einsum("het,htd->hed", feat_query, grad_num, precision=HIGHEST)
    later_in = lax.all_to_all(
        carried.reshape(1, -1), "ctx", split_axis=1, concat_axis=0, tiled=True
    )
    later_running = exclusive(later_in, True)
    suffix = lax.all_to_all(later_running, "ctx", split_axis=0, concat_axis=1, tiled=True).reshape(
        carried.shape
    )
    grad_query, grad_key, grad_value = local_backward(
        query_part,
        key_part,
        value_part,
        grad_num,
        causal,
        scores,
        kernel,
        pull_query,
        pull_key,
        feat_key,
        prefix,
        suffix,
    )
    grad_proj_rows = jnp.concatenate(
        [merge_heads(grad_query), merge_heads(grad_key)], axis=1
    ).astype(jnp.bfloat16)
    grad_tokens = lax.dot_general(
        grad_proj_rows,
        lax.all_gather(proj_weight, "dp", axis=0, tiled=True),
        (((1,), (1,)), ((), ())),
        preferred_element_type=jnp.float32,
    ).astype(jnp.bfloat16)
    rows_all = lax.all_gather(grad_proj_rows, "dp", axis=0, tiled=True)
    grad_proj = lax.psum_scatter(
        lax.dot_general(
            tokens_cols, rows_all, (((0,), (0,)), ((), ())), preferred_element_type=jnp.float32
        ),
        "ctx",
        scatter_dimension=0,
        tiled=True,
    )
    grad_values = merge_heads(grad_value).astype(jnp.bfloat16)
    return (attended[None], grad_tokens[None], grad_values[None], grad_proj)


def solution(mesh):
    return jax.shard_map(
        local,
        mesh=mesh,
        in_specs=(P("dp", "ctx", None), P("dp", None), P("dp", "ctx", None), P("dp", "ctx", None)),
        out_specs=(
            P("dp", "ctx", None),
            P("dp", "ctx", None),
            P("dp", "ctx", None),
            P(("dp", "ctx"), None),
        ),
        check_vma=False,
    )
```

```python
import functools

import jax
import jax.numpy as jnp
from jax import lax
from jax.experimental import pallas as pl
from jax.experimental.pallas import tpu as pltpu
from jax.sharding import PartitionSpec as P

H = 16
F = 16
DH = 128
EP = 160
QUAD = 1.0 / 32.0
EPSILON = 1e-05
MESH = pl.DeviceIdType.MESH
F32 = jnp.float32
BF16 = jnp.bfloat16
VMEM = pl.BlockSpec(memory_space=pltpu.VMEM)
NY = 4
NZ = 4
NDP = 8
NC = 2
RC = 2 * EP // NC


def dot(lhs, rhs, left, right):
    return lax.dot_general(lhs, rhs, (((left,), (right,)), ((), ())), preferred_element_type=F32)


def remote(src, dst, send, recv, **where):
    return pltpu.make_async_remote_copy(
        src_ref=src, dst_ref=dst, send_sem=send, recv_sem=recv, device_id=where, device_id_type=MESH
    )


def greet(peers):
    barrier = pltpu.get_barrier_semaphore()
    for where in peers:
        pl.semaphore_signal(barrier, inc=1, device_id=where, device_id_type=MESH)
    pl.semaphore_wait(barrier, len(peers))


def across(dp, dz, dx):
    return (dp // 4 + dz) % 2 * 4 + (dp % 4 + dx + 4) % 4


def place():
    ctx = lax.axis_index("ctx")
    return ctx // 8, (ctx // 2) % 4, ctx % 2


def at(z, y, c):
    return z * 8 + y * 2 + c


def gather_weight_kernel(w_ref, out_ref, own_sem, send1, recv1, send2, recv2):
    dp = lax.axis_index("dp")
    z, y, c = place()
    partner = at(z, y, 1 - c)
    greet([{"dp": (dp + d) % NDP} for d in range(1, NDP)] + [{"ctx": partner}])
    half = w_ref.shape[0] // 2
    rows = w_ref.shape[0]

    def spot(owner):
        return pl.ds(pl.multiple_of(owner * rows + c * half, half), half)

    own = pltpu.make_async_copy(
        w_ref, out_ref.at[pl.ds(pl.multiple_of(dp * rows, rows), rows)], own_sem
    )
    mine = w_ref.at[pl.ds(pl.multiple_of(c * half, half), half)]
    first = []
    for d in range(1, NDP):
        first.append(
            remote(mine, out_ref.at[spot(dp)], send1.at[d], recv1.at[d], dp=(dp + d) % NDP)
        )
        first[-1].start()
    own.start()
    second = []
    for d in range(1, NDP):
        first[d - 1].wait_recv()
        landed = out_ref.at[spot((dp + NDP - d) % NDP)]
        second.append(remote(landed, landed, send2.at[d], recv2.at[d], ctx=partner))
        second[-1].start()
    for copy in first:
        copy.wait_send()
    for copy in second:
        copy.wait()
    own.wait()


def gather_weight(w):
    return pl.pallas_call(
        gather_weight_kernel,
        out_shape=jax.ShapeDtypeStruct((NDP * w.shape[0], w.shape[1]), w.dtype),
        in_specs=[VMEM],
        out_specs=VMEM,
        scratch_shapes=[pltpu.SemaphoreType.DMA] + [pltpu.SemaphoreType.DMA((NDP,))] * 4,
        compiler_params=pltpu.CompilerParams(collective_id=0, has_side_effects=True),
        name="gather_weight",
    )(w)


def scan_kernel(later, slots, *refs):
    s_ref, tok_ref, out_ref, cols_ref = refs[:4]
    rest = refs[4:]
    sib, chip, yin, tz, zin, yout, pin, hand, pre, sem_c, sem_y, sem_z, sem_b, sem_p = rest[:14]
    z, y, c = place()
    dp = lax.axis_index("dp")
    partner = at(z, y, 1 - c)
    peers = [{"ctx": partner}]
    peers += [{"ctx": at(z, (y + d) % NY, c)} for d in range(1, NY)]
    peers += [{"ctx": at((z + d) % NZ, y, c)} for d in range(1, NZ)]
    moves = [move for move in slots if move != (0, 0)]
    met = sorted({(dz, step % 4) for dz, dx in moves for step in (dx, -dx)})
    peers += [{"dp": across(dp, dz, dx)} for dz, dx in met]
    greet(peers)

    def before(other, me):
        return other > me if later else other < me

    copies_c = []
    for n in range(NC):
        copies_c.append(
            remote(s_ref.at[1 - c, n], sib.at[n], sem_c.at[0, n], sem_c.at[1, n], ctx=partner)
        )
        copies_c[-1].start()
    token_copies = []

    def send_tokens(slots):
        for index, (dz, dx) in slots:
            peer = across(dp, dz, dx)
            where = pl.ds(pl.multiple_of(peer * width, width), width)
            token_copies.append(
                remote(
                    tok_ref.at[:, where], cols_ref.at[index], sem_t.at[0, index],
                    sem_t.at[1, index], dp=peer,
                )
            )
            token_copies[-1].start()

    sem_t, own_t = rest[14:]
    width = cols_ref.shape[2]
    listed = list(enumerate(slots))
    send_tokens([(i, s) for i, s in listed if s[0] == 0 and s[1] > 0])
    own_copies = []
    for index, s in listed:
        if s == (0, 0):
            where = pl.ds(pl.multiple_of(dp * width, width), width)
            own_copies.append(
                pltpu.make_async_copy(tok_ref.at[:, where], cols_ref.at[index], own_t)
            )
            own_copies[-1].start()
    copies_y = []
    for n in range(NC):
        copies_c[n].wait_recv()
        for j in range(NY):
            chip[n, j] = (s_ref[c, n, j] + sib[n, j]).astype(BF16)
        for d in range(1, NY):
            to = (y + d) % NY
            copies_y.append(
                remote(
                    chip.at[n, to], yin.at[n, y], sem_y.at[0, n, d], sem_y.at[1, n, d],
                    ctx=at(z, to, c),
                )
            )
            copies_y[-1].start()
    copies_z = []
    for n in range(NC):
        for d in range(1, NY):
            copies_y[n * 3 + d - 1].wait_recv()
        blocks = [
            jnp.where(j == y, chip[n, j], yin[n, j]).astype(F32) for j in range(NY)
        ]
        order = list(range(NY))[::-1] if later else list(range(NY))
        total = jnp.zeros_like(blocks[0])
        for j in order:
            pre[n, j] = total
            total = total + blocks[j]
        tz[n] = total.astype(BF16)
        for d in range(1, NZ):
            copies_z.append(
                remote(
                    tz.at[n], zin.at[n, z], sem_z.at[0, n, d], sem_z.at[1, n, d],
                    ctx=at((z + d) % NZ, y, c),
                )
            )
            copies_z[-1].start()
    send_tokens([(i, s) for i, s in listed if s[0] == 1])
    copies_b = []
    for n in range(NC):
        for d in range(1, NZ):
            copies_z[n * 3 + d - 1].wait_recv()
        base = jnp.zeros(pre.shape[2:], F32)
        for j in range(NZ):
            base = base + jnp.where(before(j, z), zin[n, j].astype(F32), 0.0)
        for j in range(NY):
            yout[n, j] = (base + pre[n, j]).astype(BF16)
        for d in range(1, NY):
            to = (y + d) % NY
            copies_b.append(
                remote(
                    yout.at[n, to], pin.at[n, y], sem_b.at[0, n, d], sem_b.at[1, n, d],
                    ctx=at(z, to, c),
                )
            )
            copies_b[-1].start()
    copies_p = []
    for n in range(NC):
        for d in range(1, NY):
            copies_b[n * 3 + d - 1].wait_recv()
        for j in range(NY):
            prefix = jnp.where(j == y, yout[n, j], pin[n, j]).astype(F32)
            mine = prefix + jnp.where(before(1 - c, c), sib[n, j], 0.0)
            theirs = prefix + jnp.where(before(c, 1 - c), s_ref[c, n, j], 0.0)
            hand[n, j] = theirs
            out_ref[c, n, j] = mine
        copies_p.append(
            remote(hand.at[n], out_ref.at[c, n], sem_p.at[0, n], sem_p.at[1, n], ctx=partner)
        )
        copies_p[-1].start()
    for copy in copies_p:
        copy.wait()
    for copy in copies_c + copies_y + copies_z + copies_b:
        copy.wait_send()
    for copy in token_copies + own_copies:
        copy.wait()


def scan(state, later, collective, tokens, slots):
    shape = (2, NC, NY, RC, DH)
    slab = (NC, NY, RC, DH)
    thin = (NC, RC, DH)
    rows, width = tokens.shape
    dma = pltpu.SemaphoreType.DMA
    return pl.pallas_call(
        functools.partial(scan_kernel, later, slots),
        out_shape=(
            jax.ShapeDtypeStruct(shape, F32),
            jax.ShapeDtypeStruct((len(slots), rows, width // NDP), BF16),
        ),
        in_specs=[VMEM, VMEM],
        out_specs=(VMEM, VMEM),
        scratch_shapes=[
            pltpu.VMEM(slab, F32),
            pltpu.VMEM(slab, BF16),
            pltpu.VMEM(slab, BF16),
            pltpu.VMEM(thin, BF16),
            pltpu.VMEM((NC, NZ, RC, DH), BF16),
            pltpu.VMEM(slab, BF16),
            pltpu.VMEM(slab, BF16),
            pltpu.VMEM(slab, F32),
            pltpu.VMEM(slab, F32),
            dma((2, NC)),
            dma((2, NC, NY)),
            dma((2, NC, NZ)),
            dma((2, NC, NY)),
            dma((2, NC)),
            dma((2, len(slots))),
            dma,
        ],
        compiler_params=pltpu.CompilerParams(collective_id=collective, has_side_effects=True),
        name="scan_later" if later else "scan_earlier",
    )(state, tokens)


def gather_rows_kernel(r_ref, out_ref, own_sem, send, recv):
    dp = lax.axis_index("dp")
    right, left, other = across(dp, 0, 1), across(dp, 0, 3), across(dp, 1, 0)
    greet([{"dp": right}, {"dp": left}, {"dp": other}])
    half = r_ref.shape[0] // 2
    low, high = pl.ds(0, half), pl.ds(half, half)
    started = []

    def push(index, src, dst, to):
        copy = remote(src, dst, send.at[index], recv.at[index], dp=to)
        copy.start()
        started.append(copy)
        return copy

    over = push(0, r_ref, out_ref.at[4], other)
    rights = [push(1, r_ref, out_ref.at[1], right), None]
    lefts = [push(2, r_ref, out_ref.at[3], left), None]
    own = pltpu.make_async_copy(r_ref, out_ref.at[0], own_sem)
    own.start()
    over.wait_recv()
    rights[1] = push(3, out_ref.at[4], out_ref.at[5], right)
    lefts[1] = push(4, out_ref.at[4], out_ref.at[7], left)
    ends = []
    for n in range(2):
        base = 4 * n
        rights[n].wait_recv()
        ends.append(
            push(5 + n, out_ref.at[base + 1, low], out_ref.at[base + 2, low], right)
        )
        lefts[n].wait_recv()
        ends.append(
            push(7 + n, out_ref.at[base + 3, high], out_ref.at[base + 2, high], left)
        )
    for copy in ends:
        copy.wait_recv()
    for copy in started:
        copy.wait_send()
    own.wait()


def gather_rows(r):
    return pl.pallas_call(
        gather_rows_kernel,
        out_shape=jax.ShapeDtypeStruct((NDP,) + r.shape, r.dtype),
        in_specs=[VMEM],
        out_specs=VMEM,
        scratch_shapes=[pltpu.SemaphoreType.DMA] + [pltpu.SemaphoreType.DMA((9,))] * 2,
        compiler_params=pltpu.CompilerParams(collective_id=3, has_side_effects=True),
        name="gather_rows",
    )(r)


def reduce_kernel(g_ref, out_ref, sib, pair, yin, ysum, zin, sem_c, sem_y, sem_z):
    z, y, c = place()
    partner = at(z, y, 1 - c)
    peers = [{"ctx": partner}]
    peers += [{"ctx": at(z, (y + d) % NY, c)} for d in range(1, NY)]
    peers += [{"ctx": at((z + d) % NZ, y, c)} for d in range(1, NZ)]
    greet(peers)
    copies_c, copies_y, copies_z = [], [], []
    for d in range(NY):
        to = (y + d) % NY
        copies_c.append(
            remote(
                g_ref.at[:, to, 1 - c], sib.at[to], sem_c.at[0, d], sem_c.at[1, d], ctx=partner
            )
        )
    for d in (1, 2, 3, 0):
        copies_c[d].start()
    for d in (1, 2, 3, 0):
        to = (y + d) % NY
        copies_c[d].wait_recv()
        both = g_ref[:, to, c] + sib[to]
        if d == 0:
            ysum[...] = both
        else:
            pair[to] = both.astype(BF16)
            copies_y.append(
                remote(pair.at[to], yin.at[y], sem_y.at[0, d], sem_y.at[1, d], ctx=at(z, to, c))
            )
            copies_y[-1].start()
    for copy in copies_y:
        copy.wait_recv()
    for j in range(NY):
        ysum[...] += jnp.where(j == y, 0.0, yin[j].astype(F32))
    for d in range(1, NZ):
        to = (z + d) % NZ
        copies_z.append(
            remote(ysum.at[to], zin.at[z], sem_z.at[0, d], sem_z.at[1, d], ctx=at(to, y, c))
        )
        copies_z[-1].start()
    for copy in copies_z:
        copy.wait_recv()
    total = ysum[z]
    for j in range(NZ):
        total = total + jnp.where(j == z, 0.0, zin[j])
    out_ref[...] = total
    for copy in copies_c + copies_y + copies_z:
        copy.wait_send()


def reduce_ctx(grad):
    rows, width = grad.shape
    own = rows // (2 * NY * NZ)
    view = grad.reshape(NZ, NY, 2, own, width)
    slab = (NY, NZ, own, width)
    dma = pltpu.SemaphoreType.DMA
    return pl.pallas_call(
        reduce_kernel,
        out_shape=jax.ShapeDtypeStruct((own, width), F32),
        in_specs=[VMEM],
        out_specs=VMEM,
        scratch_shapes=[
            pltpu.VMEM(slab, F32),
            pltpu.VMEM(slab, BF16),
            pltpu.VMEM(slab, BF16),
            pltpu.VMEM((NZ, own, width), F32),
            pltpu.VMEM((NZ, own, width), F32),
            dma((2, NY)),
            dma((2, NY)),
            dma((2, NZ)),
        ],
        compiler_params=pltpu.CompilerParams(collective_id=4, has_side_effects=True),
        name="reduce_ctx",
    )(view)


def ahead(x, d):
    return pltpu.roll(x, F - d, 0)


def behind(x, d):
    return pltpu.roll(x, d, 0)


def features(x, weighted):
    quad, linear = (QUAD, 0.25) if weighted else (1.0, 1.0)
    twice = 2.0 * quad if weighted else 1.0
    parts = [x * x * quad] + [x * ahead(x, d) * twice for d in range(1, 8)]
    parts += [x[:8] * x[8:] * twice, x * linear]
    row = lax.broadcasted_iota(jnp.int32, (8, x.shape[1]), 0)
    parts.append(jnp.where(row == 0, 1.0, 0.0))
    return jnp.concatenate(parts, axis=0)


def pull_features(x, cot):
    out = 2.0 * QUAD * cot[:F] * x
    for d in range(1, 8):
        part = 2.0 * QUAD * cot[F * d : F * (d + 1)]
        out = out + part * ahead(x, d) + behind(part * x, d)
    half = 2.0 * QUAD * cot[128:136]
    out = out + jnp.concatenate([half * x[8:], half * x[:8]], axis=0)
    return out + 0.25 * cot[136:152]


def split(x):
    high = x.astype(BF16)
    return high, (x - high.astype(F32)).astype(BF16)


def scores(q, k):
    qh, ql = split(q)
    kh, kl = split(k)
    left = jnp.concatenate([qh, qh, ql, ql], axis=0)
    right = jnp.concatenate([kh, kl, kh, kl], axis=0)
    return dot(left, right, 0, 0) * 0.25


def product(feat, state):
    fh, fl = split(feat)
    sh, sl = split(state)
    left = jnp.concatenate([fh, fl, fh], axis=0)
    right = jnp.concatenate([sh, sh, sl], axis=0)
    return dot(left, right, 0, 0)


def pulled(state, rows, fine=None):
    high, low = split(state)
    both = dot(jnp.concatenate([high, low], axis=0), rows, 1, 1)
    both = both[:EP] + both[EP:]
    return both if fine is None else both + dot(high, fine, 1, 1)


def causal():
    shape = (128, 128)
    return lax.broadcasted_iota(jnp.int32, shape, 0) >= lax.broadcasted_iota(jnp.int32, shape, 1)


def head_cols(h):
    return slice(h * DH, (h + 1) * DH)


def head_rows(h):
    return slice(h * F, (h + 1) * F)


def slot(h):
    return h // 8, h % 2, (h // 2) % 4


def project_kernel(tok_ref, w_ref, v_ref, proj_ref, state_ref):
    proj = dot(tok_ref[...], w_ref[...], 1, 0)
    proj_ref[...] = proj.T
    for h in range(H):
        keys = proj_ref[256 + h * F : 256 + (h + 1) * F, :]
        high, low = split(features(keys, False))
        v = v_ref[:, head_cols(h)]
        state = dot(
            jnp.concatenate([high, low], axis=1), jnp.concatenate([v, v], axis=0), 1, 0
        )
        state_ref[slot(h)] = state


def forward_kernel(proj_ref, v_ref, g_ref, prefix_ref, att_ref, gn_ref, state_ref):
    mask = causal()
    for h in range(H):
        q = proj_ref[head_rows(h), :]
        k = proj_ref[256 + h * F : 256 + (h + 1) * F, :]
        a = scores(q, k)
        kernel = jnp.where(mask, 1.0 + a + 0.5 * a * a, 0.0)
        feat = features(q, False)
        v = v_ref[:, head_cols(h)]
        numerator = dot(
            jnp.concatenate(split(kernel), axis=1), jnp.concatenate([v, v], axis=0), 1, 0
        )
        numerator += product(features(q, True), prefix_ref[slot(h)])
        inv = lax.rsqrt(jnp.mean(numerator * numerator, axis=1, keepdims=True) + EPSILON)
        normed = numerator * inv
        att_ref[:, head_cols(h)] = normed.astype(BF16)
        g = g_ref[:, head_cols(h)].astype(F32)
        gn = inv * (g - normed * jnp.mean(normed * g, axis=1, keepdims=True))
        gn_ref[:, head_cols(h)] = gn
        high, low = split(feat)
        gh, gl = split(gn)
        state_ref[slot(h)] = dot(
            jnp.concatenate([high, low, high], axis=1),
            jnp.concatenate([gh, gh, gl], axis=0),
            1,
            0,
        )


def backward_kernel(proj_ref, v_ref, gn_ref, prefix_ref, suffix_ref, gv_ref, rows_ref, acc):
    mask = causal()
    for h in range(H):
        q = proj_ref[head_rows(h), :]
        k = proj_ref[256 + h * F : 256 + (h + 1) * F, :]
        v = v_ref[:, head_cols(h)]
        gh, gl = split(gn_ref[:, head_cols(h)])
        a = scores(q, k)
        mh, ml = split(jnp.where(mask, 1.0 + a + 0.5 * a * a, 0.0))
        mixing = dot(
            jnp.concatenate([gh, gl], axis=1), jnp.concatenate([v, v], axis=1), 1, 1
        )
        sh, sl = split(jnp.where(mask, mixing * (1.0 + a) * 0.25, 0.0))
        qh, ql = split(q)
        kh, kl = split(k)
        dq = dot(jnp.concatenate([kh, kl], axis=0), sh, 1, 1)
        dq = dq[:F] + dq[F:] + dot(kh, sl, 1, 1)
        dk = dot(jnp.concatenate([qh, ql], axis=0), sh, 1, 0)
        dk = dk[:F] + dk[F:] + dot(qh, sl, 1, 0)
        pre = prefix_ref[slot(h)]
        suf = suffix_ref[slot(h)]
        acc[head_rows(h), :] = dq + pull_features(q, pulled(pre, gh, gl))
        acc[256 + h * F : 256 + (h + 1) * F, :] = dk + pull_features(k, pulled(suf, v))
        gv = dot(
            jnp.concatenate([mh, ml, mh], axis=0), jnp.concatenate([gh, gh, gl], axis=0), 0, 0
        )
        gv += product(features(k, True), suf)
        gv_ref[:, head_cols(h)] = gv.astype(BF16)
    rows_ref[...] = acc[...].T.astype(BF16)


def weight_grad_kernel(early_ref, late_ref, rows_ref, out_ref):
    early = early_ref.shape[0]
    flat = rows_ref[...].reshape(-1, rows_ref.shape[2])
    cols = jnp.concatenate(
        [early_ref[n] for n in range(early)] + [late_ref[n] for n in range(late_ref.shape[0])],
        axis=0,
    )
    out_ref[...] = dot(cols, flat, 0, 0)


def plain(kernel, outs, args, scratch=(), name=None):
    return pl.pallas_call(
        kernel,
        out_shape=outs,
        in_specs=[VMEM] * len(args),
        out_specs=jax.tree.map(lambda _: VMEM, outs),
        scratch_shapes=list(scratch),
        name=name,
    )(*args)


def shaped(shape, dtype):
    return jax.ShapeDtypeStruct(shape, dtype)


def local(tokens, proj_weight, values, grad_out):
    tok, val, up = tokens[0], values[0], grad_out[0]
    rows = tok.shape[0]
    packed = shaped((2, NC, NY, RC, DH), F32)
    weight = gather_weight(proj_weight)
    proj, state = plain(
        project_kernel, (shaped((2 * H * F, rows), F32), packed), (tok, weight, val), name="project"
    )
    early = ((0, 0), (0, 1), (0, 2), (0, 3), (1, 0), (1, 1))
    late = ((1, 2), (1, 3))
    prefix, cols_early = scan(state, False, 1, tok, early)
    attended, grad_num, carried = plain(
        forward_kernel,
        (shaped(val.shape, BF16), shaped(val.shape, F32), packed),
        (proj, val, up, prefix),
        name="forward",
    )
    suffix, cols_late = scan(carried, True, 2, tok, late)
    grad_values, grad_rows = plain(
        backward_kernel,
        (shaped(val.shape, BF16), shaped((rows, 2 * H * F), BF16)),
        (proj, val, grad_num, prefix, suffix),
        scratch=[pltpu.VMEM((2 * H * F, rows), F32)],
        name="backward",
    )
    rows_all = gather_rows(grad_rows)
    grad_tokens = dot(grad_rows, weight, 1, 1).astype(BF16)
    (part,) = plain(
        weight_grad_kernel,
        (shaped((tok.shape[1] // NDP, 2 * H * F), F32),),
        (cols_early, cols_late, rows_all),
        name="weight_grad",
    )
    grad_proj = reduce_ctx(part)
    return (attended[None], grad_tokens[None], grad_values[None], grad_proj)


def solution(mesh):
    return jax.shard_map(
        local,
        mesh=mesh,
        in_specs=(P("dp", "ctx", None), P("dp", None), P("dp", "ctx", None), P("dp", "ctx", None)),
        out_specs=(
            P("dp", "ctx", None),
            P("dp", "ctx", None),
            P("dp", "ctx", None),
            P(("dp", "ctx"), None),
        ),
        check_vma=False,
    )
```

```python
import functools

import jax
import jax.numpy as jnp
from jax import lax
from jax.experimental import pallas as pl
from jax.experimental.pallas import tpu as pltpu
from jax.sharding import PartitionSpec as P

H = 16
F = 16
DH = 128
EP = 160
QUAD = 1.0 / 32.0
EPSILON = 1e-05
MESH = pl.DeviceIdType.MESH
F32 = jnp.float32
BF16 = jnp.bfloat16
VMEM = pl.BlockSpec(memory_space=pltpu.VMEM)
NY = 4
NZ = 4
NDP = 8
NC = 2
RC = 2 * EP // NC


def dot(lhs, rhs, left, right):
    return lax.dot_general(lhs, rhs, (((left,), (right,)), ((), ())), preferred_element_type=F32)


def remote(src, dst, send, recv, **where):
    return pltpu.make_async_remote_copy(
        src_ref=src, dst_ref=dst, send_sem=send, recv_sem=recv, device_id=where, device_id_type=MESH
    )


def greet(peers):
    barrier = pltpu.get_barrier_semaphore()
    for where in peers:
        pl.semaphore_signal(barrier, inc=1, device_id=where, device_id_type=MESH)
    pl.semaphore_wait(barrier, len(peers))


def across(dp, dz, dx):
    return (dp // 4 + dz) % 2 * 4 + (dp % 4 + dx + 4) % 4


def place():
    ctx = lax.axis_index("ctx")
    return ctx // 8, (ctx // 2) % 4, ctx % 2


def at(z, y, c):
    return z * 8 + y * 2 + c


class Wires:
    def __init__(self, send, recv):
        self.send, self.recv, self.copies = send, recv, []

    def push(self, src, dst, **where):
        n = len(self.copies)
        copy = remote(src, dst, self.send.at[n], self.recv.at[n], **where)
        copy.start()
        self.copies.append(copy)
        return copy

    def drain(self):
        for copy in self.copies:
            copy.wait_send()


def gather_weight_kernel(w_ref, out_ref, own_sem, send, recv):
    dp = lax.axis_index("dp")
    z, y, c = place()
    partner = at(z, y, 1 - c)
    up, down = at(z, (y + 1) % NY, c), at(z, (y + 3) % NY, c)
    right, left, other = across(dp, 0, 1), across(dp, 0, 3), across(dp, 1, 0)
    greet(
        [{"dp": right}, {"dp": left}, {"dp": other}, {"ctx": partner}, {"ctx": up}, {"ctx": down}]
    )
    rows = w_ref.shape[0]
    half = rows // 2
    wide = half // 2
    thin = wide // NY
    wires = Wires(send, recv)

    def part(owner, start, size):
        return out_ref.at[pl.ds(pl.multiple_of(owner * rows + start, thin // 2), size)]

    def here(start, size):
        return w_ref.at[pl.ds(pl.multiple_of(start, thin // 2), size)]

    base_a = c * half
    base_b = c * half + wide

    def own_sends(start, size):
        src, dst = here(start, size), part(dp, start, size)
        return (
            wires.push(src, dst, dp=other),
            wires.push(src, dst, dp=right),
            wires.push(src, dst, dp=left),
        )

    def pass_on(owner, start, size):
        piece = part(owner, start, size)
        return wires.push(piece, piece, dp=right), wires.push(piece, piece, dp=left)

    def relay(near, far, start, size):
        one = part(near, start, size // 2)
        two = part(far, start + size // 2, size // 2)
        return wires.push(one, one, dp=right), wires.push(two, two, dp=left)

    def over_y(owner):
        piece = part(owner, base_b + y * thin, thin)
        return wires.push(piece, piece, ctx=up), wires.push(piece, piece, ctx=down)

    def on_chip(owner, start, size):
        piece = part(owner, start, size)
        return wires.push(piece, piece, ctx=partner)

    mine_b = base_b + y * thin
    b_over, b_right, b_left = own_sends(mine_b, thin)
    a_over, a_right, a_left = own_sends(base_a, wide)
    own = pltpu.make_async_copy(
        w_ref, out_ref.at[pl.ds(pl.multiple_of(dp * rows, rows), rows)], own_sem
    )
    own.start()
    owners = [other, left, right, across(dp, 1, 3), across(dp, 1, 1), across(dp, 0, 2), across(dp, 1, 2)]
    chain_y = []
    b_over.wait_recv()
    b_right2, b_left2 = pass_on(other, mine_b, thin)
    chain_y.append(over_y(owners[0]))
    b_right.wait_recv()
    b_left.wait_recv()
    b_ends = relay(left, right, mine_b, thin)
    chain_y.append(over_y(owners[1]))
    chain_y.append(over_y(owners[2]))
    a_over.wait_recv()
    a_right2, a_left2 = pass_on(other, base_a, wide)
    b_right2.wait_recv()
    b_left2.wait_recv()
    b_ends2 = relay(owners[3], owners[4], mine_b, thin)
    chain_y.append(over_y(owners[3]))
    chain_y.append(over_y(owners[4]))
    last = [on_chip(owners[0], base_a, wide)]
    a_right.wait_recv()
    a_left.wait_recv()
    a_ends = relay(left, right, base_a, wide)
    for copy in b_ends:
        copy.wait_recv()
    chain_y.append(over_y(owners[5]))
    for copy in b_ends2:
        copy.wait_recv()
    chain_y.append(over_y(owners[6]))
    last += [on_chip(owners[1], base_a, wide), on_chip(owners[2], base_a, wide)]
    ends_y = []
    below = base_b + (y + 3) % NY * thin
    above = base_b + (y + 1) % NY * thin + thin // 2

    def relay_y(n):
        chain_y[n][0].wait_recv()
        one = part(owners[n], below, thin // 2)
        ends_y.append([wires.push(one, one, ctx=up)])
        chain_y[n][1].wait_recv()
        two = part(owners[n], above, thin // 2)
        ends_y[-1].append(wires.push(two, two, ctx=down))

    for n in range(3):
        relay_y(n)
    a_right2.wait_recv()
    a_left2.wait_recv()
    a_ends2 = relay(owners[3], owners[4], base_a, wide)
    last += [on_chip(owners[3], base_a, wide), on_chip(owners[4], base_a, wide)]
    for n in range(3, 7):
        relay_y(n)
    for n in range(5):
        for copy in ends_y[n]:
            copy.wait_recv()
        last.append(on_chip(owners[n], base_b, wide))
    for copy in a_ends:
        copy.wait_recv()
    last.append(on_chip(owners[5], base_a, wide))
    for n in (5, 6):
        for copy in ends_y[n]:
            copy.wait_recv()
        last.append(on_chip(owners[n], base_b, wide))
    for copy in a_ends2:
        copy.wait_recv()
    last.append(on_chip(owners[6], base_a, wide))
    for copy in last:
        copy.wait_recv()
    wires.drain()
    own.wait()


def gather_weight(w):
    return pl.pallas_call(
        gather_weight_kernel,
        out_shape=jax.ShapeDtypeStruct((NDP * w.shape[0], w.shape[1]), w.dtype),
        in_specs=[VMEM],
        out_specs=VMEM,
        scratch_shapes=[pltpu.SemaphoreType.DMA] + [pltpu.SemaphoreType.DMA((64,))] * 2,
        compiler_params=pltpu.CompilerParams(collective_id=0, has_side_effects=True),
        name="gather_weight",
    )(w)


def scan_kernel(later, slots, *refs):
    s_ref, tok_ref, out_ref, cols_ref = refs[:4]
    sib, chip, yin, tz, zin, yout, pin, hand, pre, hop_y, hop_b, send, recv, send_t, recv_t, own_t = refs[4:]
    z, y, c = place()
    dp = lax.axis_index("dp")
    partner = at(z, y, 1 - c)
    up, down = at(z, (y + 1) % NY, c), at(z, (y + 3) % NY, c)
    fore, back = at((z + 1) % NZ, y, c), at((z + 3) % NZ, y, c)
    moves = [move for move in slots if move != (0, 0)]
    met = sorted({(dz, step % 4) for dz, dx in moves for step in (dx, -dx)})
    greet(
        [{"ctx": peer} for peer in (partner, up, down, fore, back)]
        + [{"dp": across(dp, dz, dx)} for dz, dx in met]
    )
    low, high = pl.ds(0, RC // 2), pl.ds(RC // 2, RC // 2)
    wires, token_wires = Wires(send, recv), Wires(send_t, recv_t)

    def before(other, me):
        return other > me if later else other < me

    copies_c = [wires.push(s_ref.at[1 - c, n], sib.at[n], ctx=partner) for n in range(NC)]
    width = cols_ref.shape[2]
    own_copies = []

    def send_tokens(dz_now):
        for index, (dz, dx) in enumerate(slots):
            if dz != dz_now:
                continue
            peer = across(dp, dz, dx)
            src = tok_ref.at[:, pl.ds(pl.multiple_of(peer * width, width), width)]
            if (dz, dx) == (0, 0):
                own_copies.append(pltpu.make_async_copy(src, cols_ref.at[index], own_t))
                own_copies[-1].start()
            else:
                token_wires.push(src, cols_ref.at[index], dp=peer)

    def exchange_y(src, dst, hop, n):
        far = src.at[n, (y + 2) % NY]
        return [
            wires.push(far.at[low], hop.at[n, 0], ctx=up),
            wires.push(far.at[high], hop.at[n, 1], ctx=down),
            wires.push(src.at[n, (y + 1) % NY], dst.at[n, y], ctx=up),
            wires.push(src.at[n, (y + 3) % NY], dst.at[n, y], ctx=down),
        ]

    def relay_y(copies, dst, hop, n):
        copies[0].wait_recv()
        one = wires.push(hop.at[n, 0], dst.at[n, (y + 3) % NY, low], ctx=up)
        copies[1].wait_recv()
        two = wires.push(hop.at[n, 1], dst.at[n, (y + 1) % NY, high], ctx=down)
        return copies[2:] + [one, two]

    copies_y = []
    for n in range(NC):
        copies_c[n].wait_recv()
        for j in range(NY):
            chip[n, j] = (s_ref[c, n, j] + sib[n, j]).astype(BF16)
        copies_y.append(exchange_y(chip, yin, hop_y, n))
    send_tokens(0)
    for n in range(NC):
        copies_y[n] = relay_y(copies_y[n], yin, hop_y, n)
    copies_z = []
    for n in range(NC):
        for copy in copies_y[n]:
            copy.wait_recv()
        blocks = [jnp.where(j == y, chip[n, j], yin[n, j]).astype(F32) for j in range(NY)]
        order = list(range(NY))[::-1] if later else list(range(NY))
        total = jnp.zeros_like(blocks[0])
        for j in order:
            pre[n, j] = total
            total = total + blocks[j]
        tz[n] = total.astype(BF16)
        copies_z.append(
            [
                wires.push(tz.at[n], zin.at[n, z], ctx=fore),
                wires.push(tz.at[n], zin.at[n, z], ctx=back),
            ]
        )
    for n in range(NC):
        copies_z[n][0].wait_recv()
        behind_me, ahead_me = (z + 3) % NZ, (z + 1) % NZ
        one = wires.push(zin.at[n, behind_me, low], zin.at[n, behind_me, low], ctx=fore)
        copies_z[n][1].wait_recv()
        two = wires.push(zin.at[n, ahead_me, high], zin.at[n, ahead_me, high], ctx=back)
        copies_z[n] = [one, two]
    send_tokens(1)
    copies_b = []
    for n in range(NC):
        for copy in copies_z[n]:
            copy.wait_recv()
        base = jnp.zeros(pre.shape[2:], F32)
        for j in range(NZ):
            base = base + jnp.where(before(j, z), zin[n, j].astype(F32), 0.0)
        for j in range(NY):
            yout[n, j] = (base + pre[n, j]).astype(BF16)
        copies_b.append(exchange_y(yout, pin, hop_b, n))
    for n in range(NC):
        copies_b[n] = relay_y(copies_b[n], pin, hop_b, n)
    copies_p = []
    for n in range(NC):
        for copy in copies_b[n]:
            copy.wait_recv()
        for j in range(NY):
            prefix = jnp.where(j == y, yout[n, j], pin[n, j]).astype(F32)
            hand[n, j] = prefix + jnp.where(before(c, 1 - c), s_ref[c, n, j], 0.0)
            out_ref[c, n, j] = prefix + jnp.where(before(1 - c, c), sib[n, j], 0.0)
        copies_p.append(wires.push(hand.at[n], out_ref.at[c, n], ctx=partner))
    for copy in copies_p:
        copy.wait_recv()
    wires.drain()
    for copy in token_wires.copies + own_copies:
        copy.wait()


def scan(state, later, collective, tokens, slots):
    shape = (2, NC, NY, RC, DH)
    slab = (NC, NY, RC, DH)
    thin = (NC, RC, DH)
    rows, width = tokens.shape
    dma = pltpu.SemaphoreType.DMA
    return pl.pallas_call(
        functools.partial(scan_kernel, later, slots),
        out_shape=(
            jax.ShapeDtypeStruct(shape, F32),
            jax.ShapeDtypeStruct((len(slots), rows, width // NDP), BF16),
        ),
        in_specs=[VMEM, VMEM],
        out_specs=(VMEM, VMEM),
        scratch_shapes=[
            pltpu.VMEM(slab, F32),
            pltpu.VMEM(slab, BF16),
            pltpu.VMEM(slab, BF16),
            pltpu.VMEM(thin, BF16),
            pltpu.VMEM((NC, NZ, RC, DH), BF16),
            pltpu.VMEM(slab, BF16),
            pltpu.VMEM(slab, BF16),
            pltpu.VMEM(slab, F32),
            pltpu.VMEM(slab, F32),
            pltpu.VMEM((NC, 2, RC // 2, DH), BF16),
            pltpu.VMEM((NC, 2, RC // 2, DH), BF16),
            dma((18 * NC,)),
            dma((18 * NC,)),
            dma((len(slots),)),
            dma((len(slots),)),
            dma,
        ],
        compiler_params=pltpu.CompilerParams(collective_id=collective, has_side_effects=True),
        name="scan_later" if later else "scan_earlier",
    )(state, tokens)


def tail_kernel(
    order, r_ref, early_ref, late_ref, w_hbm, gt_ref, out_ref,
    w_ref, all_ref, g_ref, sib, pair, yin, ysum, hop, zin, send, recv, w_sem,
):
    dp = lax.axis_index("dp")
    z, y, c = place()
    partner = at(z, y, 1 - c)
    up, down = at(z, (y + 1) % NY, c), at(z, (y + 3) % NY, c)
    right, left, other = across(dp, 0, 1), across(dp, 0, 3), across(dp, 1, 0)
    greet(
        [{"dp": right}, {"dp": left}, {"dp": other}]
        + [{"ctx": peer} for peer in (partner, up, down)]
        + [{"ctx": at((z + d) % NZ, y, c)} for d in range(1, NZ)]
    )
    wires = Wires(send, recv)
    half = r_ref.shape[0] // 2
    low, high = pl.ds(0, half), pl.ds(half, half)
    over = wires.push(r_ref, all_ref.at[4], dp=other)
    rights = [wires.push(r_ref, all_ref.at[1], dp=right)]
    lefts = [wires.push(r_ref, all_ref.at[3], dp=left)]
    load = pltpu.make_async_copy(w_hbm, w_ref, w_sem)
    load.start()
    early = early_ref.shape[0]

    def cols(slot_at):
        n = order.index((slot_at // 4, slot_at % 4))
        return early_ref[n] if n < early else late_ref[n - early]

    def product_of(slots):
        left_rows = jnp.concatenate([cols(n) for n in slots], axis=0)
        right_rows = jnp.concatenate([r_ref[...] if n == 0 else all_ref[n] for n in slots], axis=0)
        return dot(left_rows, right_rows, 0, 0).reshape(g_ref.shape)

    block = w_ref.shape[0] // 4

    def input_grad(n):
        piece = dot(r_ref[...], w_ref[n * block : (n + 1) * block, :], 1, 1)
        gt_ref[:, n * block : (n + 1) * block] = piece.astype(BF16)

    over.wait_recv()
    rights.append(wires.push(all_ref.at[4], all_ref.at[5], dp=right))
    lefts.append(wires.push(all_ref.at[4], all_ref.at[7], dp=left))
    load.wait()
    input_grad(0)
    ends = []
    for n in range(2):
        rights[n].wait_recv()
        one = wires.push(all_ref.at[4 * n + 1, low], all_ref.at[4 * n + 2, low], dp=right)
        lefts[n].wait_recv()
        two = wires.push(all_ref.at[4 * n + 3, high], all_ref.at[4 * n + 2, high], dp=left)
        ends.append((one, two))
        input_grad(2 * n + 1)
        if n == 0:
            g_ref[...] = product_of((0, 1, 3, 4))
            input_grad(2)
    for pair_of in ends:
        for copy in pair_of:
            copy.wait_recv()
    g_ref[...] += product_of((2, 5, 6, 7))

    copies_c = {}
    for d in (2, 1, 3, 0):
        to = (y + d) % NY
        copies_c[d] = wires.push(g_ref.at[:, to, 1 - c], sib.at[to], ctx=partner)
    near = []
    for d in (2, 1, 3, 0):
        to = (y + d) % NY
        copies_c[d].wait_recv()
        both = g_ref[:, to, c] + sib[to]
        if d == 0:
            ysum[...] = both
        else:
            pair[to] = both.astype(BF16)
            if d == 2:
                far = pair.at[to]
                relays = [
                    wires.push(far.at[pl.ds(0, NZ // 2)], hop.at[0], ctx=up),
                    wires.push(far.at[pl.ds(NZ // 2, NZ // 2)], hop.at[1], ctx=down),
                ]
            else:
                near.append(wires.push(pair.at[to], yin.at[y], ctx=up if d == 1 else down))
    relays[0].wait_recv()
    near.append(wires.push(hop.at[0], yin.at[(y + 3) % NY, pl.ds(0, NZ // 2)], ctx=up))
    relays[1].wait_recv()
    near.append(wires.push(hop.at[1], yin.at[(y + 1) % NY, pl.ds(NZ // 2, NZ // 2)], ctx=down))
    for copy in near:
        copy.wait_recv()
    for j in range(NY):
        ysum[...] += jnp.where(j == y, 0.0, yin[j].astype(F32))
    copies_z = []
    for d in (2, 1, 3):
        to = (z + d) % NZ
        copies_z.append(wires.push(ysum.at[to], zin.at[z], ctx=at(to, y, c)))
    for copy in copies_z:
        copy.wait_recv()
    total = ysum[z]
    for j in range(NZ):
        total = total + jnp.where(j == z, 0.0, zin[j])
    out_ref[...] = total
    wires.drain()


def tail(rows, early, late, order, weight):
    width = rows.shape[1]
    own = early.shape[2] // (2 * NY * NZ)
    slab = (NY, NZ, own, width)
    dma = pltpu.SemaphoreType.DMA
    return pl.pallas_call(
        functools.partial(tail_kernel, order),
        out_shape=(
            jax.ShapeDtypeStruct((rows.shape[0], weight.shape[0]), BF16),
            jax.ShapeDtypeStruct((own, width), F32),
        ),
        in_specs=[VMEM, VMEM, VMEM, pl.BlockSpec(memory_space=pl.ANY)],
        out_specs=(VMEM, VMEM),
        scratch_shapes=[
            pltpu.VMEM(weight.shape, BF16),
            pltpu.VMEM((NDP,) + rows.shape, BF16),
            pltpu.VMEM((NZ, NY, 2, own, width), F32),
            pltpu.VMEM(slab, F32),
            pltpu.VMEM(slab, BF16),
            pltpu.VMEM(slab, BF16),
            pltpu.VMEM((NZ, own, width), F32),
            pltpu.VMEM((2, NZ // 2, own, width), BF16),
            pltpu.VMEM((NZ, own, width), F32),
            dma((24,)),
            dma((24,)),
            dma,
        ],
        compiler_params=pltpu.CompilerParams(collective_id=3, has_side_effects=True),
        name="tail",
    )(rows, early, late, weight)


def ahead(x, d):
    return pltpu.roll(x, F - d, 0)


def behind(x, d):
    return pltpu.roll(x, d, 0)


def features(x, weighted):
    quad, linear = (QUAD, 0.25) if weighted else (1.0, 1.0)
    twice = 2.0 * quad if weighted else 1.0
    parts = [x * x * quad] + [x * ahead(x, d) * twice for d in range(1, 8)]
    parts += [x[:8] * x[8:] * twice, x * linear]
    row = lax.broadcasted_iota(jnp.int32, (8, x.shape[1]), 0)
    parts.append(jnp.where(row == 0, 1.0, 0.0))
    return jnp.concatenate(parts, axis=0)


def pull_features(x, cot):
    out = 2.0 * QUAD * cot[:F] * x
    for d in range(1, 8):
        part = 2.0 * QUAD * cot[F * d : F * (d + 1)]
        out = out + part * ahead(x, d) + behind(part * x, d)
    half = 2.0 * QUAD * cot[128:136]
    out = out + jnp.concatenate([half * x[8:], half * x[:8]], axis=0)
    return out + 0.25 * cot[136:152]


def split(x):
    high = x.astype(BF16)
    return high, (x - high.astype(F32)).astype(BF16)


def scores(q, k):
    qh, ql = split(q)
    kh, kl = split(k)
    left = jnp.concatenate([qh, qh, ql, ql], axis=0)
    right = jnp.concatenate([kh, kl, kh, kl], axis=0)
    return dot(left, right, 0, 0) * 0.25


def product(feat, state):
    fh, fl = split(feat)
    sh, sl = split(state)
    left = jnp.concatenate([fh, fl, fh], axis=0)
    right = jnp.concatenate([sh, sh, sl], axis=0)
    return dot(left, right, 0, 0)


def pulled(state, rows, fine=None):
    high, low = split(state)
    both = dot(jnp.concatenate([high, low], axis=0), rows, 1, 1)
    both = both[:EP] + both[EP:]
    return both if fine is None else both + dot(high, fine, 1, 1)


def causal():
    shape = (128, 128)
    return lax.broadcasted_iota(jnp.int32, shape, 0) >= lax.broadcasted_iota(jnp.int32, shape, 1)


def head_cols(h):
    return slice(h * DH, (h + 1) * DH)


def head_rows(h):
    return slice(h * F, (h + 1) * F)


def slot(h):
    return h // 8, h % 2, (h // 2) % 4


def project_kernel(tok_ref, w_ref, v_ref, proj_ref, state_ref):
    proj = dot(tok_ref[...], w_ref[...], 1, 0)
    proj_ref[...] = proj.T
    for h in range(H):
        keys = proj_ref[256 + h * F : 256 + (h + 1) * F, :]
        high, low = split(features(keys, False))
        v = v_ref[:, head_cols(h)]
        state = dot(
            jnp.concatenate([high, low], axis=1), jnp.concatenate([v, v], axis=0), 1, 0
        )
        state_ref[slot(h)] = state


def forward_kernel(proj_ref, v_ref, g_ref, prefix_ref, att_ref, gn_ref, state_ref):
    mask = causal()
    for h in range(H):
        q = proj_ref[head_rows(h), :]
        k = proj_ref[256 + h * F : 256 + (h + 1) * F, :]
        a = scores(q, k)
        kernel = jnp.where(mask, 1.0 + a + 0.5 * a * a, 0.0)
        feat = features(q, False)
        v = v_ref[:, head_cols(h)]
        numerator = dot(
            jnp.concatenate(split(kernel), axis=1), jnp.concatenate([v, v], axis=0), 1, 0
        )
        numerator += product(features(q, True), prefix_ref[slot(h)])
        inv = lax.rsqrt(jnp.mean(numerator * numerator, axis=1, keepdims=True) + EPSILON)
        normed = numerator * inv
        att_ref[:, head_cols(h)] = normed.astype(BF16)
        g = g_ref[:, head_cols(h)].astype(F32)
        gn = inv * (g - normed * jnp.mean(normed * g, axis=1, keepdims=True))
        gn_ref[:, head_cols(h)] = gn
        high, low = split(feat)
        gh, gl = split(gn)
        state_ref[slot(h)] = dot(
            jnp.concatenate([high, low, high], axis=1),
            jnp.concatenate([gh, gh, gl], axis=0),
            1,
            0,
        )


def backward_kernel(proj_ref, v_ref, gn_ref, prefix_ref, suffix_ref, gv_ref, rows_ref, acc):
    mask = causal()
    for h in range(H):
        q = proj_ref[head_rows(h), :]
        k = proj_ref[256 + h * F : 256 + (h + 1) * F, :]
        v = v_ref[:, head_cols(h)]
        gh, gl = split(gn_ref[:, head_cols(h)])
        a = scores(q, k)
        mh, ml = split(jnp.where(mask, 1.0 + a + 0.5 * a * a, 0.0))
        mixing = dot(
            jnp.concatenate([gh, gl], axis=1), jnp.concatenate([v, v], axis=1), 1, 1
        )
        sh, sl = split(jnp.where(mask, mixing * (1.0 + a) * 0.25, 0.0))
        qh, ql = split(q)
        kh, kl = split(k)
        dq = dot(jnp.concatenate([kh, kl], axis=0), sh, 1, 1)
        dq = dq[:F] + dq[F:] + dot(kh, sl, 1, 1)
        dk = dot(jnp.concatenate([qh, ql], axis=0), sh, 1, 0)
        dk = dk[:F] + dk[F:] + dot(qh, sl, 1, 0)
        pre = prefix_ref[slot(h)]
        suf = suffix_ref[slot(h)]
        acc[head_rows(h), :] = dq + pull_features(q, pulled(pre, gh, gl))
        acc[256 + h * F : 256 + (h + 1) * F, :] = dk + pull_features(k, pulled(suf, v))
        gv = dot(
            jnp.concatenate([mh, ml, mh], axis=0), jnp.concatenate([gh, gh, gl], axis=0), 0, 0
        )
        gv += product(features(k, True), suf)
        gv_ref[:, head_cols(h)] = gv.astype(BF16)
    rows_ref[...] = acc[...].T.astype(BF16)


def plain(kernel, outs, args, scratch=(), name=None):
    return pl.pallas_call(
        kernel,
        out_shape=outs,
        in_specs=[VMEM] * len(args),
        out_specs=jax.tree.map(lambda _: VMEM, outs),
        scratch_shapes=list(scratch),
        name=name,
    )(*args)


def shaped(shape, dtype):
    return jax.ShapeDtypeStruct(shape, dtype)


def local(tokens, proj_weight, values, grad_out):
    tok, val, up = tokens[0], values[0], grad_out[0]
    rows = tok.shape[0]
    packed = shaped((2, NC, NY, RC, DH), F32)
    weight = gather_weight(proj_weight)
    proj, state = plain(
        project_kernel, (shaped((2 * H * F, rows), F32), packed), (tok, weight, val), name="project"
    )
    early = ((0, 0), (0, 1), (0, 3), (1, 0), (1, 2))
    late = ((0, 2), (1, 1), (1, 3))
    prefix, cols_early = scan(state, False, 1, tok, early)
    attended, grad_num, carried = plain(
        forward_kernel,
        (shaped(val.shape, BF16), shaped(val.shape, F32), packed),
        (proj, val, up, prefix),
        name="forward",
    )
    suffix, cols_late = scan(carried, True, 2, tok, late)
    grad_values, grad_rows = plain(
        backward_kernel,
        (shaped(val.shape, BF16), shaped((rows, 2 * H * F), BF16)),
        (proj, val, grad_num, prefix, suffix),
        scratch=[pltpu.VMEM((2 * H * F, rows), F32)],
        name="backward",
    )
    grad_tokens, grad_proj = tail(grad_rows, cols_early, cols_late, early + late, weight)
    return (attended[None], grad_tokens[None], grad_values[None], grad_proj)


def solution(mesh):
    return jax.shard_map(
        local,
        mesh=mesh,
        in_specs=(P("dp", "ctx", None), P("dp", None), P("dp", "ctx", None), P("dp", "ctx", None)),
        out_specs=(
            P("dp", "ctx", None),
            P("dp", "ctx", None),
            P("dp", "ctx", None),
            P(("dp", "ctx"), None),
        ),
        check_vma=False,
    )
```

```python
import functools

import jax
import jax.numpy as jnp
from jax import lax
from jax.experimental import pallas as pl
from jax.experimental.pallas import tpu as pltpu
from jax.sharding import PartitionSpec as P

H = 8
F = 16
DH = 128
EP = 160
QUAD = 1.0 / 32.0
EPSILON = 1e-05
MESH = pl.DeviceIdType.MESH
F32 = jnp.float32
BF16 = jnp.bfloat16
VMEM = pl.BlockSpec(memory_space=pltpu.VMEM)
NY = 4
NZ = 4
NDP = 8
NC = 2
RC = 2 * EP // NC
HF = H * F
HD = H * DH


def dot(lhs, rhs, left, right):
    return lax.dot_general(lhs, rhs, (((left,), (right,)), ((), ())), preferred_element_type=F32)


def remote(src, dst, send, recv, **where):
    return pltpu.make_async_remote_copy(
        src_ref=src, dst_ref=dst, send_sem=send, recv_sem=recv, device_id=where, device_id_type=MESH
    )


def greet(peers):
    barrier = pltpu.get_barrier_semaphore()
    for where in peers:
        pl.semaphore_signal(barrier, inc=1, device_id=where, device_id_type=MESH)
    pl.semaphore_wait(barrier, len(peers))


def across(dp, dz, dx):
    return (dp // 4 + dz) % 2 * 4 + (dp % 4 + dx + 4) % 4


def place():
    ctx = lax.axis_index("ctx")
    return ctx // 8, (ctx // 2) % 4, ctx % 2


def at(z, y, c):
    return z * 8 + y * 2 + c


class Wires:
    def __init__(self, send, recv):
        self.send, self.recv, self.copies = send, recv, []

    def push(self, src, dst, **where):
        n = len(self.copies)
        copy = remote(src, dst, self.send.at[n], self.recv.at[n], **where)
        copy.start()
        self.copies.append(copy)
        return copy

    def drain(self):
        for copy in self.copies:
            copy.wait_send()


def gather_kernel(w_ref, tok_ref, v_ref, g_ref, out_ref, tok2_ref, v2_ref, g2_ref, own_sem, send, recv):
    dp = lax.axis_index("dp")
    z, y, c = place()
    partner = at(z, y, 1 - c)
    up, down = at(z, (y + 1) % NY, c), at(z, (y + 3) % NY, c)
    right, left, other = across(dp, 0, 1), across(dp, 0, 3), across(dp, 1, 0)
    rows = w_ref.shape[0]
    wide = rows // 2
    thin = wide // NY
    wires = Wires(send, recv)
    mine = pl.ds(pl.multiple_of(dp * rows, rows), rows)
    for n in range(2):
        columns = pl.ds(pl.multiple_of(n * 2 * HF + c * HF, HF), HF)
        out_ref[mine, n * HF : (n + 1) * HF] = w_ref[:, columns]
    greet(
        [{"dp": right}, {"dp": left}, {"dp": other}, {"ctx": partner}, {"ctx": up}, {"ctx": down}]
    )

    def part(owner, start, size):
        return out_ref.at[pl.ds(pl.multiple_of(owner * rows + start, thin // 2), size)]

    base_a, base_b = 0, wide

    def own_sends(start, size):
        src = dst = part(dp, start, size)
        return (
            wires.push(src, dst, dp=other),
            wires.push(src, dst, dp=right),
            wires.push(src, dst, dp=left),
        )

    def pass_on(owner, start, size):
        piece = part(owner, start, size)
        return wires.push(piece, piece, dp=right), wires.push(piece, piece, dp=left)

    def relay(near, far, start, size):
        one = part(near, start, size // 2)
        two = part(far, start + size // 2, size // 2)
        return wires.push(one, one, dp=right), wires.push(two, two, dp=left)

    def over_y(owner):
        piece = part(owner, base_b + y * thin, thin)
        return wires.push(piece, piece, ctx=up), wires.push(piece, piece, ctx=down)

    mine_b = base_b + y * thin
    b_over, b_right, b_left = own_sends(mine_b, thin)
    a_over, a_right, a_left = own_sends(base_a, wide)
    count = tok_ref.shape[0]
    ours = pl.ds(pl.multiple_of(c * count, count), count)
    own_half = pl.ds(pl.multiple_of(c * HD, HD), HD)
    their_half = pl.ds(pl.multiple_of((1 - c) * HD, HD), HD)
    last = [
        wires.push(v_ref.at[:, their_half], v2_ref.at[ours], ctx=partner),
        wires.push(g_ref.at[:, their_half], g2_ref.at[ours], ctx=partner),
        wires.push(tok_ref, tok2_ref.at[ours], ctx=partner),
    ]
    own = [
        pltpu.make_async_copy(v_ref.at[:, own_half], v2_ref.at[ours], own_sem.at[0]),
        pltpu.make_async_copy(g_ref.at[:, own_half], g2_ref.at[ours], own_sem.at[1]),
        pltpu.make_async_copy(tok_ref, tok2_ref.at[ours], own_sem.at[2]),
    ]
    for copy in own:
        copy.start()
    owners = [other, left, right, across(dp, 1, 3), across(dp, 1, 1), across(dp, 0, 2), across(dp, 1, 2)]
    chain_y = []
    b_over.wait_recv()
    b_right2, b_left2 = pass_on(other, mine_b, thin)
    chain_y.append(over_y(owners[0]))
    b_right.wait_recv()
    b_left.wait_recv()
    b_ends = relay(left, right, mine_b, thin)
    chain_y.append(over_y(owners[1]))
    chain_y.append(over_y(owners[2]))
    a_over.wait_recv()
    a_right2, a_left2 = pass_on(other, base_a, wide)
    b_right2.wait_recv()
    b_left2.wait_recv()
    b_ends2 = relay(owners[3], owners[4], mine_b, thin)
    chain_y.append(over_y(owners[3]))
    chain_y.append(over_y(owners[4]))
    a_right.wait_recv()
    a_left.wait_recv()
    a_ends = relay(left, right, base_a, wide)
    for copy in b_ends:
        copy.wait_recv()
    chain_y.append(over_y(owners[5]))
    for copy in b_ends2:
        copy.wait_recv()
    chain_y.append(over_y(owners[6]))
    ends_y = []
    below = base_b + (y + 3) % NY * thin
    above = base_b + (y + 1) % NY * thin + thin // 2

    def relay_y(n):
        chain_y[n][0].wait_recv()
        one = part(owners[n], below, thin // 2)
        ends_y.append([wires.push(one, one, ctx=up)])
        chain_y[n][1].wait_recv()
        two = part(owners[n], above, thin // 2)
        ends_y[-1].append(wires.push(two, two, ctx=down))

    for n in range(3):
        relay_y(n)
    a_right2.wait_recv()
    a_left2.wait_recv()
    a_ends2 = relay(owners[3], owners[4], base_a, wide)
    for n in range(3, 7):
        relay_y(n)
    for copies in ends_y + [a_ends, a_ends2, last]:
        for copy in copies:
            copy.wait_recv()
    wires.drain()
    for copy in own:
        copy.wait()


def gather(w, tokens, values, grad_out):
    count = 2 * tokens.shape[0]
    return pl.pallas_call(
        gather_kernel,
        out_shape=(
            jax.ShapeDtypeStruct((NDP * w.shape[0], 2 * HF), w.dtype),
            jax.ShapeDtypeStruct((count, tokens.shape[1]), BF16),
            jax.ShapeDtypeStruct((count, HD), BF16),
            jax.ShapeDtypeStruct((count, HD), BF16),
        ),
        in_specs=[VMEM] * 4,
        out_specs=(VMEM,) * 4,
        scratch_shapes=[pltpu.SemaphoreType.DMA((3,))] + [pltpu.SemaphoreType.DMA((52,))] * 2,
        compiler_params=pltpu.CompilerParams(collective_id=0, has_side_effects=True),
        name="gather",
    )(w, tokens, values, grad_out)


def scan_kernel(
    later, slots, across_chip, s_ref, tok_ref, side_ref, out_ref, cols_ref, far_ref,
    yin, tz, zin, yout, pre, hop_y, hop_b, send, recv, send_t, recv_t, own_t,
):
    z, y, c = place()
    dp = lax.axis_index("dp")
    partner = at(z, y, 1 - c)
    up, down = at(z, (y + 1) % NY, c), at(z, (y + 3) % NY, c)
    fore, back = at((z + 1) % NZ, y, c), at((z + 3) % NZ, y, c)
    moves = [move for move in slots if move != (0, 0)]
    met = sorted({(dz, step % 4) for dz, dx in moves for step in (dx, -dx)})
    greet(
        [{"ctx": peer} for peer in (partner, up, down, fore, back)]
        + [{"dp": across(dp, dz, dx)} for dz, dx in met]
    )
    low, high = pl.ds(0, RC // 2), pl.ds(RC // 2, RC // 2)
    wires, token_wires = Wires(send, recv), Wires(send_t, recv_t)

    def before(other, me):
        return other > me if later else other < me

    width = cols_ref.shape[2]
    own_copies = []

    def send_tokens(dz_now):
        for index, (dz, dx) in enumerate(slots):
            if dz != dz_now:
                continue
            peer = across(dp, dz, dx)
            src = tok_ref.at[:, pl.ds(pl.multiple_of(peer * width, width), width)]
            if (dz, dx) == (0, 0):
                own_copies.append(pltpu.make_async_copy(src, cols_ref.at[index], own_t))
                own_copies[-1].start()
            else:
                token_wires.push(src, cols_ref.at[index], dp=peer)

    def exchange_y(src, dst, hop, n):
        far = src.at[n, (y + 2) % NY]
        return [
            wires.push(far.at[low], hop.at[n, 0], ctx=up),
            wires.push(far.at[high], hop.at[n, 1], ctx=down),
            wires.push(src.at[n, (y + 1) % NY], dst.at[n, y], ctx=up),
            wires.push(src.at[n, (y + 3) % NY], dst.at[n, y], ctx=down),
        ]

    def relay_y(copies, dst, hop, n):
        copies[0].wait_recv()
        one = wires.push(hop.at[n, 0], dst.at[n, (y + 3) % NY, low], ctx=up)
        copies[1].wait_recv()
        two = wires.push(hop.at[n, 1], dst.at[n, (y + 1) % NY, high], ctx=down)
        return copies[2:] + [one, two]

    copies_y = []
    for n in range(NC):
        copies_y.append(exchange_y(s_ref, yin, hop_y, n))
    token_wires.push(*across_chip(side_ref, far_ref, c), ctx=partner)
    send_tokens(0)
    for n in range(NC):
        copies_y[n] = relay_y(copies_y[n], yin, hop_y, n)
    copies_z = []
    for n in range(NC):
        for copy in copies_y[n]:
            copy.wait_recv()
        blocks = [jnp.where(j == y, s_ref[n, j], yin[n, j]).astype(F32) for j in range(NY)]
        order = list(range(NY))[::-1] if later else list(range(NY))
        total = jnp.zeros_like(blocks[0])
        for j in order:
            pre[n, j] = total
            total = total + blocks[j]
        tz[n] = total.astype(BF16)
        copies_z.append(
            [
                wires.push(tz.at[n], zin.at[n, z], ctx=fore),
                wires.push(tz.at[n], zin.at[n, z], ctx=back),
            ]
        )
    for n in range(NC):
        copies_z[n][0].wait_recv()
        behind_me, ahead_me = (z + 3) % NZ, (z + 1) % NZ
        one = wires.push(zin.at[n, behind_me, low], zin.at[n, behind_me, low], ctx=fore)
        copies_z[n][1].wait_recv()
        two = wires.push(zin.at[n, ahead_me, high], zin.at[n, ahead_me, high], ctx=back)
        copies_z[n] = [one, two]
    send_tokens(1)
    copies_b = []
    for n in range(NC):
        for copy in copies_z[n]:
            copy.wait_recv()
        base = jnp.zeros(pre.shape[2:], F32)
        for j in range(NZ):
            base = base + jnp.where(before(j, z), zin[n, j].astype(F32), 0.0)
        for j in range(NY):
            yout[n, j] = (base + pre[n, j]).astype(BF16)
        out_ref[n, y] = yout[n, y]
        copies_b.append(exchange_y(yout, out_ref, hop_b, n))
    for n in range(NC):
        copies_b[n] = relay_y(copies_b[n], out_ref, hop_b, n)
    for copies in copies_b:
        for copy in copies:
            copy.wait_recv()
    wires.drain()
    for copy in token_wires.copies + own_copies:
        copy.wait()


def scan(state, later, collective, tokens, slots, side, far, across_chip):
    slab = (NC, NY, RC, DH)
    rows, width = tokens.shape
    dma = pltpu.SemaphoreType.DMA
    hbm = pl.BlockSpec(memory_space=pl.ANY)
    return pl.pallas_call(
        functools.partial(scan_kernel, later, slots, across_chip),
        out_shape=(
            jax.ShapeDtypeStruct(slab, BF16),
            jax.ShapeDtypeStruct((len(slots), rows, width // NDP), BF16),
            far,
        ),
        in_specs=[VMEM, VMEM, hbm],
        out_specs=(VMEM, VMEM, hbm),
        scratch_shapes=[
            pltpu.VMEM(slab, BF16),
            pltpu.VMEM((NC, RC, DH), BF16),
            pltpu.VMEM((NC, NZ, RC, DH), BF16),
            pltpu.VMEM(slab, BF16),
            pltpu.VMEM(slab, F32),
            pltpu.VMEM((NC, 2, RC // 2, DH), BF16),
            pltpu.VMEM((NC, 2, RC // 2, DH), BF16),
            dma((16 * NC,)),
            dma((16 * NC,)),
            dma((len(slots) + 1,)),
            dma((len(slots) + 1,)),
            dma,
        ],
        compiler_params=pltpu.CompilerParams(collective_id=collective, has_side_effects=True),
        name="scan_later" if later else "scan_earlier",
    )(state, tokens, side)


def whole(side_ref, far_ref, c):
    return side_ref, far_ref


def their_rows(side_ref, far_ref, c):
    count = far_ref.shape[0]
    return side_ref.at[pl.ds(pl.multiple_of((1 - c) * count, count), count)], far_ref


def tail_kernel(
    order, rows_ref, early_ref, late_ref, w_hbm, far_hbm, gv_ref, gt_ref, out_ref, gv_far_ref,
    w_ref, far_ref, r_ref, r_far, all_ref, g_ref, sib, pair, yin, ysum, hop, zin, send, recv, w_sem,
):
    dp = lax.axis_index("dp")
    z, y, c = place()
    partner = at(z, y, 1 - c)
    up, down = at(z, (y + 1) % NY, c), at(z, (y + 3) % NY, c)
    right, left, other = across(dp, 0, 1), across(dp, 0, 3), across(dp, 1, 0)
    greet(
        [{"dp": right}, {"dp": left}, {"dp": other}]
        + [{"ctx": peer} for peer in (partner, up, down)]
        + [{"ctx": at((z + d) % NZ, y, c)} for d in range(1, NZ)]
    )
    wires = Wires(send, recv)
    count = r_ref.shape[0]
    half = count // 2
    ours = pl.ds(pl.multiple_of(c * count, count), count)
    theirs = pl.ds(pl.multiple_of((1 - c) * count, count), count)
    swap = wires.push(rows_ref.at[theirs], r_far, ctx=partner)
    loads = [
        pltpu.make_async_copy(w_hbm, w_ref, w_sem.at[0]),
        pltpu.make_async_copy(far_hbm, far_ref, w_sem.at[1]),
    ]
    for load in loads:
        load.start()
    for n in range(2):
        columns = pl.ds(pl.multiple_of(n * 2 * HF + c * HF, HF), HF)
        r_ref[:, columns] = rows_ref[ours, n * HF : (n + 1) * HF]
    swap.wait_recv()
    for n in range(2):
        columns = pl.ds(pl.multiple_of(n * 2 * HF + (1 - c) * HF, HF), HF)
        r_ref[:, columns] = r_far[:, n * HF : (n + 1) * HF]
    low, high = pl.ds(0, half), pl.ds(half, half)
    over = wires.push(r_ref, all_ref.at[4], dp=other)
    rights = [wires.push(r_ref, all_ref.at[1], dp=right)]
    lefts = [wires.push(r_ref, all_ref.at[3], dp=left)]
    swap_values = wires.push(gv_ref.at[theirs], gv_far_ref, ctx=partner)
    early = early_ref.shape[0]

    def cols(slot_at):
        n = order.index((slot_at // 4, slot_at % 4))
        return early_ref[n] if n < early else late_ref[n - early]

    def product_of(slots):
        left_rows = jnp.concatenate([cols(n) for n in slots], axis=0)
        right_rows = jnp.concatenate([r_ref[...] if n == 0 else all_ref[n] for n in slots], axis=0)
        return dot(left_rows, right_rows, 0, 0).reshape(g_ref.shape)

    block = w_ref.shape[0] // 4

    def input_grad(n):
        span = slice(n * block, (n + 1) * block)
        piece = dot(rows_ref[ours, :], w_ref[span, :], 1, 1)
        piece += dot(r_far[...], far_ref[span, :], 1, 1)
        gt_ref[:, n * block : (n + 1) * block] = piece.astype(BF16)

    over.wait_recv()
    rights.append(wires.push(all_ref.at[4], all_ref.at[5], dp=right))
    lefts.append(wires.push(all_ref.at[4], all_ref.at[7], dp=left))
    for load in loads:
        load.wait()
    input_grad(0)
    ends = []
    for n in range(2):
        rights[n].wait_recv()
        one = wires.push(all_ref.at[4 * n + 1, low], all_ref.at[4 * n + 2, low], dp=right)
        lefts[n].wait_recv()
        two = wires.push(all_ref.at[4 * n + 3, high], all_ref.at[4 * n + 2, high], dp=left)
        ends.append((one, two))
        input_grad(2 * n + 1)
        if n == 0:
            g_ref[...] = product_of((0, 1, 3, 4))
            input_grad(2)
    for pair_of in ends:
        for copy in pair_of:
            copy.wait_recv()
    g_ref[...] += product_of((2, 5, 6, 7))

    copies_c = {}
    for d in (2, 1, 3, 0):
        to = (y + d) % NY
        copies_c[d] = wires.push(g_ref.at[:, to, 1 - c], sib.at[to], ctx=partner)
    near = []
    for d in (2, 1, 3, 0):
        to = (y + d) % NY
        copies_c[d].wait_recv()
        both = g_ref[:, to, c] + sib[to]
        if d == 0:
            ysum[...] = both
        else:
            pair[to] = both.astype(BF16)
            if d == 2:
                far = pair.at[to]
                relays = [
                    wires.push(far.at[pl.ds(0, NZ // 2)], hop.at[0], ctx=up),
                    wires.push(far.at[pl.ds(NZ // 2, NZ // 2)], hop.at[1], ctx=down),
                ]
            else:
                near.append(wires.push(pair.at[to], yin.at[y], ctx=up if d == 1 else down))
    relays[0].wait_recv()
    near.append(wires.push(hop.at[0], yin.at[(y + 3) % NY, pl.ds(0, NZ // 2)], ctx=up))
    relays[1].wait_recv()
    near.append(wires.push(hop.at[1], yin.at[(y + 1) % NY, pl.ds(NZ // 2, NZ // 2)], ctx=down))
    for copy in near:
        copy.wait_recv()
    for j in range(NY):
        ysum[...] += jnp.where(j == y, 0.0, yin[j].astype(F32))
    copies_z = []
    for d in (2, 1, 3):
        to = (z + d) % NZ
        copies_z.append(wires.push(ysum.at[to], zin.at[z], ctx=at(to, y, c)))
    for copy in copies_z:
        copy.wait_recv()
    total = ysum[z]
    for j in range(NZ):
        total = total + jnp.where(j == z, 0.0, zin[j])
    out_ref[...] = total
    swap_values.wait_recv()
    wires.drain()


def tail(rows, early, late, order, weight, weight_far, grad_values):
    count, width = rows.shape[0] // 2, 2 * rows.shape[1]
    hbm = pl.BlockSpec(memory_space=pl.ANY)
    own = early.shape[2] // (2 * NY * NZ)
    slab = (NY, NZ, own, width)
    dma = pltpu.SemaphoreType.DMA
    return pl.pallas_call(
        functools.partial(tail_kernel, order),
        out_shape=(
            jax.ShapeDtypeStruct((count, weight.shape[0]), BF16),
            jax.ShapeDtypeStruct((own, width), F32),
            jax.ShapeDtypeStruct((count, HD), BF16),
        ),
        in_specs=[VMEM, VMEM, VMEM, hbm, hbm, hbm],
        out_specs=(VMEM, VMEM, hbm),
        scratch_shapes=[
            pltpu.VMEM(weight.shape, BF16),
            pltpu.VMEM(weight.shape, BF16),
            pltpu.VMEM((count, width), BF16),
            pltpu.VMEM((count, width // 2), BF16),
            pltpu.VMEM((NDP, count, width), BF16),
            pltpu.VMEM((NZ, NY, 2, own, width), F32),
            pltpu.VMEM(slab, F32),
            pltpu.VMEM(slab, BF16),
            pltpu.VMEM(slab, BF16),
            pltpu.VMEM((NZ, own, width), F32),
            pltpu.VMEM((2, NZ // 2, own, width), BF16),
            pltpu.VMEM((NZ, own, width), F32),
            dma((24,)),
            dma((24,)),
            dma((2,)),
        ],
        compiler_params=pltpu.CompilerParams(collective_id=3, has_side_effects=True),
        name="tail",
    )(rows, early, late, weight, weight_far, grad_values)


def ahead(x, d):
    return pltpu.roll(x, F - d, 0)


def behind(x, d):
    return pltpu.roll(x, d, 0)


def features(x, weighted):
    quad, linear = (QUAD, 0.25) if weighted else (1.0, 1.0)
    twice = 2.0 * quad if weighted else 1.0
    parts = [x * x * quad] + [x * ahead(x, d) * twice for d in range(1, 8)]
    parts += [x[:8] * x[8:] * twice, x * linear]
    row = lax.broadcasted_iota(jnp.int32, (8, x.shape[1]), 0)
    parts.append(jnp.where(row == 0, 1.0, 0.0))
    return jnp.concatenate(parts, axis=0)


def pull_features(x, cot):
    out = 2.0 * QUAD * cot[:F] * x
    for d in range(1, 8):
        part = 2.0 * QUAD * cot[F * d : F * (d + 1)]
        out = out + part * ahead(x, d) + behind(part * x, d)
    half = 2.0 * QUAD * cot[128:136]
    out = out + jnp.concatenate([half * x[8:], half * x[:8]], axis=0)
    return out + 0.25 * cot[136:152]


def split(x):
    high = x.astype(BF16)
    return high, (x - high.astype(F32)).astype(BF16)


def scores(q, k):
    qh, ql = split(q)
    kh, kl = split(k)
    left = jnp.concatenate([qh, qh, ql, ql], axis=0)
    right = jnp.concatenate([kh, kl, kh, kl], axis=0)
    return dot(left, right, 0, 0) * 0.25


def product(feat, state):
    return dot(jnp.concatenate(split(feat), axis=0), jnp.concatenate([state, state], axis=0), 0, 0)


def causal():
    shape = (256, 256)
    return lax.broadcasted_iota(jnp.int32, shape, 0) >= lax.broadcasted_iota(jnp.int32, shape, 1)


def head_cols(h):
    return slice(h * DH, (h + 1) * DH)


def head_rows(h):
    return slice(h * F, (h + 1) * F)


def slot(h):
    return h % 2, h // 2


def project_kernel(tok_ref, w_ref, v_ref, proj_ref, state_ref):
    proj = dot(tok_ref[...], w_ref[...], 1, 0)
    proj_ref[...] = proj.T
    for h in range(H):
        keys = proj_ref[HF + h * F : HF + (h + 1) * F, :]
        high, low = split(features(keys, False))
        v = v_ref[:, head_cols(h)]
        state = dot(
            jnp.concatenate([high, low], axis=1), jnp.concatenate([v, v], axis=0), 1, 0
        )
        state_ref[slot(h)] = state.astype(BF16)


def forward_kernel(proj_ref, v_ref, g_ref, prefix_ref, att_ref, gn_ref, state_ref):
    mask = causal()
    for h in range(H):
        q = proj_ref[head_rows(h), :]
        k = proj_ref[HF + h * F : HF + (h + 1) * F, :]
        a = scores(q, k)
        kernel = jnp.where(mask, 1.0 + a + 0.5 * a * a, 0.0)
        feat = features(q, False)
        v = v_ref[:, head_cols(h)]
        numerator = dot(
            jnp.concatenate(split(kernel), axis=1), jnp.concatenate([v, v], axis=0), 1, 0
        )
        numerator += product(features(q, True), prefix_ref[slot(h)])
        inv = lax.rsqrt(jnp.mean(numerator * numerator, axis=1, keepdims=True) + EPSILON)
        normed = numerator * inv
        att_ref[:, head_cols(h)] = normed.astype(BF16)
        g = g_ref[:, head_cols(h)].astype(F32)
        gn = inv * (g - normed * jnp.mean(normed * g, axis=1, keepdims=True))
        gn_ref[:, head_cols(h)] = gn
        high, low = split(feat)
        gh, gl = split(gn)
        state_ref[slot(h)] = dot(
            jnp.concatenate([high, low, high], axis=1),
            jnp.concatenate([gh, gh, gl], axis=0),
            1,
            0,
        ).astype(BF16)


def backward_kernel(proj_ref, v_ref, gn_ref, prefix_ref, suffix_ref, gv_ref, rows_ref, acc):
    mask = causal()
    for h in range(H):
        q = proj_ref[head_rows(h), :]
        k = proj_ref[HF + h * F : HF + (h + 1) * F, :]
        v = v_ref[:, head_cols(h)]
        gh, gl = split(gn_ref[:, head_cols(h)])
        a = scores(q, k)
        mh, ml = split(jnp.where(mask, 1.0 + a + 0.5 * a * a, 0.0))
        mixing = dot(
            jnp.concatenate([gh, gl], axis=1), jnp.concatenate([v, v], axis=1), 1, 1
        )
        sh, sl = split(jnp.where(mask, mixing * (1.0 + a) * 0.25, 0.0))
        qh, ql = split(q)
        kh, kl = split(k)
        dq = dot(jnp.concatenate([kh, kl], axis=0), sh, 1, 1)
        dq = dq[:F] + dq[F:] + dot(kh, sl, 1, 1)
        dk = dot(jnp.concatenate([qh, ql], axis=0), sh, 1, 0)
        dk = dk[:F] + dk[F:] + dot(qh, sl, 1, 0)
        pre = prefix_ref[slot(h)]
        suf = suffix_ref[slot(h)]
        acc[head_rows(h), :] = dq + pull_features(q, dot(jnp.concatenate([pre, pre], axis=1), jnp.concatenate([gh, gl], axis=1), 1, 1))
        acc[HF + h * F : HF + (h + 1) * F, :] = dk + pull_features(k, dot(suf, v, 1, 1))
        gv = dot(
            jnp.concatenate([mh, ml, mh], axis=0), jnp.concatenate([gh, gh, gl], axis=0), 0, 0
        )
        gv += product(features(k, True), suf)
        gv_ref[:, head_cols(h)] = gv.astype(BF16)
    rows_ref[...] = acc[...].T.astype(BF16)


def plain(kernel, outs, args, scratch=(), name=None):
    return pl.pallas_call(
        kernel,
        out_shape=outs,
        in_specs=[VMEM] * len(args),
        out_specs=jax.tree.map(lambda _: VMEM, outs),
        scratch_shapes=list(scratch),
        name=name,
    )(*args)


def shaped(shape, dtype):
    return jax.ShapeDtypeStruct(shape, dtype)


def joined(c, mine, far):
    pair = jnp.where(c == 0, jnp.concatenate([mine, far], axis=1), jnp.concatenate([far, mine], axis=1))
    return pair[None]


def local(tokens, proj_weight, values, grad_out):
    c = lax.axis_index("ctx") % 2
    tok = tokens[0]
    count = tok.shape[0]
    packed = shaped((NC, NY, RC, DH), BF16)
    weight, tok2, val, up = gather(proj_weight, tok, values[0], grad_out[0])
    proj, state = plain(
        project_kernel, (shaped((2 * HF, 2 * count), F32), packed), (tok2, weight, val), name="project"
    )
    early = ((0, 0), (0, 1), (0, 3), (1, 0), (1, 2))
    late = ((0, 2), (1, 1), (1, 3))
    prefix, cols_early, weight_far = scan(
        state, False, 1, tok, early, weight, shaped(weight.shape, BF16), whole
    )
    attended, grad_num, carried = plain(
        forward_kernel,
        (shaped(val.shape, BF16), shaped(val.shape, F32), packed),
        (proj, val, up, prefix),
        name="forward",
    )
    suffix, cols_late, attended_far = scan(
        carried, True, 2, tok, late, attended, shaped((count, HD), BF16), their_rows
    )
    grad_values, grad_rows = plain(
        backward_kernel,
        (shaped(val.shape, BF16), shaped((2 * count, 2 * HF), BF16)),
        (proj, val, grad_num, prefix, suffix),
        scratch=[pltpu.VMEM((2 * HF, 2 * count), F32)],
        name="backward",
    )
    grad_tokens, grad_proj, values_far = tail(
        grad_rows, cols_early, cols_late, early + late, weight, weight_far, grad_values
    )
    attended = joined(c, lax.dynamic_slice_in_dim(attended, c * count, count), attended_far)
    grad_values = joined(c, lax.dynamic_slice_in_dim(grad_values, c * count, count), values_far)
    return (attended, grad_tokens[None], grad_values, grad_proj)


def solution(mesh):
    return jax.shard_map(
        local,
        mesh=mesh,
        in_specs=(P("dp", "ctx", None), P("dp", None), P("dp", "ctx", None), P("dp", "ctx", None)),
        out_specs=(
            P("dp", "ctx", None),
            P("dp", "ctx", None),
            P("dp", "ctx", None),
            P(("dp", "ctx"), None),
        ),
        check_vma=False,
    )
```

```python
import jax
import jax.numpy as jnp
from jax import lax
from jax.experimental import pallas as pl
from jax.experimental.pallas import tpu as pltpu
from jax.sharding import PartitionSpec as P

H = 8
F = 16
DH = 128
EP = 160
QUAD = 1.0 / 32.0
EPSILON = 1e-05
MESH = pl.DeviceIdType.MESH
F32 = jnp.float32
BF16 = jnp.bfloat16
VMEM = pl.BlockSpec(memory_space=pltpu.VMEM)
NY = 4
NZ = 4
NDP = 8
RC = 2 * EP
HF = H * F
HD = H * DH


def dot(lhs, rhs, left, right):
    return lax.dot_general(lhs, rhs, (((left,), (right,)), ((), ())), preferred_element_type=F32)


def remote(src, dst, send, recv, **where):
    return pltpu.make_async_remote_copy(
        src_ref=src, dst_ref=dst, send_sem=send, recv_sem=recv, device_id=where, device_id_type=MESH
    )


def greet(peers):
    barrier = pltpu.get_barrier_semaphore()
    for where in peers:
        pl.semaphore_signal(barrier, inc=1, device_id=where, device_id_type=MESH)
    pl.semaphore_wait(barrier, len(peers))


def across(dp, dz, dx):
    return (dp // 4 + dz) % 2 * 4 + (dp % 4 + dx + 4) % 4


def place():
    ctx = lax.axis_index("ctx")
    return ctx // 8, (ctx // 2) % 4, ctx % 2


def at(z, y, c):
    return z * 8 + y * 2 + c


class Wires:
    def __init__(self, send, recv):
        self.send, self.recv, self.copies = send, recv, []

    def push(self, src, dst, **where):
        n = len(self.copies)
        copy = remote(src, dst, self.send.at[n], self.recv.at[n], **where)
        copy.start()
        self.copies.append(copy)
        return copy

    def drain(self):
        for copy in self.copies:
            copy.wait_send()


def ahead(x, d):
    return pltpu.roll(x, F - d, 0)


def behind(x, d):
    return pltpu.roll(x, d, 0)


def features(x, weighted):
    quad, linear = (QUAD, 0.25) if weighted else (1.0, 1.0)
    twice = 2.0 * quad if weighted else 1.0
    parts = [x * x * quad] + [x * ahead(x, d) * twice for d in range(1, 8)]
    parts += [x[:8] * x[8:] * twice, x * linear]
    row = lax.broadcasted_iota(jnp.int32, (8, x.shape[1]), 0)
    parts.append(jnp.where(row == 0, 1.0, 0.0))
    return jnp.concatenate(parts, axis=0)


def pull_features(x, cot):
    out = 2.0 * QUAD * cot[:F] * x
    for d in range(1, 8):
        part = 2.0 * QUAD * cot[F * d : F * (d + 1)]
        out = out + part * ahead(x, d) + behind(part * x, d)
    half = 2.0 * QUAD * cot[128:136]
    out = out + jnp.concatenate([half * x[8:], half * x[:8]], axis=0)
    return out + 0.25 * cot[136:152]


def split(x):
    high = x.astype(BF16)
    return high, (x - high.astype(F32)).astype(BF16)


def scores(q, k):
    qh, ql = split(q)
    kh, kl = split(k)
    left = jnp.concatenate([qh, qh, ql, ql], axis=0)
    right = jnp.concatenate([kh, kl, kh, kl], axis=0)
    return dot(left, right, 0, 0) * 0.25


def product(feat, state):
    return dot(jnp.concatenate(split(feat), axis=0), jnp.concatenate([state, state], axis=0), 0, 0)


def causal():
    shape = (256, 256)
    return lax.broadcasted_iota(jnp.int32, shape, 0) >= lax.broadcasted_iota(jnp.int32, shape, 1)


def head_cols(h):
    return slice(h * DH, (h + 1) * DH)


def head_rows(h):
    return slice(h * F, (h + 1) * F)


def rows_of(h):
    return h // 2, slice(h % 2 * EP, (h % 2 + 1) * EP)


def aligned(start, size, step=None):
    return pl.ds(pl.multiple_of(start, step or size), size)


def layer_kernel(
    w_ref, tok_ref, v_ref, g_ref, att_ref, gt_ref, gv_ref, gp_ref,
    wc, w_far, tok2, v2, g2, proj, projt, state, yin, tz, zin, yout, pre, prefix, suffix,
    carried, yin_b, zin_b, yout_b, tz_b, work, gn, att2, gv2, acc, rows2, r_far, r_all, cols,
    all_ref, grad, sib, pair, yred, ysum, zred, send, recv, local_sem,
):
    dp = lax.axis_index("dp")
    z, y, c = place()
    partner = at(z, y, 1 - c)
    up, down = at(z, (y + 1) % NY, c), at(z, (y + 3) % NY, c)
    right, left, other = across(dp, 0, 1), across(dp, 0, 3), across(dp, 1, 0)
    count = tok_ref.shape[0]
    rows = w_ref.shape[0]
    ours = aligned(c * count, count)
    theirs = aligned((1 - c) * count, count)
    own_half = aligned(c * HD, HD)
    their_half = aligned((1 - c) * HD, HD)
    wires = Wires(send, recv)
    locals_ = []

    def copy_here(src, dst):
        copy = pltpu.make_async_copy(src, dst, local_sem.at[len(locals_)])
        copy.start()
        locals_.append(copy)
        return copy

    own_rows = aligned(dp * rows, rows)
    for n in range(2):
        wc[own_rows, n * HF : (n + 1) * HF] = w_ref[:, aligned(n * 2 * HF + c * HF, HF)]
    greet(
        [{"ctx": partner}]
        + [{"ctx": at(z, (y + d) % NY, c)} for d in range(1, NY)]
        + [{"ctx": at((z + d) % NZ, y, c)} for d in range(1, NZ)]
        + [{"dp": across(dp, n // 4, n % 4)} for n in range(1, NDP)]
    )

    wide = rows // 2
    thin = wide // NY
    base_a, base_b = 0, wide

    def part(owner, start, size):
        return wc.at[aligned(owner * rows + start, size, thin // 2)]

    def own_sends(start, size):
        piece = part(dp, start, size)
        return [wires.push(piece, piece, dp=to) for to in (other, right, left)]

    def pass_on(owner, start, size):
        piece = part(owner, start, size)
        return wires.push(piece, piece, dp=right), wires.push(piece, piece, dp=left)

    def relay(near, far, start, size):
        one = part(near, start, size // 2)
        two = part(far, start + size // 2, size // 2)
        return wires.push(one, one, dp=right), wires.push(two, two, dp=left)

    def over_y(owner):
        piece = part(owner, base_b + y * thin, thin)
        return wires.push(piece, piece, ctx=up), wires.push(piece, piece, ctx=down)

    mine_b = base_b + y * thin
    b_over, b_right, b_left = own_sends(mine_b, thin)
    a_over, a_right, a_left = own_sends(base_a, wide)
    from_partner = [
        wires.push(tok_ref, tok2.at[ours], ctx=partner),
        wires.push(v_ref.at[:, their_half], v2.at[ours], ctx=partner),
        wires.push(g_ref.at[:, their_half], g2.at[ours], ctx=partner),
    ]
    here = [
        copy_here(tok_ref, tok2.at[ours]),
        copy_here(v_ref.at[:, own_half], v2.at[ours]),
        copy_here(g_ref.at[:, own_half], g2.at[ours]),
    ]
    owners = [other, left, right] + [across(dp, dz, dx) for dz, dx in ((1, 3), (1, 1), (0, 2), (1, 2))]
    chain_y = []
    b_over.wait_recv()
    b_right2, b_left2 = pass_on(other, mine_b, thin)
    chain_y.append(over_y(owners[0]))
    b_right.wait_recv()
    b_left.wait_recv()
    b_ends = relay(left, right, mine_b, thin)
    chain_y.append(over_y(owners[1]))
    chain_y.append(over_y(owners[2]))
    a_over.wait_recv()
    a_right2, a_left2 = pass_on(other, base_a, wide)
    b_right2.wait_recv()
    b_left2.wait_recv()
    b_ends2 = relay(owners[3], owners[4], mine_b, thin)
    chain_y.append(over_y(owners[3]))
    chain_y.append(over_y(owners[4]))
    a_right.wait_recv()
    a_left.wait_recv()
    a_ends = relay(left, right, base_a, wide)
    for copy in b_ends:
        copy.wait_recv()
    chain_y.append(over_y(owners[5]))
    for copy in b_ends2:
        copy.wait_recv()
    chain_y.append(over_y(owners[6]))
    ends_y = []
    below = base_b + (y + 3) % NY * thin
    above = base_b + (y + 1) % NY * thin + thin // 2

    def relay_y(n):
        chain_y[n][0].wait_recv()
        one = part(owners[n], below, thin // 2)
        ends_y.append([wires.push(one, one, ctx=up)])
        chain_y[n][1].wait_recv()
        two = part(owners[n], above, thin // 2)
        ends_y[-1].append(wires.push(two, two, ctx=down))

    for n in range(3):
        relay_y(n)
    a_right2.wait_recv()
    a_left2.wait_recv()
    a_ends2 = relay(owners[3], owners[4], base_a, wide)
    for n in range(3, 7):
        relay_y(n)

    def project(owner):
        return dot(
            tok2[:, aligned(owner * rows, rows)], wc[aligned(owner * rows, rows), :], 1, 0
        )

    for copy in from_partner:
        copy.wait_recv()
    for copy in here:
        copy.wait()
    proj[...] = project(dp)
    for n in range(7):
        for copy in ends_y[n]:
            copy.wait_recv()
        if n == 5:
            for copy in a_ends:
                copy.wait_recv()
        if n == 6:
            for copy in a_ends2:
                copy.wait_recv()
        proj[...] += project(owners[n])
    far_weight = wires.push(wc, w_far, ctx=partner)
    width = cols.shape[2]
    token_copies = []

    def send_tokens(slots):
        for n in slots:
            peer = across(dp, n // 4, n % 4)
            token_copies.append(
                wires.push(tok_ref.at[:, aligned(peer * width, width)], cols.at[n], dp=peer)
            )

    projt[...] = proj[...].T

    def query(h):
        return projt[h * F : (h + 1) * F, :]

    def key(h):
        return projt[HF + h * F : HF + (h + 1) * F, :]

    def head(h):
        return slice(h * DH, (h + 1) * DH)

    for h in range(H):
        high, low = split(features(key(h), False))
        v = v2[:, head(h)]
        new = dot(jnp.concatenate([high, low], axis=1), jnp.concatenate([v, v], axis=0), 1, 0)
        j, at_rows = rows_of(h)
        state[j, at_rows, :] = new.astype(BF16)

    def scan(later, src, land, total_ref, planes, out, result, fill_y, fill_z):
        copies = []
        for d in (2, 1, 3):
            to = (y + d) % NY
            copies.append(wires.push(src.at[to], land.at[y], ctx=at(z, to, c)))
        fill_y()
        for copy in copies:
            copy.wait_recv()
        total = jnp.zeros(pre.shape[1:], F32)
        for j in list(range(NY))[::-1] if later else range(NY):
            pre[j] = total
            total = total + jnp.where(j == y, src[j], land[j]).astype(F32)
        total_ref[...] = total.astype(BF16)
        copies = []
        for d in (2, 1, 3):
            to = (z + d) % NZ
            copies.append(wires.push(total_ref, planes.at[z], ctx=at(to, y, c)))
        fill_z()
        for copy in copies:
            copy.wait_recv()
        base = jnp.zeros(pre.shape[1:], F32)
        for j in range(NZ):
            wanted = (j > z) if later else (j < z)
            base = base + jnp.where(wanted, planes[j].astype(F32), 0.0)
        for j in range(NY):
            out[j] = (base + pre[j]).astype(BF16)
        copies = []
        for d in (2, 1, 3):
            to = (y + d) % NY
            copies.append(wires.push(out.at[to], result.at[y], ctx=at(z, to, c)))
        result[y] = out[y]
        for copy in copies:
            copy.wait_recv()

    mask = causal()

    def local_numerator(h):
        a = scores(query(h), key(h))
        kernel = jnp.where(mask, 1.0 + a + 0.5 * a * a, 0.0)
        v = v2[:, head(h)]
        work[:, head(h)] = dot(
            jnp.concatenate(split(kernel), axis=1), jnp.concatenate([v, v], axis=0), 1, 0
        )

    def first_fill():
        send_tokens((1, 2, 3))
        for h in range(3):
            local_numerator(h)

    def second_fill():
        send_tokens((4, 5, 6, 7))
        for h in range(3, H):
            local_numerator(h)

    scan(False, state, yin, tz, zin, yout, prefix, first_fill, second_fill)

    for h in range(H):
        j, at_rows = rows_of(h)
        q = query(h)
        numerator = work[:, head(h)] + product(features(q, True), prefix[j, at_rows, :])
        inv = lax.rsqrt(jnp.mean(numerator * numerator, axis=1, keepdims=True) + EPSILON)
        normed = numerator * inv
        att2[:, head(h)] = normed.astype(BF16)
        g = g2[:, head(h)].astype(F32)
        grad_num = inv * (g - normed * jnp.mean(normed * g, axis=1, keepdims=True))
        gn[:, head(h)] = grad_num
        high, low = split(features(q, False))
        gh, gl = split(grad_num)
        new = dot(
            jnp.concatenate([high, low, high], axis=1), jnp.concatenate([gh, gh, gl], axis=0), 1, 0
        )
        carried[j, at_rows, :] = new.astype(BF16)

    def local_grads(h):
        q, k = query(h), key(h)
        v = v2[:, head(h)]
        gh, gl = split(gn[:, head(h)])
        a = scores(q, k)
        mh, ml = split(jnp.where(mask, 1.0 + a + 0.5 * a * a, 0.0))
        mixing = dot(
            jnp.concatenate([gh, gl], axis=1), jnp.concatenate([v, v], axis=1), 1, 1
        )
        sh, sl = split(jnp.where(mask, mixing * (1.0 + a) * 0.25, 0.0))
        qh, ql = split(q)
        kh, kl = split(k)
        dq = dot(jnp.concatenate([kh, kl], axis=0), sh, 1, 1)
        dq = dq[:F] + dq[F:] + dot(kh, sl, 1, 1)
        dk = dot(jnp.concatenate([qh, ql], axis=0), sh, 1, 0)
        dk = dk[:F] + dk[F:] + dot(qh, sl, 1, 0)
        j, at_rows = rows_of(h)
        before = prefix[j, at_rows, :]
        pulled = dot(
            jnp.concatenate([before, before], axis=1), jnp.concatenate([gh, gl], axis=1), 1, 1
        )
        acc[h * F : (h + 1) * F, :] = dq + pull_features(q, pulled)
        acc[HF + h * F : HF + (h + 1) * F, :] = dk
        work[:, head(h)] = dot(
            jnp.concatenate([mh, ml, mh], axis=0), jnp.concatenate([gh, gh, gl], axis=0), 0, 0
        )

    outs = []

    def third_fill():
        outs.append(wires.push(att2.at[theirs], att_ref.at[:, own_half], ctx=partner))
        copy_here(att2.at[ours], att_ref.at[:, own_half])
        for h in range(3):
            local_grads(h)

    def fourth_fill():
        for h in range(3, H):
            local_grads(h)

    scan(True, carried, yin_b, tz_b, zin_b, yout_b, suffix, third_fill, fourth_fill)

    for h in range(H):
        j, at_rows = rows_of(h)
        after = suffix[j, at_rows, :]
        k = key(h)
        span = slice(HF + h * F, HF + (h + 1) * F)
        acc[span, :] = acc[span, :] + pull_features(k, dot(after, v2[:, head(h)], 1, 1))
    rows2[...] = acc[...].T.astype(BF16)

    swap = wires.push(rows2.at[theirs], r_far, ctx=partner)
    for h in range(H):
        j, at_rows = rows_of(h)
        total = work[:, head(h)] + product(features(key(h), True), suffix[j, at_rows, :])
        gv2[:, head(h)] = total.astype(BF16)
    for n in range(2):
        r_all[:, aligned(n * 2 * HF + c * HF, HF)] = rows2[ours, n * HF : (n + 1) * HF]
    swap.wait_recv()
    for n in range(2):
        r_all[:, aligned(n * 2 * HF + (1 - c) * HF, HF)] = r_far[:, n * HF : (n + 1) * HF]
    half = count // 2
    low_rows, high_rows = pl.ds(0, half), pl.ds(half, half)
    over = wires.push(r_all, all_ref.at[4], dp=other)
    rights = [wires.push(r_all, all_ref.at[1], dp=right)]
    lefts = [wires.push(r_all, all_ref.at[3], dp=left)]
    outs.append(wires.push(gv2.at[theirs], gv_ref.at[:, own_half], ctx=partner))
    copy_here(gv2.at[ours], gv_ref.at[:, own_half])
    far_weight.wait_recv()
    for copy in token_copies:
        copy.wait_recv()

    def tokens_of(n):
        if n == 0:
            return tok2[ours, aligned(dp * width, width)]
        return cols[n]

    def product_of(slots):
        left_rows = jnp.concatenate([tokens_of(n) for n in slots], axis=0)
        right_rows = jnp.concatenate([r_all[...] if n == 0 else all_ref[n] for n in slots], axis=0)
        return dot(left_rows, right_rows, 0, 0).reshape(grad.shape)

    block = wc.shape[0] // 4

    def input_grad(n):
        span = slice(n * block, (n + 1) * block)
        piece = dot(rows2[ours, :], wc[span, :], 1, 1)
        piece += dot(r_far[...], w_far[span, :], 1, 1)
        gt_ref[:, span] = piece.astype(BF16)

    over.wait_recv()
    rights.append(wires.push(all_ref.at[4], all_ref.at[5], dp=right))
    lefts.append(wires.push(all_ref.at[4], all_ref.at[7], dp=left))
    input_grad(0)
    ends = []
    for n in range(2):
        rights[n].wait_recv()
        ends.append(
            wires.push(all_ref.at[4 * n + 1, low_rows], all_ref.at[4 * n + 2, low_rows], dp=right)
        )
        lefts[n].wait_recv()
        ends.append(
            wires.push(all_ref.at[4 * n + 3, high_rows], all_ref.at[4 * n + 2, high_rows], dp=left)
        )
        input_grad(2 * n + 1)
        if n == 0:
            grad[...] = product_of((0, 1, 3, 4))
            input_grad(2)
    for copy in ends:
        copy.wait_recv()
    grad[...] += product_of((2, 5, 6, 7))

    copies_c = {}
    for d in (2, 1, 3, 0):
        to = (y + d) % NY
        copies_c[d] = wires.push(grad.at[:, to, 1 - c], sib.at[to], ctx=partner)
    near = []
    for d in (2, 1, 3, 0):
        to = (y + d) % NY
        copies_c[d].wait_recv()
        both = grad[:, to, c] + sib[to]
        if d == 0:
            ysum[...] = both
        else:
            pair[to] = both.astype(BF16)
            near.append(wires.push(pair.at[to], yred.at[y], ctx=at(z, to, c)))
    for copy in near:
        copy.wait_recv()
    for j in range(NY):
        ysum[...] += jnp.where(j == y, 0.0, yred[j].astype(F32))
    copies_z = []
    for d in (2, 1, 3):
        to = (z + d) % NZ
        copies_z.append(wires.push(ysum.at[to], zred.at[z], ctx=at(to, y, c)))
    for copy in copies_z:
        copy.wait_recv()
    total = ysum[z]
    for j in range(NZ):
        total = total + jnp.where(j == z, 0.0, zred[j])
    gp_ref[...] = total
    for copy in outs:
        copy.wait_recv()
    for copy in locals_[3:]:
        copy.wait()
    wires.drain()


def local(tokens, proj_weight, values, grad_out):
    tok, val, up = tokens[0], values[0], grad_out[0]
    count, model = tok.shape
    shard, width = proj_weight.shape
    both = 2 * count
    own = shard // (2 * NY * NZ)
    parts = (NY, RC, DH)
    dma = pltpu.SemaphoreType.DMA
    hbm = pl.BlockSpec(memory_space=pl.ANY)

    def half(*shape):
        return pltpu.VMEM(shape, BF16)

    def full(*shape):
        return pltpu.VMEM(shape, F32)

    attended, grad_tokens, grad_values, grad_proj = pl.pallas_call(
        layer_kernel,
        out_shape=(
            jax.ShapeDtypeStruct(val.shape, BF16),
            jax.ShapeDtypeStruct(tok.shape, BF16),
            jax.ShapeDtypeStruct(val.shape, BF16),
            jax.ShapeDtypeStruct((own, width), F32),
        ),
        in_specs=[VMEM, hbm, hbm, hbm],
        out_specs=(VMEM,) * 4,
        scratch_shapes=[
            half(model, 2 * HF),
            half(model, 2 * HF),
            half(both, model),
            half(both, HD),
            half(both, HD),
            full(both, 2 * HF),
            full(2 * HF, both),
            half(*parts),
            half(*parts),
            half(RC, DH),
            half(NZ, RC, DH),
            half(*parts),
            full(*parts),
            half(*parts),
            half(*parts),
            half(*parts),
            half(*parts),
            half(NZ, RC, DH),
            half(*parts),
            half(RC, DH),
            full(both, HD),
            full(both, HD),
            half(both, HD),
            half(both, HD),
            full(2 * HF, both),
            half(both, 2 * HF),
            half(count, 2 * HF),
            half(count, width),
            half(NDP, count, shard),
            half(NDP, count, width),
            full(NZ, NY, 2, own, width),
            full(NY, NZ, own, width),
            half(NY, NZ, own, width),
            half(NY, NZ, own, width),
            full(NZ, own, width),
            full(NZ, own, width),
            dma((112,)),
            dma((112,)),
            dma((5,)),
        ],
        compiler_params=pltpu.CompilerParams(collective_id=0, has_side_effects=True),
        name="layer",
    )(proj_weight, tok, val, up)
    return (attended[None], grad_tokens[None], grad_values[None], grad_proj)


def solution(mesh):
    return jax.shard_map(
        local,
        mesh=mesh,
        in_specs=(P("dp", "ctx", None), P("dp", None), P("dp", "ctx", None), P("dp", "ctx", None)),
        out_specs=(
            P("dp", "ctx", None),
            P("dp", "ctx", None),
            P("dp", "ctx", None),
            P(("dp", "ctx"), None),
        ),
        check_vma=False,
    )
```

```python
import jax
import jax.numpy as jnp
from jax import lax
from jax.experimental import pallas as pl
from jax.experimental.pallas import tpu as pltpu
from jax.sharding import PartitionSpec as P

H = 8
F = 16
DH = 128
EP = 160
QUAD = 1.0 / 32.0
EPSILON = 1e-05
MESH = pl.DeviceIdType.MESH
F32 = jnp.float32
BF16 = jnp.bfloat16
VMEM = pl.BlockSpec(memory_space=pltpu.VMEM)
NY = 4
NZ = 4
NDP = 8
RC = 2 * EP
HF = H * F
HD = H * DH


def dot(lhs, rhs, left, right):
    return lax.dot_general(lhs, rhs, (((left,), (right,)), ((), ())), preferred_element_type=F32)


def remote(src, dst, send, recv, **where):
    return pltpu.make_async_remote_copy(
        src_ref=src, dst_ref=dst, send_sem=send, recv_sem=recv, device_id=where, device_id_type=MESH
    )


def meet(peers):
    for where in peers:
        pl.semaphore_signal(
            pltpu.get_barrier_semaphore(), inc=1, device_id=where, device_id_type=MESH
        )


def met(count):
    pl.semaphore_wait(pltpu.get_barrier_semaphore(), count)


def across(dp, dz, dx):
    return (dp // 4 + dz) % 2 * 4 + (dp % 4 + dx + 4) % 4


def place():
    ctx = lax.axis_index("ctx")
    return ctx // 8, (ctx // 2) % 4, ctx % 2


def at(z, y, c):
    return z * 8 + y * 2 + c


class Wires:
    def __init__(self, send, recv):
        self.send, self.recv, self.copies = send, recv, []

    def push(self, src, dst, **where):
        n = len(self.copies)
        copy = remote(src, dst, self.send.at[n], self.recv.at[n], **where)
        copy.start()
        self.copies.append(copy)
        return copy

    def drain(self):
        for copy in self.copies:
            copy.wait_send()


def ahead(x, d):
    return pltpu.roll(x, F - d, 0)


def behind(x, d):
    return pltpu.roll(x, d, 0)


def features(x, weighted):
    quad, linear = (QUAD, 0.25) if weighted else (1.0, 1.0)
    twice = 2.0 * quad if weighted else 1.0
    parts = [x * x * quad] + [x * ahead(x, d) * twice for d in range(1, 8)]
    parts += [x[:8] * x[8:] * twice, x * linear]
    row = lax.broadcasted_iota(jnp.int32, (8, x.shape[1]), 0)
    parts.append(jnp.where(row == 0, 1.0, 0.0))
    return jnp.concatenate(parts, axis=0)


def pull_features(x, cot):
    out = 2.0 * QUAD * cot[:F] * x
    for d in range(1, 8):
        part = 2.0 * QUAD * cot[F * d : F * (d + 1)]
        out = out + part * ahead(x, d) + behind(part * x, d)
    half = 2.0 * QUAD * cot[128:136]
    out = out + jnp.concatenate([half * x[8:], half * x[:8]], axis=0)
    return out + 0.25 * cot[136:152]


def split(x):
    high = x.astype(BF16)
    return high, (x - high.astype(F32)).astype(BF16)


def scores(q, k):
    qh, ql = split(q)
    kh, kl = split(k)
    left = jnp.concatenate([qh, qh, ql, ql], axis=0)
    right = jnp.concatenate([kh, kl, kh, kl], axis=0)
    return dot(left, right, 0, 0) * 0.25


def product(feat, state):
    return dot(jnp.concatenate(split(feat), axis=0), jnp.concatenate([state, state], axis=0), 0, 0)


def causal():
    shape = (256, 256)
    return lax.broadcasted_iota(jnp.int32, shape, 0) >= lax.broadcasted_iota(jnp.int32, shape, 1)


def head_cols(h):
    return slice(h * DH, (h + 1) * DH)


def head_rows(h):
    return slice(h * F, (h + 1) * F)


def rows_of(h):
    return h // 2, slice(h % 2 * EP, (h % 2 + 1) * EP)


def aligned(start, size, step=None):
    return pl.ds(pl.multiple_of(start, step or size), size)


def layer_kernel(
    w_ref, tok_ref, v_ref, g_ref, att_ref, gt_ref, gv_ref, gp_ref,
    wq, wk, wq_far, wk_far, tok2, v2, g2, proj, projt, state, yin, tz, zin, yout, pre, prefix,
    suffix, carried, yin_b, zin_b, yout_b, tz_b, work, gn, att2, gv2, acc, rows_q, rows_k, rq_far,
    rk_far, rq_all, rk_all, cols, all_q, all_k, grad_q, grad_k, sib, pair, yred, ysum, zred,
    send, recv, local_sem,
):
    dp = lax.axis_index("dp")
    z, y, c = place()
    partner = at(z, y, 1 - c)
    up, down = at(z, (y + 1) % NY, c), at(z, (y + 3) % NY, c)
    right, left, other = across(dp, 0, 1), across(dp, 0, 3), across(dp, 1, 0)
    count = tok_ref.shape[0]
    rows = w_ref.shape[0]
    ours = aligned(c * count, count)
    theirs = aligned((1 - c) * count, count)
    own_half = aligned(c * HD, HD)
    their_half = aligned((1 - c) * HD, HD)
    wires = Wires(send, recv)
    locals_ = []

    def copy_here(src, dst):
        copy = pltpu.make_async_copy(src, dst, local_sem.at[len(locals_)])
        copy.start()
        locals_.append(copy)
        return copy

    own_rows = aligned(dp * rows, rows)
    meet(
        [{"ctx": partner}]
        + [{"ctx": at(z, (y + d) % NY, c)} for d in range(1, NY)]
        + [{"ctx": at((z + d) % NZ, y, c)} for d in range(1, NZ)]
        + [{"dp": across(dp, n // 4, n % 4)} for n in range(1, NDP)]
    )
    here = [
        copy_here(tok_ref, tok2.at[ours]),
        copy_here(v_ref.at[:, own_half], v2.at[ours]),
        copy_here(g_ref.at[:, own_half], g2.at[ours]),
    ]
    wk[own_rows, :] = w_ref[:, aligned(2 * HF + c * HF, HF)]
    wq[own_rows, :] = w_ref[:, aligned(c * HF, HF)]
    met(NY + NZ + NDP - 2)

    wide = rows // 2
    thin = wide // NY
    base_a, base_b = 0, wide

    def part(owner, start, size):
        return wk.at[aligned(owner * rows + start, size, thin // 2)]

    def own_sends(start, size):
        piece = part(dp, start, size)
        return [wires.push(piece, piece, dp=to) for to in (other, right, left)]

    def pass_on(owner, start, size):
        piece = part(owner, start, size)
        return wires.push(piece, piece, dp=right), wires.push(piece, piece, dp=left)

    def relay(near, far, start, size):
        one = part(near, start, size // 2)
        two = part(far, start + size // 2, size // 2)
        return wires.push(one, one, dp=right), wires.push(two, two, dp=left)

    def over_y(owner):
        piece = part(owner, base_b + y * thin, thin)
        return wires.push(piece, piece, ctx=up), wires.push(piece, piece, ctx=down)

    mine_b = base_b + y * thin
    b_over, b_right, b_left = own_sends(mine_b, thin)
    a_over, a_right, a_left = own_sends(base_a, wide)
    from_partner = [
        wires.push(tok_ref, tok2.at[ours], ctx=partner),
        wires.push(v_ref.at[:, their_half], v2.at[ours], ctx=partner),
        wires.push(g_ref.at[:, their_half], g2.at[ours], ctx=partner),
    ]
    owners = [other, left, right] + [across(dp, dz, dx) for dz, dx in ((1, 3), (1, 1), (0, 2), (1, 2))]
    chain_y = []
    b_over.wait_recv()
    b_right2, b_left2 = pass_on(other, mine_b, thin)
    chain_y.append(over_y(owners[0]))
    b_right.wait_recv()
    b_left.wait_recv()
    b_ends = relay(left, right, mine_b, thin)
    chain_y.append(over_y(owners[1]))
    chain_y.append(over_y(owners[2]))
    a_over.wait_recv()
    a_right2, a_left2 = pass_on(other, base_a, wide)
    b_right2.wait_recv()
    b_left2.wait_recv()
    b_ends2 = relay(owners[3], owners[4], mine_b, thin)
    chain_y.append(over_y(owners[3]))
    chain_y.append(over_y(owners[4]))
    a_right.wait_recv()
    a_left.wait_recv()
    a_ends = relay(left, right, base_a, wide)
    for copy in b_ends:
        copy.wait_recv()
    chain_y.append(over_y(owners[5]))
    for copy in b_ends2:
        copy.wait_recv()
    chain_y.append(over_y(owners[6]))
    ends_y = []
    below = base_b + (y + 3) % NY * thin
    above = base_b + (y + 1) % NY * thin + thin // 2

    def relay_y(n):
        chain_y[n][0].wait_recv()
        one = part(owners[n], below, thin // 2)
        ends_y.append([wires.push(one, one, ctx=up)])
        chain_y[n][1].wait_recv()
        two = part(owners[n], above, thin // 2)
        ends_y[-1].append(wires.push(two, two, ctx=down))

    for n in range(3):
        relay_y(n)
    a_right2.wait_recv()
    a_left2.wait_recv()
    a_ends2 = relay(owners[3], owners[4], base_a, wide)

    def query_part(owner):
        return wq.at[aligned(owner * rows, rows)]

    def query_halves(near, far):
        one = wq.at[aligned(near * rows, wide)]
        two = wq.at[aligned(far * rows + wide, wide)]
        return wires.push(one, one, dp=right), wires.push(two, two, dp=left)

    q_over, q_right, q_left = [
        wires.push(query_part(dp), query_part(dp), dp=to) for to in (other, right, left)
    ]
    for n in range(3, 7):
        relay_y(n)

    def project(weight, owner):
        return dot(
            tok2[:, aligned(owner * rows, rows)], weight[aligned(owner * rows, rows), :], 1, 0
        )

    for copy in from_partner:
        copy.wait_recv()
    for copy in here:
        copy.wait()
    proj[...] = project(wk, dp)
    for n in range(7):
        for copy in ends_y[n]:
            copy.wait_recv()
        if n == 5:
            for copy in a_ends:
                copy.wait_recv()
        if n == 6:
            for copy in a_ends2:
                copy.wait_recv()
        proj[...] += project(wk, owners[n])
    far_weight = [wires.push(wk, wk_far, ctx=partner)]
    width = cols.shape[2]
    token_copies = []

    def send_tokens(slots):
        for n in slots:
            peer = across(dp, n // 4, n % 4)
            token_copies.append(
                wires.push(tok_ref.at[:, aligned(peer * width, width)], cols.at[n], dp=peer)
            )

    q_over.wait_recv()
    q_passed = [wires.push(query_part(other), query_part(other), dp=to) for to in (right, left)]

    projt[HF:, :] = proj[...].T

    def query(h):
        return projt[h * F : (h + 1) * F, :]

    def key(h):
        return projt[HF + h * F : HF + (h + 1) * F, :]

    def head(h):
        return slice(h * DH, (h + 1) * DH)

    for h in range(H):
        high, low = split(features(key(h), False))
        v = v2[:, head(h)]
        new = dot(jnp.concatenate([high, low], axis=1), jnp.concatenate([v, v], axis=0), 1, 0)
        j, at_rows = rows_of(h)
        state[j, at_rows, :] = new.astype(BF16)

    def scan(later, src, land, total_ref, planes, out, result, fill_y, fill_z, fill_b):
        copies = []
        for d in (2, 1, 3):
            to = (y + d) % NY
            copies.append(wires.push(src.at[to], land.at[y], ctx=at(z, to, c)))
        fill_y()
        for copy in copies:
            copy.wait_recv()
        total = jnp.zeros(pre.shape[1:], F32)
        for j in list(range(NY))[::-1] if later else range(NY):
            pre[j] = total
            total = total + jnp.where(j == y, src[j], land[j]).astype(F32)
        total_ref[...] = total.astype(BF16)
        copies = []
        for d in (2, 1, 3):
            to = (z + d) % NZ
            copies.append(wires.push(total_ref, planes.at[z], ctx=at(to, y, c)))
        fill_z()
        for copy in copies:
            copy.wait_recv()
        base = jnp.zeros(pre.shape[1:], F32)
        for j in range(NZ):
            wanted = (j > z) if later else (j < z)
            base = base + jnp.where(wanted, planes[j].astype(F32), 0.0)
        for j in range(NY):
            out[j] = (base + pre[j]).astype(BF16)
        copies = []
        for d in (2, 1, 3):
            to = (y + d) % NY
            copies.append(wires.push(out.at[to], result.at[y], ctx=at(z, to, c)))
        result[y] = out[y]
        fill_b()
        for copy in copies:
            copy.wait_recv()

    mask = causal()

    def local_numerator(h):
        a = scores(query(h), key(h))
        kernel = jnp.where(mask, 1.0 + a + 0.5 * a * a, 0.0)
        v = v2[:, head(h)]
        work[:, head(h)] = dot(
            jnp.concatenate(split(kernel), axis=1), jnp.concatenate([v, v], axis=0), 1, 0
        )

    q_ends = []

    def first_fill():
        q_right.wait_recv()
        q_left.wait_recv()
        q_ends.append(query_halves(left, right))

    def second_fill():
        for copy in q_passed:
            copy.wait_recv()
        q_ends.append(query_halves(owners[3], owners[4]))
        proj[...] = project(wq, dp)
        for n in range(5):
            proj[...] += project(wq, owners[n])
        for n in range(2):
            for copy in q_ends[n]:
                copy.wait_recv()
            proj[...] += project(wq, owners[5 + n])
        projt[:HF, :] = proj[...].T
        far_weight.append(wires.push(wq, wq_far, ctx=partner))
        send_tokens((1, 2, 3))
        for h in range(H):
            local_numerator(h)

    def send_rest():
        send_tokens((4, 5, 6, 7))

    scan(False, state, yin, tz, zin, yout, prefix, first_fill, second_fill, send_rest)

    for h in range(H):
        j, at_rows = rows_of(h)
        q = query(h)
        numerator = work[:, head(h)] + product(features(q, True), prefix[j, at_rows, :])
        inv = lax.rsqrt(jnp.mean(numerator * numerator, axis=1, keepdims=True) + EPSILON)
        normed = numerator * inv
        att2[:, head(h)] = normed.astype(BF16)
        g = g2[:, head(h)].astype(F32)
        grad_num = inv * (g - normed * jnp.mean(normed * g, axis=1, keepdims=True))
        gn[:, head(h)] = grad_num
        high, low = split(features(q, False))
        gh, gl = split(grad_num)
        new = dot(
            jnp.concatenate([high, low, high], axis=1), jnp.concatenate([gh, gh, gl], axis=0), 1, 0
        )
        carried[j, at_rows, :] = new.astype(BF16)

    def local_grads(h):
        q, k = query(h), key(h)
        v = v2[:, head(h)]
        gh, gl = split(gn[:, head(h)])
        a = scores(q, k)
        mh, ml = split(jnp.where(mask, 1.0 + a + 0.5 * a * a, 0.0))
        mixing = dot(
            jnp.concatenate([gh, gl], axis=1), jnp.concatenate([v, v], axis=1), 1, 1
        )
        sh, sl = split(jnp.where(mask, mixing * (1.0 + a) * 0.25, 0.0))
        qh, ql = split(q)
        kh, kl = split(k)
        dq = dot(jnp.concatenate([kh, kl], axis=0), sh, 1, 1)
        dq = dq[:F] + dq[F:] + dot(kh, sl, 1, 1)
        dk = dot(jnp.concatenate([qh, ql], axis=0), sh, 1, 0)
        dk = dk[:F] + dk[F:] + dot(qh, sl, 1, 0)
        j, at_rows = rows_of(h)
        before = prefix[j, at_rows, :]
        pulled = dot(
            jnp.concatenate([before, before], axis=1), jnp.concatenate([gh, gl], axis=1), 1, 1
        )
        acc[h * F : (h + 1) * F, :] = dq + pull_features(q, pulled)
        acc[HF + h * F : HF + (h + 1) * F, :] = dk
        work[:, head(h)] = dot(
            jnp.concatenate([mh, ml, mh], axis=0), jnp.concatenate([gh, gh, gl], axis=0), 0, 0
        )

    outs = []
    half = count // 2
    low_rows, high_rows = pl.ds(0, half), pl.ds(half, half)

    class Gathered:
        def __init__(self, mine, far, both, land):
            self.mine, self.far, self.both, self.land = mine, far, both, land

        def swap(self):
            self.swapped = wires.push(self.mine.at[theirs], self.far, ctx=partner)

        def start(self):
            self.both[:, aligned(c * HF, HF)] = self.mine[ours, :]
            self.swapped.wait_recv()
            self.both[:, aligned((1 - c) * HF, HF)] = self.far[...]
            self.over = wires.push(self.both, self.land.at[4], dp=other)
            self.near = [
                (
                    wires.push(self.both, self.land.at[1], dp=right),
                    wires.push(self.both, self.land.at[3], dp=left),
                )
            ]
            self.ends = []

        def pass_on(self):
            self.over.wait_recv()
            self.near.append(
                (
                    wires.push(self.land.at[4], self.land.at[5], dp=right),
                    wires.push(self.land.at[4], self.land.at[7], dp=left),
                )
            )

        def relay(self, n):
            at_slot = 4 * n
            self.near[n][0].wait_recv()
            self.ends.append(
                wires.push(
                    self.land.at[at_slot + 1, low_rows], self.land.at[at_slot + 2, low_rows],
                    dp=right,
                )
            )
            self.near[n][1].wait_recv()
            self.ends.append(
                wires.push(
                    self.land.at[at_slot + 3, high_rows], self.land.at[at_slot + 2, high_rows],
                    dp=left,
                )
            )

        def finish(self):
            for copy in self.ends:
                copy.wait_recv()

    queries = Gathered(rows_q, rq_far, rq_all, all_q)
    keys = Gathered(rows_k, rk_far, rk_all, all_k)

    def third_fill():
        outs.append(wires.push(att2.at[theirs], att_ref.at[:, own_half], ctx=partner))
        copy_here(att2.at[ours], att_ref.at[:, own_half])
        for h in range(4):
            local_grads(h)

    def fourth_fill():
        for h in range(4, H):
            local_grads(h)
        rows_q[...] = acc[:HF, :].T.astype(BF16)
        queries.swap()
        queries.start()

    def fifth_fill():
        queries.pass_on()
        queries.relay(0)

    scan(
        True, carried, yin_b, tz_b, zin_b, yout_b, suffix, third_fill, fourth_fill, fifth_fill
    )

    for h in range(H):
        j, at_rows = rows_of(h)
        after = suffix[j, at_rows, :]
        k = key(h)
        span = slice(HF + h * F, HF + (h + 1) * F)
        acc[span, :] = acc[span, :] + pull_features(k, dot(after, v2[:, head(h)], 1, 1))
    rows_k[...] = acc[HF:, :].T.astype(BF16)
    keys.swap()
    queries.relay(1)
    keys.start()
    for h in range(H):
        j, at_rows = rows_of(h)
        total = work[:, head(h)] + product(features(key(h), True), suffix[j, at_rows, :])
        gv2[:, head(h)] = total.astype(BF16)
    outs.append(wires.push(gv2.at[theirs], gv_ref.at[:, own_half], ctx=partner))
    copy_here(gv2.at[ours], gv_ref.at[:, own_half])
    for copy in token_copies + far_weight:
        copy.wait_recv()

    def tokens_of(n):
        if n == 0:
            return tok2[ours, aligned(dp * width, width)]
        return cols[n]

    def product_of(part_rows, slots):
        left_rows = jnp.concatenate([tokens_of(n) for n in slots], axis=0)
        right_rows = jnp.concatenate(
            [part_rows.both[...] if n == 0 else part_rows.land[n] for n in slots], axis=0
        )
        return dot(left_rows, right_rows, 0, 0).reshape(grad_q.shape)

    block = wq.shape[0] // 4

    def input_grad(n):
        span = slice(n * block, (n + 1) * block)
        near_rows = jnp.concatenate([rows_q[ours, :], rows_k[ours, :]], axis=1)
        far_rows = jnp.concatenate([rq_far[...], rk_far[...]], axis=1)
        piece = dot(near_rows, jnp.concatenate([wq[span, :], wk[span, :]], axis=1), 1, 1)
        piece += dot(far_rows, jnp.concatenate([wq_far[span, :], wk_far[span, :]], axis=1), 1, 1)
        gt_ref[:, span] = piece.astype(BF16)

    class Reduced:
        def __init__(self, n, grad):
            self.n, self.grad = n, grad

        def chip(self):
            n = self.n
            self.halves = {
                d: wires.push(
                    self.grad.at[:, (y + d) % NY, 1 - c], sib.at[n, (y + d) % NY], ctx=partner
                )
                for d in (2, 1, 3, 0)
            }

        def over_y(self):
            n = self.n
            self.near = []
            for d in (2, 1, 3, 0):
                to = (y + d) % NY
                self.halves[d].wait_recv()
                both = self.grad[:, to, c] + sib[n, to]
                if d == 0:
                    ysum[n] = both
                else:
                    pair[n, to] = both.astype(BF16)
                    self.near.append(
                        wires.push(pair.at[n, to], yred.at[n, y], ctx=at(z, to, c))
                    )

        def over_z(self):
            n = self.n
            for copy in self.near:
                copy.wait_recv()
            for j in range(NY):
                ysum[n] += jnp.where(j == y, 0.0, yred[n, j].astype(F32))
            self.planes = [
                wires.push(ysum.at[n, (z + d) % NZ], zred.at[n, z], ctx=at((z + d) % NZ, y, c))
                for d in (2, 1, 3)
            ]

        def finish(self):
            n = self.n
            for copy in self.planes:
                copy.wait_recv()
            total = ysum[n, z]
            for j in range(NZ):
                total = total + jnp.where(j == z, 0.0, zred[n, j])
            span = total.shape[1]
            gp_ref[:, n * span : (n + 1) * span] = total

    first, second = Reduced(0, grad_q), Reduced(1, grad_k)
    queries.finish()
    grad_q[...] = product_of(queries, range(NDP))
    first.chip()
    keys.pass_on()
    keys.relay(0)
    first.over_y()
    input_grad(0)
    grad_k[...] = product_of(keys, (0, 1, 3, 4))
    keys.relay(1)
    input_grad(1)
    first.over_z()
    keys.finish()
    grad_k[...] += product_of(keys, (2, 5, 6, 7))
    second.chip()
    input_grad(2)
    second.over_y()
    input_grad(3)
    first.finish()
    second.over_z()
    second.finish()
    for copy in outs:
        copy.wait_recv()
    for copy in locals_[3:]:
        copy.wait()
    wires.drain()


def hand_over_kernel(*refs):
    for src, dst in zip(refs[:3], refs[3:]):
        dst[...] = src[...]


def hand_over(*arrays):
    steps = 4
    specs = [
        pl.BlockSpec((a.shape[0], a.shape[1] // steps), lambda i: (0, i)) for a in arrays
    ]
    return pl.pallas_call(
        hand_over_kernel,
        grid=(steps,),
        out_shape=[jax.ShapeDtypeStruct(a.shape, a.dtype) for a in arrays],
        in_specs=specs,
        out_specs=specs,
        name="hand_over",
    )(*arrays)


def local(tokens, proj_weight, values, grad_out):
    tok, val, up = tokens[0], values[0], grad_out[0]
    count, model = tok.shape
    shard, width = proj_weight.shape
    both = 2 * count
    own = shard // (2 * NY * NZ)
    parts = (NY, RC, DH)
    dma = pltpu.SemaphoreType.DMA
    hbm = pl.BlockSpec(memory_space=pl.ANY)

    def half(*shape):
        return pltpu.VMEM(shape, BF16)

    def full(*shape):
        return pltpu.VMEM(shape, F32)

    attended, grad_tokens, grad_values, grad_proj = pl.pallas_call(
        layer_kernel,
        out_shape=(
            jax.ShapeDtypeStruct(val.shape, BF16),
            jax.ShapeDtypeStruct(tok.shape, BF16),
            jax.ShapeDtypeStruct(val.shape, BF16),
            jax.ShapeDtypeStruct((own, width), F32),
        ),
        in_specs=[VMEM, hbm, hbm, hbm],
        out_specs=(VMEM,) * 4,
        scratch_shapes=[
            half(model, HF),
            half(model, HF),
            half(model, HF),
            half(model, HF),
            half(both, model),
            half(both, HD),
            half(both, HD),
            full(both, HF),
            full(2 * HF, both),
            half(*parts),
            half(*parts),
            half(RC, DH),
            half(NZ, RC, DH),
            half(*parts),
            full(*parts),
            half(*parts),
            half(*parts),
            half(*parts),
            half(*parts),
            half(NZ, RC, DH),
            half(*parts),
            half(RC, DH),
            full(both, HD),
            full(both, HD),
            half(both, HD),
            half(both, HD),
            full(2 * HF, both),
            half(both, HF),
            half(both, HF),
            half(count, HF),
            half(count, HF),
            half(count, 2 * HF),
            half(count, 2 * HF),
            half(NDP, count, shard),
            half(NDP, count, 2 * HF),
            half(NDP, count, 2 * HF),
            full(NZ, NY, 2, own, 2 * HF),
            full(NZ, NY, 2, own, 2 * HF),
            full(2, NY, NZ, own, 2 * HF),
            half(2, NY, NZ, own, 2 * HF),
            half(2, NY, NZ, own, 2 * HF),
            full(2, NZ, own, 2 * HF),
            full(2, NZ, own, 2 * HF),
            dma((144,)),
            dma((144,)),
            dma((5,)),
        ],
        compiler_params=pltpu.CompilerParams(collective_id=0, has_side_effects=True),
        name="layer",
    )(proj_weight, tok, val, up)
    attended, grad_tokens, grad_values = hand_over(attended, grad_tokens, grad_values)
    return (attended[None], grad_tokens[None], grad_values[None], grad_proj)


def solution(mesh):
    return jax.shard_map(
        local,
        mesh=mesh,
        in_specs=(P("dp", "ctx", None), P("dp", None), P("dp", "ctx", None), P("dp", "ctx", None)),
        out_specs=(
            P("dp", "ctx", None),
            P("dp", "ctx", None),
            P("dp", "ctx", None),
            P(("dp", "ctx"), None),
        ),
        check_vma=False,
    )
```

```python
import jax
import jax.numpy as jnp
from jax import lax
from jax.experimental import pallas as pl
from jax.experimental.pallas import tpu as pltpu
from jax.sharding import PartitionSpec as P

H = 8
F = 16
DH = 128
EP = 160
QUAD = 1.0 / 32.0
EPSILON = 1e-05
MESH = pl.DeviceIdType.MESH
F32 = jnp.float32
BF16 = jnp.bfloat16
VMEM = pl.BlockSpec(memory_space=pltpu.VMEM)
NY = 4
NZ = 4
NDP = 8
RC = 2 * EP
HF = H * F
HD = H * DH


def dot(lhs, rhs, left, right):
    return lax.dot_general(lhs, rhs, (((left,), (right,)), ((), ())), preferred_element_type=F32)


def remote(src, dst, send, recv, **where):
    return pltpu.make_async_remote_copy(
        src_ref=src, dst_ref=dst, send_sem=send, recv_sem=recv, device_id=where, device_id_type=MESH
    )


def meet(peers):
    for where in peers:
        pl.semaphore_signal(
            pltpu.get_barrier_semaphore(), inc=1, device_id=where, device_id_type=MESH
        )


def met(count):
    pl.semaphore_wait(pltpu.get_barrier_semaphore(), count)


def across(dp, dz, dx):
    return (dp // 4 + dz) % 2 * 4 + (dp % 4 + dx + 4) % 4


def place():
    ctx = lax.axis_index("ctx")
    return ctx // 8, (ctx // 2) % 4, ctx % 2


def at(z, y, c):
    return z * 8 + y * 2 + c


class Wires:
    def __init__(self, send, recv):
        self.send, self.recv, self.copies = send, recv, []

    def push(self, src, dst, **where):
        n = len(self.copies)
        copy = remote(src, dst, self.send.at[n], self.recv.at[n], **where)
        copy.start()
        self.copies.append(copy)
        return copy

    def drain(self):
        for copy in self.copies:
            copy.wait_send()


def ahead(x, d):
    return pltpu.roll(x, F - d, 0)


def behind(x, d):
    return pltpu.roll(x, d, 0)


def features(x, weighted):
    quad, linear = (QUAD, 0.25) if weighted else (1.0, 1.0)
    twice = 2.0 * quad if weighted else 1.0
    parts = [x * x * quad] + [x * ahead(x, d) * twice for d in range(1, 8)]
    parts += [x[:8] * x[8:] * twice, x * linear]
    row = lax.broadcasted_iota(jnp.int32, (8, x.shape[1]), 0)
    parts.append(jnp.where(row == 0, 1.0, 0.0))
    return jnp.concatenate(parts, axis=0)


def pull_features(x, cot):
    out = 2.0 * QUAD * cot[:F] * x
    for d in range(1, 8):
        part = 2.0 * QUAD * cot[F * d : F * (d + 1)]
        out = out + part * ahead(x, d) + behind(part * x, d)
    half = 2.0 * QUAD * cot[128:136]
    out = out + jnp.concatenate([half * x[8:], half * x[:8]], axis=0)
    return out + 0.25 * cot[136:152]


def split(x):
    high = x.astype(BF16)
    return high, (x - high.astype(F32)).astype(BF16)


def scores(q, k):
    qh, ql = split(q)
    kh, kl = split(k)
    left = jnp.concatenate([qh, qh, ql, ql], axis=0)
    right = jnp.concatenate([kh, kl, kh, kl], axis=0)
    return dot(left, right, 0, 0) * 0.25


def product(feat, state):
    return dot(jnp.concatenate(split(feat), axis=0), jnp.concatenate([state, state], axis=0), 0, 0)


def causal():
    shape = (256, 256)
    return lax.broadcasted_iota(jnp.int32, shape, 0) >= lax.broadcasted_iota(jnp.int32, shape, 1)


def head_cols(h):
    return slice(h * DH, (h + 1) * DH)


def head_rows(h):
    return slice(h * F, (h + 1) * F)


def rows_of(h):
    return h // 2, slice(h % 2 * EP, (h % 2 + 1) * EP)


def aligned(start, size, step=None):
    return pl.ds(pl.multiple_of(start, step or size), size)


def layer_kernel(
    w_ref, tok_ref, v_ref, g_ref, att_ref, gt_ref, gv_ref, gp_ref,
    wq, wk, wq_far, wk_far, tok2, v2, g2, proj, projt, state, yin, tz, zin, yout, pre, prefix,
    suffix, carried, yin_b, zin_b, yout_b, tz_b, work, gn, att2, gv2, acc, rows_q, rows_k, rq_far,
    rk_far, rq_all, rk_all, cols, all_q, all_k, grad_q, grad_k, sib, pair, yred, ysum, zred,
    send, recv, local_sem,
):
    dp = lax.axis_index("dp")
    z, y, c = place()
    partner = at(z, y, 1 - c)
    up, down = at(z, (y + 1) % NY, c), at(z, (y + 3) % NY, c)
    right, left, other = across(dp, 0, 1), across(dp, 0, 3), across(dp, 1, 0)
    count = tok_ref.shape[0]
    rows = w_ref.shape[0]
    ours = aligned(c * count, count)
    theirs = aligned((1 - c) * count, count)
    own_half = aligned(c * HD, HD)
    their_half = aligned((1 - c) * HD, HD)
    wires = Wires(send, recv)
    locals_ = []

    def copy_here(src, dst):
        copy = pltpu.make_async_copy(src, dst, local_sem.at[len(locals_)])
        copy.start()
        locals_.append(copy)
        return copy

    own_rows = aligned(dp * rows, rows)
    meet(
        [{"ctx": partner}]
        + [{"ctx": at(z, (y + d) % NY, c)} for d in range(1, NY)]
        + [{"ctx": at((z + d) % NZ, y, c)} for d in range(1, NZ)]
        + [{"dp": across(dp, n // 4, n % 4)} for n in range(1, NDP)]
    )
    here = [
        copy_here(tok_ref, tok2.at[ours]),
        copy_here(v_ref.at[:, own_half], v2.at[ours]),
        copy_here(g_ref.at[:, own_half], g2.at[ours]),
    ]
    wk[own_rows, :] = w_ref[:, aligned(2 * HF + c * HF, HF)]
    wq[own_rows, :] = w_ref[:, aligned(c * HF, HF)]
    met(NY + NZ + NDP - 2)

    wide = rows // 2
    thin = wide // NY
    base_a, base_b = 0, wide

    def part(owner, start, size):
        return wk.at[aligned(owner * rows + start, size, thin // 2)]

    def own_sends(start, size):
        piece = part(dp, start, size)
        return [wires.push(piece, piece, dp=to) for to in (other, right, left)]

    def pass_on(owner, start, size):
        piece = part(owner, start, size)
        return wires.push(piece, piece, dp=right), wires.push(piece, piece, dp=left)

    def relay(near, far, start, size):
        one = part(near, start, size // 2)
        two = part(far, start + size // 2, size // 2)
        return wires.push(one, one, dp=right), wires.push(two, two, dp=left)

    def over_y(owner):
        piece = part(owner, base_b + y * thin, thin)
        return wires.push(piece, piece, ctx=up), wires.push(piece, piece, ctx=down)

    mine_b = base_b + y * thin
    b_over, b_right, b_left = own_sends(mine_b, thin)
    a_over, a_right, a_left = own_sends(base_a, wide)
    from_partner = [
        wires.push(tok_ref, tok2.at[ours], ctx=partner),
        wires.push(v_ref.at[:, their_half], v2.at[ours], ctx=partner),
        wires.push(g_ref.at[:, their_half], g2.at[ours], ctx=partner),
    ]
    owners = [other, left, right] + [across(dp, dz, dx) for dz, dx in ((1, 3), (1, 1), (0, 2), (1, 2))]
    chain_y = []
    b_over.wait_recv()
    b_right2, b_left2 = pass_on(other, mine_b, thin)
    chain_y.append(over_y(owners[0]))
    b_right.wait_recv()
    b_left.wait_recv()
    b_ends = relay(left, right, mine_b, thin)
    chain_y.append(over_y(owners[1]))
    chain_y.append(over_y(owners[2]))
    a_over.wait_recv()
    a_right2, a_left2 = pass_on(other, base_a, wide)
    b_right2.wait_recv()
    b_left2.wait_recv()
    b_ends2 = relay(owners[3], owners[4], mine_b, thin)
    chain_y.append(over_y(owners[3]))
    chain_y.append(over_y(owners[4]))
    a_right.wait_recv()
    a_left.wait_recv()
    a_ends = relay(left, right, base_a, wide)
    for copy in b_ends:
        copy.wait_recv()
    chain_y.append(over_y(owners[5]))
    for copy in b_ends2:
        copy.wait_recv()
    chain_y.append(over_y(owners[6]))
    ends_y = []
    below = base_b + (y + 3) % NY * thin
    above = base_b + (y + 1) % NY * thin + thin // 2

    def relay_y(n):
        chain_y[n][0].wait_recv()
        one = part(owners[n], below, thin // 2)
        ends_y.append([wires.push(one, one, ctx=up)])
        chain_y[n][1].wait_recv()
        two = part(owners[n], above, thin // 2)
        ends_y[-1].append(wires.push(two, two, ctx=down))

    for n in range(3):
        relay_y(n)
    a_right2.wait_recv()
    a_left2.wait_recv()
    a_ends2 = relay(owners[3], owners[4], base_a, wide)

    def query_part(owner):
        return wq.at[aligned(owner * rows, rows)]

    def query_halves(near, far):
        one = wq.at[aligned(near * rows, wide)]
        two = wq.at[aligned(far * rows + wide, wide)]
        return wires.push(one, one, dp=right), wires.push(two, two, dp=left)

    q_over, q_right, q_left = [
        wires.push(query_part(dp), query_part(dp), dp=to) for to in (other, right, left)
    ]
    for n in range(3, 7):
        relay_y(n)

    def project(weight, owner):
        return dot(
            tok2[:, aligned(owner * rows, rows)], weight[aligned(owner * rows, rows), :], 1, 0
        )

    for copy in from_partner:
        copy.wait_recv()
    for copy in here:
        copy.wait()
    proj[...] = project(wk, dp)
    for n in range(7):
        for copy in ends_y[n]:
            copy.wait_recv()
        if n == 5:
            for copy in a_ends:
                copy.wait_recv()
        if n == 6:
            for copy in a_ends2:
                copy.wait_recv()
        proj[...] += project(wk, owners[n])
    far_weight = [wires.push(wk, wk_far, ctx=partner)]
    width = cols.shape[2]
    token_copies = []

    def send_tokens(slots):
        for n in slots:
            peer = across(dp, n // 4, n % 4)
            token_copies.append(
                wires.push(tok_ref.at[:, aligned(peer * width, width)], cols.at[n], dp=peer)
            )

    q_over.wait_recv()
    q_passed = [wires.push(query_part(other), query_part(other), dp=to) for to in (right, left)]

    projt[HF:, :] = proj[...].T

    def query(h):
        return projt[h * F : (h + 1) * F, :]

    def key(h):
        return projt[HF + h * F : HF + (h + 1) * F, :]

    def head(h):
        return slice(h * DH, (h + 1) * DH)

    for h in range(H):
        high, low = split(features(key(h), False))
        v = v2[:, head(h)]
        new = dot(jnp.concatenate([high, low], axis=1), jnp.concatenate([v, v], axis=0), 1, 0)
        j, at_rows = rows_of(h)
        state[j, at_rows, :] = new.astype(BF16)

    def scan(later, src, land, total_ref, planes, out, result, fill_y, fill_z, fill_b):
        copies = []
        for d in (2, 1, 3):
            to = (y + d) % NY
            copies.append(wires.push(src.at[to], land.at[y], ctx=at(z, to, c)))
        fill_y()
        for copy in copies:
            copy.wait_recv()
        total = jnp.zeros(pre.shape[1:], F32)
        for j in list(range(NY))[::-1] if later else range(NY):
            pre[j] = total
            total = total + jnp.where(j == y, src[j], land[j]).astype(F32)
        total_ref[...] = total.astype(BF16)
        copies = []
        for d in (2, 1, 3):
            to = (z + d) % NZ
            copies.append(wires.push(total_ref, planes.at[z], ctx=at(to, y, c)))
        fill_z()
        for copy in copies:
            copy.wait_recv()
        base = jnp.zeros(pre.shape[1:], F32)
        for j in range(NZ):
            wanted = (j > z) if later else (j < z)
            base = base + jnp.where(wanted, planes[j].astype(F32), 0.0)
        for j in range(NY):
            out[j] = (base + pre[j]).astype(BF16)
        copies = []
        for d in (2, 1, 3):
            to = (y + d) % NY
            copies.append(wires.push(out.at[to], result.at[y], ctx=at(z, to, c)))
        result[y] = out[y]
        fill_b()
        for copy in copies:
            copy.wait_recv()

    mask = causal()

    def local_numerator(h):
        a = scores(query(h), key(h))
        kernel = jnp.where(mask, 1.0 + a + 0.5 * a * a, 0.0)
        v = v2[:, head(h)]
        work[:, head(h)] = dot(
            jnp.concatenate(split(kernel), axis=1), jnp.concatenate([v, v], axis=0), 1, 0
        )

    q_ends = []

    def first_fill():
        q_right.wait_recv()
        q_left.wait_recv()
        q_ends.append(query_halves(left, right))

    def second_fill():
        for copy in q_passed:
            copy.wait_recv()
        q_ends.append(query_halves(owners[3], owners[4]))
        proj[...] = project(wq, dp)
        for n in range(5):
            proj[...] += project(wq, owners[n])
        for n in range(2):
            for copy in q_ends[n]:
                copy.wait_recv()
            proj[...] += project(wq, owners[5 + n])
        projt[:HF, :] = proj[...].T
        far_weight.append(wires.push(wq, wq_far, ctx=partner))
        send_tokens((1, 2, 3))
        for h in range(2):
            local_numerator(h)

    def send_rest():
        send_tokens((4, 5, 6, 7))
        for h in range(2, H):
            local_numerator(h)

    scan(False, state, yin, tz, zin, yout, prefix, first_fill, second_fill, send_rest)

    for h in range(H):
        j, at_rows = rows_of(h)
        q = query(h)
        numerator = work[:, head(h)] + product(features(q, True), prefix[j, at_rows, :])
        inv = lax.rsqrt(jnp.mean(numerator * numerator, axis=1, keepdims=True) + EPSILON)
        normed = numerator * inv
        att2[:, head(h)] = normed.astype(BF16)
        g = g2[:, head(h)].astype(F32)
        grad_num = inv * (g - normed * jnp.mean(normed * g, axis=1, keepdims=True))
        gn[:, head(h)] = grad_num
        high, low = split(features(q, False))
        gh, gl = split(grad_num)
        new = dot(
            jnp.concatenate([high, low, high], axis=1), jnp.concatenate([gh, gh, gl], axis=0), 1, 0
        )
        carried[j, at_rows, :] = new.astype(BF16)

    def local_grads(h):
        q, k = query(h), key(h)
        v = v2[:, head(h)]
        gh, gl = split(gn[:, head(h)])
        a = scores(q, k)
        mh, ml = split(jnp.where(mask, 1.0 + a + 0.5 * a * a, 0.0))
        mixing = dot(
            jnp.concatenate([gh, gl], axis=1), jnp.concatenate([v, v], axis=1), 1, 1
        )
        sh, sl = split(jnp.where(mask, mixing * (1.0 + a) * 0.25, 0.0))
        qh, ql = split(q)
        kh, kl = split(k)
        dq = dot(jnp.concatenate([kh, kl], axis=0), sh, 1, 1)
        dq = dq[:F] + dq[F:] + dot(kh, sl, 1, 1)
        dk = dot(jnp.concatenate([qh, ql], axis=0), sh, 1, 0)
        dk = dk[:F] + dk[F:] + dot(qh, sl, 1, 0)
        j, at_rows = rows_of(h)
        before = prefix[j, at_rows, :]
        pulled = dot(
            jnp.concatenate([before, before], axis=1), jnp.concatenate([gh, gl], axis=1), 1, 1
        )
        acc[h * F : (h + 1) * F, :] = dq + pull_features(q, pulled)
        acc[HF + h * F : HF + (h + 1) * F, :] = dk
        work[:, head(h)] = dot(
            jnp.concatenate([mh, ml, mh], axis=0), jnp.concatenate([gh, gh, gl], axis=0), 0, 0
        )

    outs = []
    half = count // 2
    low_rows, high_rows = pl.ds(0, half), pl.ds(half, half)

    class Gathered:
        def __init__(self, mine, far, both, land):
            self.mine, self.far, self.both, self.land = mine, far, both, land

        def swap(self):
            self.swapped = wires.push(self.mine.at[theirs], self.far, ctx=partner)

        def start(self):
            self.both[:, aligned(c * HF, HF)] = self.mine[ours, :]
            self.swapped.wait_recv()
            self.both[:, aligned((1 - c) * HF, HF)] = self.far[...]
            self.over = wires.push(self.both, self.land.at[4], dp=other)
            self.near = [
                (
                    wires.push(self.both, self.land.at[1], dp=right),
                    wires.push(self.both, self.land.at[3], dp=left),
                )
            ]
            self.ends = []

        def pass_on(self):
            self.over.wait_recv()
            self.near.append(
                (
                    wires.push(self.land.at[4], self.land.at[5], dp=right),
                    wires.push(self.land.at[4], self.land.at[7], dp=left),
                )
            )

        def relay(self, n):
            at_slot = 4 * n
            self.near[n][0].wait_recv()
            self.ends.append(
                wires.push(
                    self.land.at[at_slot + 1, low_rows], self.land.at[at_slot + 2, low_rows],
                    dp=right,
                )
            )
            self.near[n][1].wait_recv()
            self.ends.append(
                wires.push(
                    self.land.at[at_slot + 3, high_rows], self.land.at[at_slot + 2, high_rows],
                    dp=left,
                )
            )

        def finish(self):
            for copy in self.ends:
                copy.wait_recv()

    queries = Gathered(rows_q, rq_far, rq_all, all_q)
    keys = Gathered(rows_k, rk_far, rk_all, all_k)

    def third_fill():
        outs.append(wires.push(att2.at[theirs], att_ref.at[:, own_half], ctx=partner))
        copy_here(att2.at[ours], att_ref.at[:, own_half])
        for h in range(5):
            local_grads(h)

    def fourth_fill():
        for h in range(5, H):
            local_grads(h)
        rows_q[...] = acc[:HF, :].T.astype(BF16)
        queries.swap()
        queries.start()

    def fifth_fill():
        queries.pass_on()
        queries.relay(0)

    scan(
        True, carried, yin_b, tz_b, zin_b, yout_b, suffix, third_fill, fourth_fill, fifth_fill
    )

    for h in range(H):
        j, at_rows = rows_of(h)
        after = suffix[j, at_rows, :]
        k = key(h)
        span = slice(HF + h * F, HF + (h + 1) * F)
        acc[span, :] = acc[span, :] + pull_features(k, dot(after, v2[:, head(h)], 1, 1))
    rows_k[...] = acc[HF:, :].T.astype(BF16)
    keys.swap()
    queries.relay(1)
    keys.start()

    def value_grad(h):
        j, at_rows = rows_of(h)
        total = work[:, head(h)] + product(features(key(h), True), suffix[j, at_rows, :])
        gv2[:, head(h)] = total.astype(BF16)

    for h in range(4):
        value_grad(h)
    keys.pass_on()
    for h in range(4, H):
        value_grad(h)
    outs.append(wires.push(gv2.at[theirs], gv_ref.at[:, own_half], ctx=partner))
    copy_here(gv2.at[ours], gv_ref.at[:, own_half])
    keys.relay(0)
    keys.relay(1)
    for copy in token_copies + far_weight:
        copy.wait_recv()

    def tokens_of(n):
        if n == 0:
            return tok2[ours, aligned(dp * width, width)]
        return cols[n]

    def product_of(part_rows, slots):
        left_rows = jnp.concatenate([tokens_of(n) for n in slots], axis=0)
        right_rows = jnp.concatenate(
            [part_rows.both[...] if n == 0 else part_rows.land[n] for n in slots], axis=0
        )
        return dot(left_rows, right_rows, 0, 0).reshape(grad_q.shape)

    block = wq.shape[0] // 4

    def input_grad(n):
        span = slice(n * block, (n + 1) * block)
        near_rows = jnp.concatenate([rows_q[ours, :], rows_k[ours, :]], axis=1)
        far_rows = jnp.concatenate([rq_far[...], rk_far[...]], axis=1)
        piece = dot(near_rows, jnp.concatenate([wq[span, :], wk[span, :]], axis=1), 1, 1)
        piece += dot(far_rows, jnp.concatenate([wq_far[span, :], wk_far[span, :]], axis=1), 1, 1)
        gt_ref[:, span] = piece.astype(BF16)

    class Reduced:
        def __init__(self, n, grad):
            self.n, self.grad = n, grad

        def chip(self):
            n = self.n
            self.halves = {
                d: wires.push(
                    self.grad.at[:, (y + d) % NY, 1 - c], sib.at[n, (y + d) % NY], ctx=partner
                )
                for d in (2, 1, 3, 0)
            }

        def over_y(self):
            n = self.n
            self.near = []
            for d in (2, 1, 3, 0):
                to = (y + d) % NY
                self.halves[d].wait_recv()
                both = self.grad[:, to, c] + sib[n, to]
                if d == 0:
                    ysum[n] = both
                else:
                    pair[n, to] = both.astype(BF16)
                    self.near.append(
                        wires.push(pair.at[n, to], yred.at[n, y], ctx=at(z, to, c))
                    )

        def over_z(self):
            n = self.n
            for copy in self.near:
                copy.wait_recv()
            for j in range(NY):
                ysum[n] += jnp.where(j == y, 0.0, yred[n, j].astype(F32))
            self.planes = [
                wires.push(ysum.at[n, (z + d) % NZ], zred.at[n, z], ctx=at((z + d) % NZ, y, c))
                for d in (2, 1, 3)
            ]

        def finish(self):
            n = self.n
            for copy in self.planes:
                copy.wait_recv()
            total = ysum[n, z]
            for j in range(NZ):
                total = total + jnp.where(j == z, 0.0, zred[n, j])
            span = total.shape[1]
            gp_ref[:, n * span : (n + 1) * span] = total

    first, second = Reduced(0, grad_q), Reduced(1, grad_k)
    queries.finish()
    grad_q[...] = product_of(queries, range(NDP))
    first.chip()
    grad_k[...] = product_of(keys, (0, 1, 3, 4, 5, 7))
    first.over_y()
    keys.finish()
    grad_k[...] += product_of(keys, (2, 6))
    second.chip()
    input_grad(0)
    second.over_y()
    first.over_z()
    input_grad(1)
    input_grad(2)
    second.over_z()
    input_grad(3)
    first.finish()
    second.finish()
    for copy in outs:
        copy.wait_recv()
    for copy in locals_[3:]:
        copy.wait()
    wires.drain()


def hand_over_kernel(*refs):
    srcs, dsts, holds, sems = refs[:3], refs[3:6], refs[6:9], refs[9]
    pieces = [(n, at_half) for at_half in range(2) for n in range(3)]
    reads, writes = [], []
    for i, (n, at_half) in enumerate(pieces):
        size = holds[n].shape[0] // 2
        rows = pl.ds(at_half * size, size)
        reads.append(
            pltpu.make_async_copy(srcs[n].at[rows], holds[n].at[rows], sems.at[0, i])
        )
        writes.append(
            pltpu.make_async_copy(holds[n].at[rows], dsts[n].at[rows], sems.at[1, i])
        )
    for copy in reads:
        copy.start()
    for read, write in zip(reads, writes):
        read.wait()
        write.start()
    for copy in writes:
        copy.wait()


def hand_over(*arrays):
    hbm = pl.BlockSpec(memory_space=pl.ANY)
    return pl.pallas_call(
        hand_over_kernel,
        out_shape=[jax.ShapeDtypeStruct(a.shape, a.dtype) for a in arrays],
        in_specs=[hbm] * 3,
        out_specs=[hbm] * 3,
        scratch_shapes=[pltpu.VMEM(a.shape, a.dtype) for a in arrays]
        + [pltpu.SemaphoreType.DMA((2, 6))],
        name="hand_over",
    )(*arrays)


def local(tokens, proj_weight, values, grad_out):
    tok, val, up = tokens[0], values[0], grad_out[0]
    count, model = tok.shape
    shard, width = proj_weight.shape
    both = 2 * count
    own = shard // (2 * NY * NZ)
    parts = (NY, RC, DH)
    dma = pltpu.SemaphoreType.DMA
    hbm = pl.BlockSpec(memory_space=pl.ANY)

    def half(*shape):
        return pltpu.VMEM(shape, BF16)

    def full(*shape):
        return pltpu.VMEM(shape, F32)

    attended, grad_tokens, grad_values, grad_proj = pl.pallas_call(
        layer_kernel,
        out_shape=(
            jax.ShapeDtypeStruct(val.shape, BF16),
            jax.ShapeDtypeStruct(tok.shape, BF16),
            jax.ShapeDtypeStruct(val.shape, BF16),
            jax.ShapeDtypeStruct((own, width), F32),
        ),
        in_specs=[VMEM, hbm, hbm, hbm],
        out_specs=(VMEM,) * 4,
        scratch_shapes=[
            half(model, HF),
            half(model, HF),
            half(model, HF),
            half(model, HF),
            half(both, model),
            half(both, HD),
            half(both, HD),
            full(both, HF),
            full(2 * HF, both),
            half(*parts),
            half(*parts),
            half(RC, DH),
            half(NZ, RC, DH),
            half(*parts),
            full(*parts),
            half(*parts),
            half(*parts),
            half(*parts),
            half(*parts),
            half(NZ, RC, DH),
            half(*parts),
            half(RC, DH),
            full(both, HD),
            full(both, HD),
            half(both, HD),
            half(both, HD),
            full(2 * HF, both),
            half(both, HF),
            half(both, HF),
            half(count, HF),
            half(count, HF),
            half(count, 2 * HF),
            half(count, 2 * HF),
            half(NDP, count, shard),
            half(NDP, count, 2 * HF),
            half(NDP, count, 2 * HF),
            full(NZ, NY, 2, own, 2 * HF),
            full(NZ, NY, 2, own, 2 * HF),
            full(2, NY, NZ, own, 2 * HF),
            half(2, NY, NZ, own, 2 * HF),
            half(2, NY, NZ, own, 2 * HF),
            full(2, NZ, own, 2 * HF),
            full(2, NZ, own, 2 * HF),
            dma((144,)),
            dma((144,)),
            dma((5,)),
        ],
        compiler_params=pltpu.CompilerParams(collective_id=0, has_side_effects=True),
        name="layer",
    )(proj_weight, tok, val, up)
    attended, grad_tokens, grad_values = hand_over(attended, grad_tokens, grad_values)
    return (attended[None], grad_tokens[None], grad_values[None], grad_proj)


def solution(mesh):
    return jax.shard_map(
        local,
        mesh=mesh,
        in_specs=(P("dp", "ctx", None), P("dp", None), P("dp", "ctx", None), P("dp", "ctx", None)),
        out_specs=(
            P("dp", "ctx", None),
            P("dp", "ctx", None),
            P("dp", "ctx", None),
            P(("dp", "ctx"), None),
        ),
        check_vma=False,
    )
```

```python
import jax
import jax.numpy as jnp
from jax import lax
from jax.experimental import pallas as pl
from jax.experimental.pallas import tpu as pltpu
from jax.sharding import PartitionSpec as P

H = 8
F = 16
DH = 128
EP = 160
QUAD = 1.0 / 32.0
EPSILON = 1e-05
MESH = pl.DeviceIdType.MESH
F32 = jnp.float32
BF16 = jnp.bfloat16
VMEM = pl.BlockSpec(memory_space=pltpu.VMEM)
NY = 4
NZ = 4
NDP = 8
RC = 2 * EP
HF = H * F
HD = H * DH


def dot(lhs, rhs, left, right):
    return lax.dot_general(lhs, rhs, (((left,), (right,)), ((), ())), preferred_element_type=F32)


def remote(src, dst, send, recv, **where):
    return pltpu.make_async_remote_copy(
        src_ref=src, dst_ref=dst, send_sem=send, recv_sem=recv, device_id=where, device_id_type=MESH
    )


def meet(peers):
    for where in peers:
        pl.semaphore_signal(
            pltpu.get_barrier_semaphore(), inc=1, device_id=where, device_id_type=MESH
        )


def met(count):
    pl.semaphore_wait(pltpu.get_barrier_semaphore(), count)


def across(dp, dz, dx):
    return (dp // 4 + dz) % 2 * 4 + (dp % 4 + dx + 4) % 4


def place():
    ctx = lax.axis_index("ctx")
    return ctx // 8, (ctx // 2) % 4, ctx % 2


def at(z, y, c):
    return z * 8 + y * 2 + c


class Wires:
    def __init__(self, send, recv):
        self.send, self.recv, self.copies = send, recv, []

    def push(self, src, dst, **where):
        n = len(self.copies)
        copy = remote(src, dst, self.send.at[n], self.recv.at[n], **where)
        copy.start()
        self.copies.append(copy)
        return copy

    def drain(self):
        for copy in self.copies:
            copy.wait_send()


def ahead(x, d):
    return pltpu.roll(x, F - d, 0)


def behind(x, d):
    return pltpu.roll(x, d, 0)


def features(x, weighted):
    quad, linear = (QUAD, 0.25) if weighted else (1.0, 1.0)
    twice = 2.0 * quad if weighted else 1.0
    parts = [x * x * quad] + [x * ahead(x, d) * twice for d in range(1, 8)]
    parts += [x[:8] * x[8:] * twice, x * linear]
    row = lax.broadcasted_iota(jnp.int32, (8, x.shape[1]), 0)
    parts.append(jnp.where(row == 0, 1.0, 0.0))
    return jnp.concatenate(parts, axis=0)


def pull_features(x, cot):
    out = 2.0 * QUAD * cot[:F] * x
    for d in range(1, 8):
        part = 2.0 * QUAD * cot[F * d : F * (d + 1)]
        out = out + part * ahead(x, d) + behind(part * x, d)
    half = 2.0 * QUAD * cot[128:136]
    out = out + jnp.concatenate([half * x[8:], half * x[:8]], axis=0)
    return out + 0.25 * cot[136:152]


def split(x):
    high = x.astype(BF16)
    return high, (x - high.astype(F32)).astype(BF16)


def scores(q, k):
    qh, ql = split(q)
    kh, kl = split(k)
    left = jnp.concatenate([qh, qh, ql, ql], axis=0)
    right = jnp.concatenate([kh, kl, kh, kl], axis=0)
    return dot(left, right, 0, 0) * 0.25


def product(feat, state):
    return dot(jnp.concatenate(split(feat), axis=0), jnp.concatenate([state, state], axis=0), 0, 0)


def causal():
    shape = (256, 256)
    return lax.broadcasted_iota(jnp.int32, shape, 0) >= lax.broadcasted_iota(jnp.int32, shape, 1)


def head_cols(h):
    return slice(h * DH, (h + 1) * DH)


def head_rows(h):
    return slice(h * F, (h + 1) * F)


def rows_of(h):
    return h // 2, slice(h % 2 * EP, (h % 2 + 1) * EP)


def aligned(start, size, step=None):
    return pl.ds(pl.multiple_of(start, step or size), size)


def layer_kernel(
    w_ref, tok_ref, v_ref, g_ref, att_ref, gt_ref, gv_ref, gp_ref,
    wq, wk, wq_far, wk_far, tok2, v2, g2, proj, projt, state, yin, tz, zin, yout, pre, prefix,
    suffix, carried, yin_b, zin_b, yout_b, tz_b, work, gn, att2, gv2, acc, rows_q, rows_k, rq_far,
    rk_far, rq_all, rk_all, cols, all_q, all_k, grad_q, grad_k, sib, pair, yred, ysum, zred,
    send, recv, local_sem,
):
    dp = lax.axis_index("dp")
    z, y, c = place()
    partner = at(z, y, 1 - c)
    right, left, other = across(dp, 0, 1), across(dp, 0, 3), across(dp, 1, 0)
    count = tok_ref.shape[0]
    rows = w_ref.shape[0]
    ours = aligned(c * count, count)
    theirs = aligned((1 - c) * count, count)
    own_half = aligned(c * HD, HD)
    their_half = aligned((1 - c) * HD, HD)
    wires = Wires(send, recv)
    locals_ = []

    def copy_here(src, dst):
        copy = pltpu.make_async_copy(src, dst, local_sem.at[len(locals_)])
        copy.start()
        locals_.append(copy)
        return copy

    own_rows = aligned(dp * rows, rows)
    meet(
        [{"ctx": partner}]
        + [{"ctx": at(z, (y + d) % NY, c)} for d in range(1, NY)]
        + [{"ctx": at((z + d) % NZ, y, c)} for d in range(1, NZ)]
        + [{"dp": across(dp, n // 4, n % 4)} for n in range(1, NDP)]
    )
    here = [
        copy_here(tok_ref, tok2.at[ours]),
        copy_here(v_ref.at[:, own_half], v2.at[ours]),
        copy_here(g_ref.at[:, own_half], g2.at[ours]),
    ]
    wk[own_rows, :] = w_ref[:, aligned(2 * HF + c * HF, HF)]
    wq[own_rows, :] = w_ref[:, aligned(c * HF, HF)]
    met(NY + NZ + NDP - 2)

    wide = 3 * rows // 4
    thin = (rows - wide) // NY
    half_rows = rows // 2
    base_a, base_b = 0, wide

    def part(owner, start, size):
        return wk.at[aligned(owner * rows + start, size, thin // 2)]

    def own_sends(start, size):
        piece = part(dp, start, size)
        return [wires.push(piece, piece, dp=to) for to in (other, right, left)]

    def pass_on(owner, start, size):
        piece = part(owner, start, size)
        return wires.push(piece, piece, dp=right), wires.push(piece, piece, dp=left)

    def relay(near, far, start, size):
        one = part(near, start, size // 2)
        two = part(far, start + size // 2, size // 2)
        return wires.push(one, one, dp=right), wires.push(two, two, dp=left)

    def over_y(owner):
        piece = part(owner, base_b + y * thin, thin)
        return [
            wires.push(piece, piece, ctx=at(z, (y + d) % NY, c)) for d in (2, 1, 3)
        ]

    mine_b = base_b + y * thin
    b_over, b_right, b_left = own_sends(mine_b, thin)
    a_over, a_right, a_left = own_sends(base_a, wide)
    from_partner = [
        wires.push(tok_ref, tok2.at[ours], ctx=partner),
        wires.push(v_ref.at[:, their_half], v2.at[ours], ctx=partner),
        wires.push(g_ref.at[:, their_half], g2.at[ours], ctx=partner),
    ]
    owners = [other, left, right] + [across(dp, dz, dx) for dz, dx in ((1, 3), (1, 1), (0, 2), (1, 2))]
    chain_y = []
    b_over.wait_recv()
    b_right2, b_left2 = pass_on(other, mine_b, thin)
    chain_y.append(over_y(owners[0]))
    b_right.wait_recv()
    b_left.wait_recv()
    b_ends = relay(left, right, mine_b, thin)
    chain_y.append(over_y(owners[1]))
    chain_y.append(over_y(owners[2]))
    a_over.wait_recv()
    a_right2, a_left2 = pass_on(other, base_a, wide)
    b_right2.wait_recv()
    b_left2.wait_recv()
    b_ends2 = relay(owners[3], owners[4], mine_b, thin)
    chain_y.append(over_y(owners[3]))
    chain_y.append(over_y(owners[4]))
    a_right.wait_recv()
    a_left.wait_recv()
    a_ends = relay(left, right, base_a, wide)
    for copy in b_ends:
        copy.wait_recv()
    chain_y.append(over_y(owners[5]))
    for copy in b_ends2:
        copy.wait_recv()
    chain_y.append(over_y(owners[6]))
    a_right2.wait_recv()
    a_left2.wait_recv()
    a_ends2 = relay(owners[3], owners[4], base_a, wide)

    def query_part(owner):
        return wq.at[aligned(owner * rows, rows)]

    def query_halves(near, far):
        one = wq.at[aligned(near * rows, half_rows)]
        two = wq.at[aligned(far * rows + half_rows, half_rows)]
        return wires.push(one, one, dp=right), wires.push(two, two, dp=left)

    q_over, q_right, q_left = [
        wires.push(query_part(dp), query_part(dp), dp=to) for to in (other, right, left)
    ]

    def project(weight, owner):
        return dot(
            tok2[:, aligned(owner * rows, rows)], weight[aligned(owner * rows, rows), :], 1, 0
        )

    for copy in from_partner:
        copy.wait_recv()
    for copy in here:
        copy.wait()
    proj[...] = project(wk, dp)
    for n in range(7):
        for copy in chain_y[n]:
            copy.wait_recv()
        if n == 5:
            for copy in a_ends:
                copy.wait_recv()
        if n == 6:
            for copy in a_ends2:
                copy.wait_recv()
        proj[...] += project(wk, owners[n])
    far_weight = [wires.push(wk, wk_far, ctx=partner)]
    width = cols.shape[2]
    token_copies = []

    def send_tokens(slots):
        for n in slots:
            peer = across(dp, n // 4, n % 4)
            token_copies.append(
                wires.push(tok_ref.at[:, aligned(peer * width, width)], cols.at[n], dp=peer)
            )

    q_over.wait_recv()
    q_passed = [wires.push(query_part(other), query_part(other), dp=to) for to in (right, left)]

    projt[HF:, :] = proj[...].T

    def query(h):
        return projt[aligned(h * F, F), :]

    def key(h):
        return projt[aligned(HF + h * F, F), :]

    def head(h):
        return aligned(h * DH, DH)

    def send_part(src, land, j):
        return wires.push(src.at[j], land.at[y], ctx=at(z, j, c))

    def arrived(copies, d):
        copies[NY - d].wait_recv()

    sent = {}
    for d in (2, 1, 3, 0):
        j = (y + d) % NY
        for e in range(2):
            h = 2 * j + e
            high, low = split(features(key(h), False))
            v = v2[:, head(h)]
            new = dot(jnp.concatenate([high, low], axis=1), jnp.concatenate([v, v], axis=0), 1, 0)
            state[j, e * EP : (e + 1) * EP, :] = new.astype(BF16)
        if d:
            sent[d] = send_part(state, yin, j)

    def scan(later, sent, src, land, total_ref, planes, out, result, fill_y, fill_z, fill_b):
        fill_y()
        for copy in sent.values():
            copy.wait_recv()
        total = jnp.zeros(pre.shape[1:], F32)
        for j in list(range(NY))[::-1] if later else range(NY):
            pre[j] = total
            total = total + jnp.where(j == y, src[j], land[j]).astype(F32)
        total_ref[...] = total.astype(BF16)
        copies = []
        for d in (2, 1, 3):
            to = (z + d) % NZ
            copies.append(wires.push(total_ref, planes.at[z], ctx=at(to, y, c)))
        fill_z()
        for copy in copies:
            copy.wait_recv()
        base = jnp.zeros(pre.shape[1:], F32)
        for j in range(NZ):
            wanted = (j > z) if later else (j < z)
            base = base + jnp.where(wanted, planes[j].astype(F32), 0.0)
        for j in range(NY):
            out[j] = (base + pre[j]).astype(BF16)
        copies = {d: send_part(out, result, (y + d) % NY) for d in (2, 1, 3)}
        result[y] = out[y]
        fill_b()
        return copies

    mask = causal()

    def local_numerator(h):
        a = scores(query(h), key(h))
        kernel = jnp.where(mask, 1.0 + a + 0.5 * a * a, 0.0)
        v = v2[:, head(h)]
        work[:, head(h)] = dot(
            jnp.concatenate(split(kernel), axis=1), jnp.concatenate([v, v], axis=0), 1, 0
        )

    q_ends = []

    def first_fill():
        q_right.wait_recv()
        q_left.wait_recv()
        q_ends.append(query_halves(left, right))
        for copy in q_passed:
            copy.wait_recv()
        q_ends.append(query_halves(owners[3], owners[4]))

    def second_fill():
        proj[...] = project(wq, dp)
        for n in range(5):
            proj[...] += project(wq, owners[n])
        for n in range(2):
            for copy in q_ends[n]:
                copy.wait_recv()
            proj[...] += project(wq, owners[5 + n])
        projt[:HF, :] = proj[...].T
        far_weight.append(wires.push(wq, wq_far, ctx=partner))
        send_tokens((1, 2, 3))
        for h in range(2):
            local_numerator(h)

    def send_rest():
        send_tokens((4, 5, 6, 7))
        for h in range(2, H):
            local_numerator(h)

    back = scan(False, sent, state, yin, tz, zin, yout, prefix, first_fill, second_fill, send_rest)

    def forward_head(j, e):
        h, at_rows = 2 * j + e, slice(e * EP, (e + 1) * EP)
        q = query(h)
        numerator = work[:, head(h)] + product(features(q, True), prefix[j, at_rows, :])
        inv = lax.rsqrt(jnp.mean(numerator * numerator, axis=1, keepdims=True) + EPSILON)
        normed = numerator * inv
        att2[:, head(h)] = normed.astype(BF16)
        g = g2[:, head(h)].astype(F32)
        grad_num = inv * (g - normed * jnp.mean(normed * g, axis=1, keepdims=True))
        gn[:, head(h)] = grad_num
        high, low = split(features(q, False))
        gh, gl = split(grad_num)
        new = dot(
            jnp.concatenate([high, low, high], axis=1), jnp.concatenate([gh, gh, gl], axis=0), 1, 0
        )
        carried[j, at_rows, :] = new.astype(BF16)

    sent = {}
    for d in (0, 1, 3, 2):
        j = (y + d) % NY
        if d:
            arrived(back, d)
        for e in range(2):
            forward_head(j, e)
        if d:
            sent[d] = send_part(carried, yin_b, j)

    def local_grads(h):
        q, k = query(h), key(h)
        v = v2[:, head(h)]
        gh, gl = split(gn[:, head(h)])
        a = scores(q, k)
        mh, ml = split(jnp.where(mask, 1.0 + a + 0.5 * a * a, 0.0))
        mixing = dot(
            jnp.concatenate([gh, gl], axis=1), jnp.concatenate([v, v], axis=1), 1, 1
        )
        sh, sl = split(jnp.where(mask, mixing * (1.0 + a) * 0.25, 0.0))
        qh, ql = split(q)
        kh, kl = split(k)
        dq = dot(jnp.concatenate([kh, kl], axis=0), sh, 1, 1)
        dq = dq[:F] + dq[F:] + dot(kh, sl, 1, 1)
        dk = dot(jnp.concatenate([qh, ql], axis=0), sh, 1, 0)
        dk = dk[:F] + dk[F:] + dot(qh, sl, 1, 0)
        j, at_rows = rows_of(h)
        before = prefix[j, at_rows, :]
        pulled = dot(
            jnp.concatenate([before, before], axis=1), jnp.concatenate([gh, gl], axis=1), 1, 1
        )
        acc[h * F : (h + 1) * F, :] = dq + pull_features(q, pulled)
        acc[HF + h * F : HF + (h + 1) * F, :] = dk
        work[:, head(h)] = dot(
            jnp.concatenate([mh, ml, mh], axis=0), jnp.concatenate([gh, gh, gl], axis=0), 0, 0
        )

    outs = []
    half = count // 2
    low_rows, high_rows = pl.ds(0, half), pl.ds(half, half)

    class Gathered:
        def __init__(self, mine, far, both, land):
            self.mine, self.far, self.both, self.land = mine, far, both, land

        def swap(self):
            self.swapped = wires.push(self.mine.at[theirs], self.far, ctx=partner)

        def start(self):
            self.both[:, aligned(c * HF, HF)] = self.mine[ours, :]
            self.swapped.wait_recv()
            self.both[:, aligned((1 - c) * HF, HF)] = self.far[...]
            self.over = wires.push(self.both, self.land.at[4], dp=other)
            self.near = [
                (
                    wires.push(self.both, self.land.at[1], dp=right),
                    wires.push(self.both, self.land.at[3], dp=left),
                )
            ]
            self.ends = []

        def pass_on(self):
            self.over.wait_recv()
            self.near.append(
                (
                    wires.push(self.land.at[4], self.land.at[5], dp=right),
                    wires.push(self.land.at[4], self.land.at[7], dp=left),
                )
            )

        def relay(self, n):
            at_slot = 4 * n
            self.near[n][0].wait_recv()
            self.ends.append(
                wires.push(
                    self.land.at[at_slot + 1, low_rows], self.land.at[at_slot + 2, low_rows],
                    dp=right,
                )
            )
            self.near[n][1].wait_recv()
            self.ends.append(
                wires.push(
                    self.land.at[at_slot + 3, high_rows], self.land.at[at_slot + 2, high_rows],
                    dp=left,
                )
            )

        def finish(self):
            for copy in self.ends:
                copy.wait_recv()

    queries = Gathered(rows_q, rq_far, rq_all, all_q)
    keys = Gathered(rows_k, rk_far, rk_all, all_k)

    def third_fill():
        outs.append(wires.push(att2.at[theirs], att_ref.at[:, own_half], ctx=partner))
        copy_here(att2.at[ours], att_ref.at[:, own_half])
        for h in range(5):
            local_grads(h)

    def fourth_fill():
        for h in range(5, H):
            local_grads(h)
        rows_q[...] = acc[:HF, :].T.astype(BF16)
        queries.swap()
        queries.start()

    def fifth_fill():
        queries.pass_on()
        queries.relay(0)

    back = scan(
        True, sent, carried, yin_b, tz_b, zin_b, yout_b, suffix, third_fill, fourth_fill, fifth_fill
    )

    for d in (0, 1, 3, 2):
        j = (y + d) % NY
        if d:
            arrived(back, d)
        for e in range(2):
            h = 2 * j + e
            after = suffix[j, e * EP : (e + 1) * EP, :]
            span = aligned(HF + h * F, F)
            pulled = dot(after, v2[:, head(h)], 1, 1)
            acc[span, :] = acc[span, :] + pull_features(key(h), pulled)
    rows_k[...] = acc[HF:, :].T.astype(BF16)
    keys.swap()
    queries.relay(1)
    keys.start()

    def value_grad(h):
        j, at_rows = rows_of(h)
        total = work[:, head(h)] + product(features(key(h), True), suffix[j, at_rows, :])
        gv2[:, head(h)] = total.astype(BF16)

    for h in range(4):
        value_grad(h)
    keys.pass_on()
    for h in range(4, H):
        value_grad(h)
    outs.append(wires.push(gv2.at[theirs], gv_ref.at[:, own_half], ctx=partner))
    copy_here(gv2.at[ours], gv_ref.at[:, own_half])
    keys.relay(0)
    keys.relay(1)
    for copy in token_copies + far_weight:
        copy.wait_recv()

    def tokens_of(n):
        if n == 0:
            return tok2[ours, aligned(dp * width, width)]
        return cols[n]

    def product_of(part_rows, slots):
        left_rows = jnp.concatenate([tokens_of(n) for n in slots], axis=0)
        right_rows = jnp.concatenate(
            [part_rows.both[...] if n == 0 else part_rows.land[n] for n in slots], axis=0
        )
        return dot(left_rows, right_rows, 0, 0).reshape(grad_q.shape)

    block = wq.shape[0] // 4

    def input_grad(n):
        span = slice(n * block, (n + 1) * block)
        near_rows = jnp.concatenate([rows_q[ours, :], rows_k[ours, :]], axis=1)
        far_rows = jnp.concatenate([rq_far[...], rk_far[...]], axis=1)
        piece = dot(near_rows, jnp.concatenate([wq[span, :], wk[span, :]], axis=1), 1, 1)
        piece += dot(far_rows, jnp.concatenate([wq_far[span, :], wk_far[span, :]], axis=1), 1, 1)
        gt_ref[:, span] = piece.astype(BF16)

    class Reduced:
        def __init__(self, n, grad):
            self.n, self.grad = n, grad

        def chip(self):
            n = self.n
            self.halves = {
                d: wires.push(
                    self.grad.at[:, (y + d) % NY, 1 - c], sib.at[n, (y + d) % NY], ctx=partner
                )
                for d in (2, 1, 3, 0)
            }

        def over_y(self):
            n = self.n
            self.near = []
            for d in (2, 1, 3, 0):
                to = (y + d) % NY
                self.halves[d].wait_recv()
                both = self.grad[:, to, c] + sib[n, to]
                if d == 0:
                    ysum[n] = both
                else:
                    pair[n, to] = both.astype(BF16)
                    self.near.append(
                        wires.push(pair.at[n, to], yred.at[n, y], ctx=at(z, to, c))
                    )

        def over_z(self):
            n = self.n
            for copy in self.near:
                copy.wait_recv()
            for j in range(NY):
                ysum[n] += jnp.where(j == y, 0.0, yred[n, j].astype(F32))
            self.planes = [
                wires.push(ysum.at[n, (z + d) % NZ], zred.at[n, z], ctx=at((z + d) % NZ, y, c))
                for d in (2, 1, 3)
            ]

        def finish(self):
            n = self.n
            for copy in self.planes:
                copy.wait_recv()
            total = ysum[n, z]
            for j in range(NZ):
                total = total + jnp.where(j == z, 0.0, zred[n, j])
            span = total.shape[1]
            gp_ref[:, n * span : (n + 1) * span] = total

    first, second = Reduced(0, grad_q), Reduced(1, grad_k)
    queries.finish()
    grad_q[...] = product_of(queries, range(NDP))
    first.chip()
    grad_k[...] = product_of(keys, (0, 1, 3, 4, 5, 7))
    first.over_y()
    keys.finish()
    grad_k[...] += product_of(keys, (2, 6))
    second.chip()
    input_grad(0)
    second.over_y()
    first.over_z()
    input_grad(1)
    input_grad(2)
    second.over_z()
    input_grad(3)
    first.finish()
    second.finish()
    for copy in outs:
        copy.wait_recv()
    for copy in locals_[3:]:
        copy.wait()
    wires.drain()


def hand_over_kernel(*refs):
    srcs, dsts, holds, sems = refs[:3], refs[3:6], refs[6:9], refs[9]
    pieces = [(n, at_half) for at_half in range(2) for n in range(3)]
    reads, writes = [], []
    for i, (n, at_half) in enumerate(pieces):
        size = holds[n].shape[0] // 2
        rows = pl.ds(at_half * size, size)
        reads.append(
            pltpu.make_async_copy(srcs[n].at[rows], holds[n].at[rows], sems.at[0, i])
        )
        writes.append(
            pltpu.make_async_copy(holds[n].at[rows], dsts[n].at[rows], sems.at[1, i])
        )
    for copy in reads:
        copy.start()
    for read, write in zip(reads, writes):
        read.wait()
        write.start()
    for copy in writes:
        copy.wait()


def hand_over(*arrays):
    hbm = pl.BlockSpec(memory_space=pl.ANY)
    return pl.pallas_call(
        hand_over_kernel,
        out_shape=[jax.ShapeDtypeStruct(a.shape, a.dtype) for a in arrays],
        in_specs=[hbm] * 3,
        out_specs=[hbm] * 3,
        scratch_shapes=[pltpu.VMEM(a.shape, a.dtype) for a in arrays]
        + [pltpu.SemaphoreType.DMA((2, 6))],
        name="hand_over",
    )(*arrays)


def local(tokens, proj_weight, values, grad_out):
    tok, val, up = tokens[0], values[0], grad_out[0]
    count, model = tok.shape
    shard, width = proj_weight.shape
    both = 2 * count
    own = shard // (2 * NY * NZ)
    parts = (NY, RC, DH)
    dma = pltpu.SemaphoreType.DMA
    hbm = pl.BlockSpec(memory_space=pl.ANY)

    def half(*shape):
        return pltpu.VMEM(shape, BF16)

    def full(*shape):
        return pltpu.VMEM(shape, F32)

    attended, grad_tokens, grad_values, grad_proj = pl.pallas_call(
        layer_kernel,
        out_shape=(
            jax.ShapeDtypeStruct(val.shape, BF16),
            jax.ShapeDtypeStruct(tok.shape, BF16),
            jax.ShapeDtypeStruct(val.shape, BF16),
            jax.ShapeDtypeStruct((own, width), F32),
        ),
        in_specs=[VMEM, hbm, hbm, hbm],
        out_specs=(VMEM,) * 4,
        scratch_shapes=[
            half(model, HF),
            half(model, HF),
            half(model, HF),
            half(model, HF),
            half(both, model),
            half(both, HD),
            half(both, HD),
            full(both, HF),
            full(2 * HF, both),
            half(*parts),
            half(*parts),
            half(RC, DH),
            half(NZ, RC, DH),
            half(*parts),
            full(*parts),
            half(*parts),
            half(*parts),
            half(*parts),
            half(*parts),
            half(NZ, RC, DH),
            half(*parts),
            half(RC, DH),
            full(both, HD),
            full(both, HD),
            half(both, HD),
            half(both, HD),
            full(2 * HF, both),
            half(both, HF),
            half(both, HF),
            half(count, HF),
            half(count, HF),
            half(count, 2 * HF),
            half(count, 2 * HF),
            half(NDP, count, shard),
            half(NDP, count, 2 * HF),
            half(NDP, count, 2 * HF),
            full(NZ, NY, 2, own, 2 * HF),
            full(NZ, NY, 2, own, 2 * HF),
            full(2, NY, NZ, own, 2 * HF),
            half(2, NY, NZ, own, 2 * HF),
            half(2, NY, NZ, own, 2 * HF),
            full(2, NZ, own, 2 * HF),
            full(2, NZ, own, 2 * HF),
            dma((144,)),
            dma((144,)),
            dma((5,)),
        ],
        compiler_params=pltpu.CompilerParams(collective_id=0, has_side_effects=True),
        name="layer",
    )(proj_weight, tok, val, up)
    attended, grad_tokens, grad_values = hand_over(attended, grad_tokens, grad_values)
    return (attended[None], grad_tokens[None], grad_values[None], grad_proj)


def solution(mesh):
    return jax.shard_map(
        local,
        mesh=mesh,
        in_specs=(P("dp", "ctx", None), P("dp", None), P("dp", "ctx", None), P("dp", "ctx", None)),
        out_specs=(
            P("dp", "ctx", None),
            P("dp", "ctx", None),
            P("dp", "ctx", None),
            P(("dp", "ctx"), None),
        ),
        check_vma=False,
    )
```

```python
import jax
import jax.numpy as jnp
from jax import lax
from jax.experimental import pallas as pl
from jax.experimental.pallas import tpu as pltpu
from jax.sharding import PartitionSpec as P

H = 8
F = 16
DH = 128
EP = 160
QUAD = 1.0 / 32.0
EPSILON = 1e-05
MESH = pl.DeviceIdType.MESH
F32 = jnp.float32
BF16 = jnp.bfloat16
VMEM = pl.BlockSpec(memory_space=pltpu.VMEM)
NY = 4
NZ = 4
NDP = 8
RC = 2 * EP
HF = H * F
HD = H * DH


def dot(lhs, rhs, left, right):
    return lax.dot_general(lhs, rhs, (((left,), (right,)), ((), ())), preferred_element_type=F32)


def remote(src, dst, send, recv, **where):
    return pltpu.make_async_remote_copy(
        src_ref=src, dst_ref=dst, send_sem=send, recv_sem=recv, device_id=where, device_id_type=MESH
    )


def meet(peers):
    for where in peers:
        pl.semaphore_signal(
            pltpu.get_barrier_semaphore(), inc=1, device_id=where, device_id_type=MESH
        )


def met(count):
    pl.semaphore_wait(pltpu.get_barrier_semaphore(), count)


def across(dp, dz, dx):
    return (dp // 4 + dz) % 2 * 4 + (dp % 4 + dx + 4) % 4


def place():
    ctx = lax.axis_index("ctx")
    return ctx // 8, (ctx // 2) % 4, ctx % 2


def at(z, y, c):
    return z * 8 + y * 2 + c


class Wires:
    def __init__(self, send, recv):
        self.send, self.recv, self.copies = send, recv, []

    def push(self, src, dst, **where):
        n = len(self.copies)
        copy = remote(src, dst, self.send.at[n], self.recv.at[n], **where)
        copy.start()
        self.copies.append(copy)
        return copy

    def drain(self):
        for copy in self.copies:
            copy.wait_send()


def ahead(x, d):
    return pltpu.roll(x, F - d, 0)


def behind(x, d):
    return pltpu.roll(x, d, 0)


def features(x, weighted):
    quad, linear = (QUAD, 0.25) if weighted else (1.0, 1.0)
    twice = 2.0 * quad if weighted else 1.0
    parts = [x * x * quad] + [x * ahead(x, d) * twice for d in range(1, 8)]
    parts += [x[:8] * x[8:] * twice, x * linear]
    row = lax.broadcasted_iota(jnp.int32, (8, x.shape[1]), 0)
    parts.append(jnp.where(row == 0, 1.0, 0.0))
    return jnp.concatenate(parts, axis=0)


def pull_features(x, cot):
    out = 2.0 * QUAD * cot[:F] * x
    for d in range(1, 8):
        part = 2.0 * QUAD * cot[F * d : F * (d + 1)]
        out = out + part * ahead(x, d) + behind(part * x, d)
    half = 2.0 * QUAD * cot[128:136]
    out = out + jnp.concatenate([half * x[8:], half * x[:8]], axis=0)
    return out + 0.25 * cot[136:152]


def split(x):
    high = x.astype(BF16)
    return high, (x - high.astype(F32)).astype(BF16)


def scores(q, k):
    qh, ql = split(q)
    kh, kl = split(k)
    left = jnp.concatenate([qh, qh, ql, ql], axis=0)
    right = jnp.concatenate([kh, kl, kh, kl], axis=0)
    return dot(left, right, 0, 0) * 0.25


def product(feat, state):
    return dot(jnp.concatenate(split(feat), axis=0), jnp.concatenate([state, state], axis=0), 0, 0)


def causal():
    shape = (256, 256)
    return lax.broadcasted_iota(jnp.int32, shape, 0) >= lax.broadcasted_iota(jnp.int32, shape, 1)


def head_cols(h):
    return slice(h * DH, (h + 1) * DH)


def head_rows(h):
    return slice(h * F, (h + 1) * F)


def rows_of(h):
    return h // 2, slice(h % 2 * EP, (h % 2 + 1) * EP)


def aligned(start, size, step=None):
    return pl.ds(pl.multiple_of(start, step or size), size)


def layer_kernel(
    w_ref, tok_ref, v_ref, g_ref, att_ref, gt_ref, gv_ref, gp_ref,
    wq, wk, wq_far, wk_far, tok2, v2, g2, proj, projt, state, yin, tz, zin, yout, pre, prefix,
    suffix, carried, yin_b, zin_b, yout_b, tz_b, work, gn, att2, gv2, acc, rows_q, rows_k, rq_far,
    rk_far, rq_all, rk_all, cols, all_q, all_k, grad_q, grad_k, sib, pair, yred, ysum, zred,
    send, recv, local_sem,
):
    dp = lax.axis_index("dp")
    z, y, c = place()
    partner = at(z, y, 1 - c)
    right, left, other = across(dp, 0, 1), across(dp, 0, 3), across(dp, 1, 0)
    count = tok_ref.shape[0]
    rows = w_ref.shape[0]
    ours = aligned(c * count, count)
    theirs = aligned((1 - c) * count, count)
    own_half = aligned(c * HD, HD)
    their_half = aligned((1 - c) * HD, HD)
    wires = Wires(send, recv)
    locals_ = []

    def copy_here(src, dst):
        copy = pltpu.make_async_copy(src, dst, local_sem.at[len(locals_)])
        copy.start()
        locals_.append(copy)
        return copy

    own_rows = aligned(dp * rows, rows)
    meet(
        [{"ctx": partner}]
        + [{"ctx": at(z, (y + d) % NY, c)} for d in range(1, NY)]
        + [{"ctx": at((z + d) % NZ, y, c)} for d in range(1, NZ)]
        + [{"dp": across(dp, n // 4, n % 4)} for n in range(1, NDP)]
    )
    here = [
        copy_here(tok_ref, tok2.at[ours]),
        copy_here(v_ref.at[:, own_half], v2.at[ours]),
        copy_here(g_ref.at[:, own_half], g2.at[ours]),
    ]
    wk[own_rows, :] = w_ref[:, aligned(2 * HF + c * HF, HF)]
    wq[own_rows, :] = w_ref[:, aligned(c * HF, HF)]
    met(NY + NZ + NDP - 2)

    wide = 3 * rows // 4
    thin = (rows - wide) // NY
    half_rows = rows // 2
    base_a, base_b = 0, wide

    def part(owner, start, size):
        return wk.at[aligned(owner * rows + start, size, thin // 2)]

    def own_sends(start, size):
        piece = part(dp, start, size)
        return [wires.push(piece, piece, dp=to) for to in (other, right, left)]

    def pass_on(owner, start, size):
        piece = part(owner, start, size)
        return wires.push(piece, piece, dp=right), wires.push(piece, piece, dp=left)

    def relay(near, far, start, size):
        one = part(near, start, size // 2)
        two = part(far, start + size // 2, size // 2)
        return wires.push(one, one, dp=right), wires.push(two, two, dp=left)

    def over_y(owner):
        piece = part(owner, base_b + y * thin, thin)
        return [
            wires.push(piece, piece, ctx=at(z, (y + d) % NY, c)) for d in (2, 1, 3)
        ]

    mine_b = base_b + y * thin
    b_over, b_right, b_left = own_sends(mine_b, thin)
    a_over, a_right, a_left = own_sends(base_a, wide)
    from_partner = [
        wires.push(tok_ref, tok2.at[ours], ctx=partner),
        wires.push(v_ref.at[:, their_half], v2.at[ours], ctx=partner),
        wires.push(g_ref.at[:, their_half], g2.at[ours], ctx=partner),
    ]
    owners = [other, left, right] + [across(dp, dz, dx) for dz, dx in ((1, 3), (1, 1), (0, 2), (1, 2))]
    chain_y = []
    b_over.wait_recv()
    b_right2, b_left2 = pass_on(other, mine_b, thin)
    chain_y.append(over_y(owners[0]))
    b_right.wait_recv()
    b_left.wait_recv()
    b_ends = relay(left, right, mine_b, thin)
    chain_y.append(over_y(owners[1]))
    chain_y.append(over_y(owners[2]))
    a_over.wait_recv()
    a_right2, a_left2 = pass_on(other, base_a, wide)
    b_right2.wait_recv()
    b_left2.wait_recv()
    b_ends2 = relay(owners[3], owners[4], mine_b, thin)
    chain_y.append(over_y(owners[3]))
    chain_y.append(over_y(owners[4]))
    a_right.wait_recv()
    a_left.wait_recv()
    a_ends = relay(left, right, base_a, wide)
    for copy in b_ends:
        copy.wait_recv()
    chain_y.append(over_y(owners[5]))
    for copy in b_ends2:
        copy.wait_recv()
    chain_y.append(over_y(owners[6]))
    a_right2.wait_recv()
    a_left2.wait_recv()
    a_ends2 = relay(owners[3], owners[4], base_a, wide)

    def query_part(owner):
        return wq.at[aligned(owner * rows, rows)]

    def query_halves(near, far):
        one = wq.at[aligned(near * rows, half_rows)]
        two = wq.at[aligned(far * rows + half_rows, half_rows)]
        return wires.push(one, one, dp=right), wires.push(two, two, dp=left)

    q_over, q_right, q_left = [
        wires.push(query_part(dp), query_part(dp), dp=to) for to in (other, right, left)
    ]

    def project(weight, owner):
        return dot(
            tok2[:, aligned(owner * rows, rows)], weight[aligned(owner * rows, rows), :], 1, 0
        )

    for copy in from_partner:
        copy.wait_recv()
    for copy in here:
        copy.wait()
    proj[...] = project(wk, dp)
    for n in range(7):
        for copy in chain_y[n]:
            copy.wait_recv()
        if n == 5:
            for copy in a_ends:
                copy.wait_recv()
        if n == 6:
            for copy in a_ends2:
                copy.wait_recv()
        proj[...] += project(wk, owners[n])
    far_weight = [wires.push(wk, wk_far, ctx=partner)]
    width = cols.shape[2]
    token_copies = []

    def send_tokens(slots):
        for n in slots:
            peer = across(dp, n // 4, n % 4)
            token_copies.append(
                wires.push(tok_ref.at[:, aligned(peer * width, width)], cols.at[n], dp=peer)
            )

    q_over.wait_recv()
    q_passed = [wires.push(query_part(other), query_part(other), dp=to) for to in (right, left)]

    projt[HF:, :] = proj[...].T

    def query(h):
        return projt[aligned(h * F, F), :]

    def key(h):
        return projt[aligned(HF + h * F, F), :]

    def head(h):
        return aligned(h * DH, DH)

    def send_part(src, land, j):
        return wires.push(src.at[j], land.at[y], ctx=at(z, j, c))

    def arrived(copies, d):
        copies[NY - d].wait_recv()

    sent = {}
    for d in (2, 1, 3, 0):
        j = (y + d) % NY
        for e in range(2):
            h = 2 * j + e
            high, low = split(features(key(h), False))
            v = v2[:, head(h)]
            new = dot(jnp.concatenate([high, low], axis=1), jnp.concatenate([v, v], axis=0), 1, 0)
            state[j, e * EP : (e + 1) * EP, :] = new.astype(BF16)
        if d:
            sent[d] = send_part(state, yin, j)

    def scan(later, sent, src, land, total_ref, planes, out, result, fill_y, fill_z, fill_b):
        fill_y()
        for copy in sent.values():
            copy.wait_recv()
        total = jnp.zeros(pre.shape[1:], F32)
        for j in list(range(NY))[::-1] if later else range(NY):
            pre[j] = total
            total = total + jnp.where(j == y, src[j], land[j]).astype(F32)
        total_ref[...] = total.astype(BF16)
        copies = []
        for d in (2, 1, 3):
            to = (z + d) % NZ
            copies.append(wires.push(total_ref, planes.at[z], ctx=at(to, y, c)))
        fill_z()
        for copy in copies:
            copy.wait_recv()
        base = jnp.zeros(pre.shape[1:], F32)
        for j in range(NZ):
            wanted = (j > z) if later else (j < z)
            base = base + jnp.where(wanted, planes[j].astype(F32), 0.0)
        for j in range(NY):
            out[j] = (base + pre[j]).astype(BF16)
        copies = {d: send_part(out, result, (y + d) % NY) for d in (2, 1, 3)}
        result[y] = out[y]
        fill_b()
        return copies

    mask = causal()

    def local_numerator(h):
        a = scores(query(h), key(h))
        kernel = jnp.where(mask, 1.0 + a + 0.5 * a * a, 0.0)
        work[:, head(h)] = dot(kernel.astype(BF16), v2[:, head(h)], 1, 0)

    q_ends = []

    def first_fill():
        q_right.wait_recv()
        q_left.wait_recv()
        q_ends.append(query_halves(left, right))
        for copy in q_passed:
            copy.wait_recv()
        q_ends.append(query_halves(owners[3], owners[4]))

    def second_fill():
        proj[...] = project(wq, dp)
        for n in range(5):
            proj[...] += project(wq, owners[n])
        for n in range(2):
            for copy in q_ends[n]:
                copy.wait_recv()
            proj[...] += project(wq, owners[5 + n])
        projt[:HF, :] = proj[...].T
        far_weight.append(wires.push(wq, wq_far, ctx=partner))
        send_tokens((1, 2, 3))
        for h in range(4):
            local_numerator(h)

    def send_rest():
        send_tokens((4, 5, 6, 7))
        for h in range(4, H):
            local_numerator(h)

    back = scan(False, sent, state, yin, tz, zin, yout, prefix, first_fill, second_fill, send_rest)

    def forward_head(j, e):
        h, at_rows = 2 * j + e, slice(e * EP, (e + 1) * EP)
        q = query(h)
        numerator = work[:, head(h)] + product(features(q, True), prefix[j, at_rows, :])
        inv = lax.rsqrt(jnp.mean(numerator * numerator, axis=1, keepdims=True) + EPSILON)
        normed = numerator * inv
        att2[:, head(h)] = normed.astype(BF16)
        g = g2[:, head(h)].astype(F32)
        grad_num = inv * (g - normed * jnp.mean(normed * g, axis=1, keepdims=True))
        gn[:, head(h)] = grad_num
        high, low = split(features(q, False))
        gh, gl = split(grad_num)
        new = dot(
            jnp.concatenate([high, low, high], axis=1), jnp.concatenate([gh, gh, gl], axis=0), 1, 0
        )
        carried[j, at_rows, :] = new.astype(BF16)

    sent = {}
    for d in (0, 1, 3, 2):
        j = (y + d) % NY
        if d:
            arrived(back, d)
        for e in range(2):
            forward_head(j, e)
        if d:
            sent[d] = send_part(carried, yin_b, j)

    def local_grads(h):
        q, k = query(h), key(h)
        v = v2[:, head(h)]
        gh, gl = split(gn[:, head(h)])
        a = scores(q, k)
        kernel = jnp.where(mask, 1.0 + a + 0.5 * a * a, 0.0).astype(BF16)
        mixing = dot(
            jnp.concatenate([gh, gl], axis=1), jnp.concatenate([v, v], axis=1), 1, 1
        )
        slope = jnp.where(mask, mixing * (1.0 + a) * 0.25, 0.0).astype(BF16)
        qh, ql = split(q)
        kh, kl = split(k)
        dq = dot(jnp.concatenate([kh, kl], axis=0), slope, 1, 1)
        dq = dq[:F] + dq[F:]
        dk = dot(jnp.concatenate([qh, ql], axis=0), slope, 1, 0)
        dk = dk[:F] + dk[F:]
        j, at_rows = rows_of(h)
        before = prefix[j, at_rows, :]
        pulled = dot(
            jnp.concatenate([before, before], axis=1), jnp.concatenate([gh, gl], axis=1), 1, 1
        )
        acc[h * F : (h + 1) * F, :] = dq + pull_features(q, pulled)
        acc[HF + h * F : HF + (h + 1) * F, :] = dk
        work[:, head(h)] = dot(kernel, gh, 0, 0)

    outs = []
    half = count // 2
    low_rows, high_rows = pl.ds(0, half), pl.ds(half, half)

    class Gathered:
        def __init__(self, mine, far, both, land):
            self.mine, self.far, self.both, self.land = mine, far, both, land

        def swap(self):
            self.swapped = wires.push(self.mine.at[theirs], self.far, ctx=partner)

        def start(self):
            self.both[:, aligned(c * HF, HF)] = self.mine[ours, :]
            self.swapped.wait_recv()
            self.both[:, aligned((1 - c) * HF, HF)] = self.far[...]
            self.over = wires.push(self.both, self.land.at[4], dp=other)
            self.near = [
                (
                    wires.push(self.both, self.land.at[1], dp=right),
                    wires.push(self.both, self.land.at[3], dp=left),
                )
            ]
            self.ends = []

        def pass_on(self):
            self.over.wait_recv()
            self.near.append(
                (
                    wires.push(self.land.at[4], self.land.at[5], dp=right),
                    wires.push(self.land.at[4], self.land.at[7], dp=left),
                )
            )

        def relay(self, n):
            at_slot = 4 * n
            self.near[n][0].wait_recv()
            self.ends.append(
                wires.push(
                    self.land.at[at_slot + 1, low_rows], self.land.at[at_slot + 2, low_rows],
                    dp=right,
                )
            )
            self.near[n][1].wait_recv()
            self.ends.append(
                wires.push(
                    self.land.at[at_slot + 3, high_rows], self.land.at[at_slot + 2, high_rows],
                    dp=left,
                )
            )

        def finish(self):
            for copy in self.ends:
                copy.wait_recv()

    queries = Gathered(rows_q, rq_far, rq_all, all_q)
    keys = Gathered(rows_k, rk_far, rk_all, all_k)

    def third_fill():
        outs.append(wires.push(att2.at[theirs], att_ref.at[:, own_half], ctx=partner))
        copy_here(att2.at[ours], att_ref.at[:, own_half])
        for h in range(4):
            local_grads(h)

    def fourth_fill():
        for h in range(4, H):
            local_grads(h)
        rows_q[...] = acc[:HF, :].T.astype(BF16)
        queries.swap()

    def fifth_fill():
        queries.start()

    back = scan(
        True, sent, carried, yin_b, tz_b, zin_b, yout_b, suffix, third_fill, fourth_fill, fifth_fill
    )

    for d in (0, 1, 3, 2):
        j = (y + d) % NY
        if d:
            arrived(back, d)
        for e in range(2):
            h = 2 * j + e
            after = suffix[j, e * EP : (e + 1) * EP, :]
            span = aligned(HF + h * F, F)
            pulled = dot(after, v2[:, head(h)], 1, 1)
            acc[span, :] = acc[span, :] + pull_features(key(h), pulled)
    rows_k[...] = acc[HF:, :].T.astype(BF16)
    keys.swap()
    queries.pass_on()
    queries.relay(0)
    keys.start()

    def value_grad(h):
        j, at_rows = rows_of(h)
        total = work[:, head(h)] + product(features(key(h), True), suffix[j, at_rows, :])
        gv2[:, head(h)] = total.astype(BF16)

    for h in range(4):
        value_grad(h)
    keys.pass_on()
    for h in range(4, H):
        value_grad(h)
    outs.append(wires.push(gv2.at[theirs], gv_ref.at[:, own_half], ctx=partner))
    copy_here(gv2.at[ours], gv_ref.at[:, own_half])
    queries.relay(1)
    keys.relay(0)
    keys.relay(1)
    for copy in token_copies + far_weight:
        copy.wait_recv()

    def tokens_of(n):
        if n == 0:
            return tok2[ours, aligned(dp * width, width)]
        return cols[n]

    def product_of(part_rows, slots):
        left_rows = jnp.concatenate([tokens_of(n) for n in slots], axis=0)
        right_rows = jnp.concatenate(
            [part_rows.both[...] if n == 0 else part_rows.land[n] for n in slots], axis=0
        )
        return dot(left_rows, right_rows, 0, 0).reshape(grad_q.shape)

    block = wq.shape[0] // 4

    def input_grad(n):
        span = slice(n * block, (n + 1) * block)
        near_rows = jnp.concatenate([rows_q[ours, :], rows_k[ours, :]], axis=1)
        far_rows = jnp.concatenate([rq_far[...], rk_far[...]], axis=1)
        piece = dot(near_rows, jnp.concatenate([wq[span, :], wk[span, :]], axis=1), 1, 1)
        piece += dot(far_rows, jnp.concatenate([wq_far[span, :], wk_far[span, :]], axis=1), 1, 1)
        gt_ref[:, span] = piece.astype(BF16)

    class Reduced:
        def __init__(self, n, grad):
            self.n, self.grad = n, grad

        def chip(self):
            n = self.n
            self.halves = {
                d: wires.push(
                    self.grad.at[:, (y + d) % NY, 1 - c], sib.at[n, (y + d) % NY], ctx=partner
                )
                for d in (2, 1, 3, 0)
            }

        def over_y(self):
            n = self.n
            self.near = []
            for d in (2, 1, 3, 0):
                to = (y + d) % NY
                self.halves[d].wait_recv()
                both = self.grad[:, to, c] + sib[n, to]
                if d == 0:
                    ysum[n] = both
                else:
                    pair[n, to] = both.astype(BF16)
                    self.near.append(
                        wires.push(pair.at[n, to], yred.at[n, y], ctx=at(z, to, c))
                    )

        def over_z(self):
            n = self.n
            for copy in self.near:
                copy.wait_recv()
            for j in range(NY):
                ysum[n] += jnp.where(j == y, 0.0, yred[n, j].astype(F32))
            self.planes = [
                wires.push(ysum.at[n, (z + d) % NZ], zred.at[n, z], ctx=at((z + d) % NZ, y, c))
                for d in (2, 1, 3)
            ]

        def finish(self):
            n = self.n
            for copy in self.planes:
                copy.wait_recv()
            total = ysum[n, z]
            for j in range(NZ):
                total = total + jnp.where(j == z, 0.0, zred[n, j])
            span = total.shape[1]
            gp_ref[:, n * span : (n + 1) * span] = total

    first, second = Reduced(0, grad_q), Reduced(1, grad_k)
    queries.finish()
    grad_q[...] = product_of(queries, range(NDP))
    first.chip()
    grad_k[...] = product_of(keys, (0, 1, 3, 4, 5, 7))
    first.over_y()
    keys.finish()
    grad_k[...] += product_of(keys, (2, 6))
    second.chip()
    input_grad(0)
    second.over_y()
    first.over_z()
    input_grad(1)
    input_grad(2)
    second.over_z()
    input_grad(3)
    first.finish()
    second.finish()
    for copy in outs:
        copy.wait_recv()
    for copy in locals_[3:]:
        copy.wait()
    wires.drain()


def hand_over_kernel(*refs):
    count = len(refs) // 3
    srcs, dsts, holds, sems = refs[:count], refs[count : 2 * count], refs[2 * count : -1], refs[-1]
    pieces = [(n, at_half) for at_half in range(2) for n in range(count)]
    reads, writes = [], []
    for i, (n, at_half) in enumerate(pieces):
        size = holds[n].shape[0] // 2
        rows = pl.ds(at_half * size, size)
        reads.append(
            pltpu.make_async_copy(srcs[n].at[rows], holds[n].at[rows], sems.at[0, i])
        )
        writes.append(
            pltpu.make_async_copy(holds[n].at[rows], dsts[n].at[rows], sems.at[1, i])
        )
    for copy in reads:
        copy.start()
    for read, write in zip(reads, writes):
        read.wait()
        write.start()
    for copy in writes:
        copy.wait()


def hand_over(*arrays):
    hbm = pl.BlockSpec(memory_space=pl.ANY)
    return pl.pallas_call(
        hand_over_kernel,
        out_shape=[jax.ShapeDtypeStruct(a.shape, a.dtype) for a in arrays],
        in_specs=[hbm] * len(arrays),
        out_specs=[hbm] * len(arrays),
        scratch_shapes=[pltpu.VMEM(a.shape, a.dtype) for a in arrays]
        + [pltpu.SemaphoreType.DMA((2, 2 * len(arrays)))],
        name="hand_over",
    )(*arrays)


def local(tokens, proj_weight, values, grad_out):
    tok, val, up = tokens[0], values[0], grad_out[0]
    count, model = tok.shape
    shard, width = proj_weight.shape
    both = 2 * count
    own = shard // (2 * NY * NZ)
    parts = (NY, RC, DH)
    dma = pltpu.SemaphoreType.DMA
    hbm = pl.BlockSpec(memory_space=pl.ANY)

    def half(*shape):
        return pltpu.VMEM(shape, BF16)

    def full(*shape):
        return pltpu.VMEM(shape, F32)

    attended, grad_tokens, grad_values, grad_proj = pl.pallas_call(
        layer_kernel,
        out_shape=(
            jax.ShapeDtypeStruct(val.shape, BF16),
            jax.ShapeDtypeStruct(tok.shape, BF16),
            jax.ShapeDtypeStruct(val.shape, BF16),
            jax.ShapeDtypeStruct((own, width), F32),
        ),
        in_specs=[VMEM, hbm, hbm, hbm],
        out_specs=(VMEM,) * 4,
        scratch_shapes=[
            half(model, HF),
            half(model, HF),
            half(model, HF),
            half(model, HF),
            half(both, model),
            half(both, HD),
            half(both, HD),
            full(both, HF),
            full(2 * HF, both),
            half(*parts),
            half(*parts),
            half(RC, DH),
            half(NZ, RC, DH),
            half(*parts),
            full(*parts),
            half(*parts),
            half(*parts),
            half(*parts),
            half(*parts),
            half(NZ, RC, DH),
            half(*parts),
            half(RC, DH),
            full(both, HD),
            full(both, HD),
            half(both, HD),
            half(both, HD),
            full(2 * HF, both),
            half(both, HF),
            half(both, HF),
            half(count, HF),
            half(count, HF),
            half(count, 2 * HF),
            half(count, 2 * HF),
            half(NDP, count, shard),
            half(NDP, count, 2 * HF),
            half(NDP, count, 2 * HF),
            full(NZ, NY, 2, own, 2 * HF),
            full(NZ, NY, 2, own, 2 * HF),
            full(2, NY, NZ, own, 2 * HF),
            half(2, NY, NZ, own, 2 * HF),
            half(2, NY, NZ, own, 2 * HF),
            full(2, NZ, own, 2 * HF),
            full(2, NZ, own, 2 * HF),
            dma((144,)),
            dma((144,)),
            dma((5,)),
        ],
        compiler_params=pltpu.CompilerParams(collective_id=0, has_side_effects=True),
        name="layer",
    )(proj_weight, tok, val, up)
    attended, grad_tokens, grad_values, grad_proj = hand_over(
        attended, grad_tokens, grad_values, grad_proj
    )
    return (attended[None], grad_tokens[None], grad_values[None], grad_proj)


def solution(mesh):
    return jax.shard_map(
        local,
        mesh=mesh,
        in_specs=(P("dp", "ctx", None), P("dp", None), P("dp", "ctx", None), P("dp", "ctx", None)),
        out_specs=(
            P("dp", "ctx", None),
            P("dp", "ctx", None),
            P("dp", "ctx", None),
            P(("dp", "ctx"), None),
        ),
        check_vma=False,
    )
```
